128 devices in a mesh: head: 8 (over x_hi, z), ctx: 16 (over y, x_lo, core).
Axes of the slice: x: 4 (x_hi: 2, x_lo: 2; x = x_hi * 2 + x_lo), y: 4, z: 4, core: 2. Of those that a mesh axis runs over, the one named last changes fastest.
Arguments:
- inputs: bfloat16 [4096, 4096], P('ctx'), may hold values from -8 to 8
- out_grad: bfloat16 [4096, 4096], P('ctx', 'head'), may hold values from -6 to 6
- w_query: bfloat16 [4096, 4096], P(None, 'head'), may hold values from -4 to 4
- w_key: bfloat16 [4096, 1024], P(None, 'head'), may hold values from -4 to 4
- value_projection: bfloat16 [4096, 1024], P(None, 'head'), may hold values from -0.09375 to 0.09375
- w_out: bfloat16 [4096, 4096], P('head'), may hold values from -0.09375 to 0.09375
- doc_lengths: int32 [8], replicated, may hold values from 1 to 2048, 4096 in all
- span_order: int32 [32], replicated, may hold values from 0 to 31, as said below
Outputs:
- input_grad: bfloat16 [4096, 4096], P('ctx', 'head')
The draws below stay inside these ranges and needn't reach their ends.
Inputs may be any that keep to these rules, and one draw needn't show every extreme that they name: `span_order`: A permutation of 0 to 31; entries 2 d and 2 d + 1 are c and 31 - c for some c, in either order.
All inputs are finite; a program needn't handle non-finite values.
Results may differ from the reference program's by a relative error of at most 0.012.
The reference program's roundings to bfloat16 on the way count: a program that leaves them out, or rounds other values in their place, can miss the bound.
Values may be sent and summed in bfloat16 or wider, within the bound.
A program may use at most 64 MiB of HBM per device.

```python
import math
import jax
import jax.numpy as jnp
import numpy as np
from jax import lax

MODEL_WIDTH = 4096
ASKER_NUM = 32
SHARED_KV_NUM = 8
CHANNEL_DIM = 128
TOK_DEV = 256
NDOC = 8
TOKEN_SPAN = 4096
SPANS = 32


def draw_inputs(key, part):
    base = jnp.clip(jax.random.normal(jax.random.fold_in(key, 1), (TOKEN_SPAN, MODEL_WIDTH), jnp.float32), -6.0, 6.0)
    return base.astype(jnp.bfloat16)


def matched_weight(key, salt, columns):
    base = jax.random.normal(jax.random.fold_in(key, salt), (MODEL_WIDTH, columns), jnp.float32)
    base = jnp.clip(base, -5.0, 5.0) / math.sqrt(MODEL_WIDTH)
    return base


def draw_w_query(key, part):
    return matched_weight(key, 21, ASKER_NUM * CHANNEL_DIM).astype(jnp.bfloat16)


def draw_w_key(key, part):
    return matched_weight(key, 22, SHARED_KV_NUM * CHANNEL_DIM).astype(jnp.bfloat16)


def draw_span_order(key, part):
    pairs = SPANS // 2
    lower = jax.random.permutation(jax.random.fold_in(key, 31), pairs).astype(jnp.int32)
    flips = jax.random.randint(jax.random.fold_in(key, 32), (pairs,), 0, 2)
    first = jnp.where(flips == 1, SPANS - 1 - lower, lower)
    second = SPANS - 1 - first
    return jnp.stack([first, second], axis=1).reshape(SPANS).astype(jnp.int32)


def block_levels(rng, shape, cuts, low, high):
    gain, own = 1.0, jax.random.fold_in(rng, 6)
    for position, parts in cuts:
        draws = jnp.exp(jax.random.uniform(jax.random.fold_in(own, position), (parts,), jnp.float32, low / len(cuts), high / len(cuts)))
        gain = gain * jnp.repeat(draws, shape[position] // parts).reshape([-1 if axis == position else 1 for axis in range(len(shape))])
    return gain


def length_profile(amount, total, bound, slope):
    loads = [(1 << 20) // math.isqrt(grade ** slope) + 1 for grade in range(2, amount + 1)]
    surplus, counts = total - bound - (amount - 1), [1] * (amount - 1)
    while surplus > 0:
        free = [i for i in range(amount - 1) if counts[i] < bound]
        pool, budget = sum([loads[i] for i in free]), surplus
        for i in free:
            extra = min(bound - counts[i], max(1, budget * loads[i] // pool), surplus)
            counts[i] = counts[i] + extra
            surplus = surplus - extra
    return np.array([bound] + counts)


def ragged(stream_key, number_of, total, bound, skew):
    if number_of == 2:
        one = jax.random.randint(stream_key, (), max(1, total - bound), min(bound, total - 1) + 1)
        return jnp.stack([one, total - one])
    sizes = jnp.asarray(length_profile(number_of, total, bound, skew), jnp.int32)
    pairs = (number_of - 1) // 2
    donor, sink = sizes[1:1 + 2 * pairs:2], sizes[2:2 + 2 * pairs:2]
    room = jnp.minimum(donor - 1, bound - sink)
    moved = jax.random.randint(jax.random.fold_in(stream_key, 1), (pairs,), 0, 1 << 20) % (room + 1)
    sizes = sizes.at[1:1 + 2 * pairs:2].set(donor - moved).at[2:2 + 2 * pairs:2].set(sink + moved)
    return sizes[jax.random.permutation(jax.random.fold_in(stream_key, 2), number_of)]


def noise(own_key, extent, scale, reach, split=(), held_as=jnp.bfloat16):
    values = jax.random.normal(own_key, extent, jnp.float32) * scale
    if len(split) > 0:
        values = block_levels(own_key, extent, split, -0.22, 0.18) * values
    return jnp.clip(values, min=-reach, max=reach).astype(held_as)


def setup_inputs(seed: int = 0) -> dict:
    splits = jax.random.split(jax.random.key(seed), 9)
    return {
        "inputs": draw_inputs(jax.random.fold_in(splits[8], 71), 0),
        "out_grad": noise(splits[1], (TOKEN_SPAN, MODEL_WIDTH), 1.0, 6.0, ((0, 16), (1, 8))),
        "w_query": draw_w_query(jax.random.fold_in(splits[8], 71), 0),
        "w_key": draw_w_key(jax.random.fold_in(splits[8], 71), 0),
        "value_projection": noise(splits[4], (MODEL_WIDTH, SHARED_KV_NUM * CHANNEL_DIM), MODEL_WIDTH ** -0.5, 0.09375, ((1, 8),)),
        "w_out": noise(splits[5], (ASKER_NUM * CHANNEL_DIM, MODEL_WIDTH), (ASKER_NUM * CHANNEL_DIM) ** -0.5, 0.09375, ((0, 8),)),
        "doc_lengths": ragged(splits[6], NDOC, TOKEN_SPAN, TOKEN_SPAN // 2, 2).astype(jnp.int32),
        "span_order": draw_span_order(jax.random.fold_in(splits[8], 71), 0),
    }


masked_score = -1e+30

def reference(inputs, out_grad, w_query, w_key, value_projection, w_out, doc_lengths, span_order):
    half = TOK_DEV // 2
    rows = jnp.arange(TOKEN_SPAN, dtype=jnp.int32)
    positions = span_order[rows // half] * half + rows % half
    ends = jnp.cumsum(doc_lengths)
    documents = lax.optimization_barrier(jnp.sum((positions[:, None] >= ends[None, :]).astype(jnp.int32), axis=1))
    allowed = (positions[None, :] <= positions[:, None]) & (documents[None, :] == documents[:, None])
    query = jnp.dot(inputs, w_query, preferred_element_type=jnp.float32).astype(jnp.bfloat16)
    keys = jnp.dot(inputs, w_key, preferred_element_type=jnp.float32).astype(jnp.bfloat16)
    values = jnp.dot(inputs, value_projection, preferred_element_type=jnp.float32).astype(jnp.bfloat16)
    context_grad = jnp.dot(out_grad, w_out.T, preferred_element_type=jnp.float32).astype(jnp.bfloat16)
    sharing_bundles = ASKER_NUM // SHARED_KV_NUM
    scale = 1.0 / math.sqrt(CHANNEL_DIM)

    def single_attender(head):
        query_head = lax.dynamic_slice_in_dim(query, head * CHANNEL_DIM, CHANNEL_DIM, 1)
        grad_head = lax.dynamic_slice_in_dim(context_grad, head * CHANNEL_DIM, CHANNEL_DIM, 1)
        key_head = lax.dynamic_slice_in_dim(keys, head // sharing_bundles * CHANNEL_DIM, CHANNEL_DIM, 1)
        value_head = lax.dynamic_slice_in_dim(values, head // sharing_bundles * CHANNEL_DIM, CHANNEL_DIM, 1)
        logits = jnp.dot(query_head, key_head.T, preferred_element_type=jnp.float32) * scale
        logits = jnp.where(allowed, logits, masked_score)
        maxima = lax.optimization_barrier(jnp.max(logits, axis=1, keepdims=True))
        weights = jnp.exp(logits - maxima)
        probability = weights / lax.optimization_barrier(jnp.sum(weights, axis=1, keepdims=True))
        slopes = jnp.dot(grad_head, value_head.T, preferred_element_type=jnp.float32)
        delta = lax.optimization_barrier(jnp.sum(probability * slopes, axis=1, keepdims=True))
        score_grad = (probability * (slopes - delta)).astype(jnp.bfloat16)
        rounded = probability.astype(jnp.bfloat16)
        value_term = jnp.dot(rounded.T, grad_head, preferred_element_type=jnp.float32)
        query_term = jnp.dot(score_grad, key_head, preferred_element_type=jnp.float32) * scale
        key_term = jnp.dot(score_grad.T, query_head, preferred_element_type=jnp.float32) * scale
        return (query_term, key_term, value_term)
    asker_pieces, lookup_pieces, content_pieces = lax.map(single_attender, jnp.arange(ASKER_NUM, dtype=jnp.int32))
    query_grad = jnp.transpose(asker_pieces, (1, 0, 2)).reshape(TOKEN_SPAN, ASKER_NUM * CHANNEL_DIM).astype(jnp.bfloat16)
    lookup_aggregate = lax.optimization_barrier(jnp.sum(lookup_pieces.reshape(SHARED_KV_NUM, sharing_bundles, TOKEN_SPAN, CHANNEL_DIM), axis=1))
    content_aggregate = lax.optimization_barrier(jnp.sum(content_pieces.reshape(SHARED_KV_NUM, sharing_bundles, TOKEN_SPAN, CHANNEL_DIM), axis=1))
    key_gradient = jnp.transpose(lookup_aggregate, (1, 0, 2)).reshape(TOKEN_SPAN, SHARED_KV_NUM * CHANNEL_DIM).astype(jnp.bfloat16)
    value_gradient = jnp.transpose(content_aggregate, (1, 0, 2)).reshape(TOKEN_SPAN, SHARED_KV_NUM * CHANNEL_DIM).astype(jnp.bfloat16)
    total = jnp.dot(query_grad, w_query.T, preferred_element_type=jnp.float32)
    total = total + jnp.dot(key_gradient, w_key.T, preferred_element_type=jnp.float32)
    total = total + jnp.dot(value_gradient, value_projection.T, preferred_element_type=jnp.float32)
    return total.astype(jnp.bfloat16)
```

```python
import math

import jax
import jax.numpy as jnp
from jax import lax
from jax.experimental import pallas as pl
from jax.experimental.pallas import tpu as pltpu
from jax.sharding import Mesh
from jax.sharding import PartitionSpec as P

ASKER_NUM = 32
SHARED_KV_NUM = 8
CHANNEL_DIM = 128
HEAD = ("head_0", "head_1")


HALF = 128
TILE = 256
BUNDLE = ASKER_NUM // SHARED_KV_NUM
LOG2E = 1.4426950408889634
MASKED = -1e30


def in_order(parts, dim):
    lengths = list(parts.shape[1:])
    lengths[dim] *= parts.shape[0]
    return jnp.moveaxis(parts, 0, dim).reshape(lengths)


def copy_for_each(value, axis):
    copies = jnp.broadcast_to(value, (lax.axis_size(axis), *value.shape))
    return lax.all_to_all(copies, axis, split_axis=0, concat_axis=0, tiled=True)


def gathered_copies(value, axis, dim):
    return in_order(copy_for_each(value, axis), dim)


def sum_in_order(parts, axes, sequence):
    lengths = [lax.axis_size(a) for a in axes]
    parts = parts.reshape(*lengths, *parts.shape[1:])
    parts = parts.transpose(*sequence, *range(len(axes), parts.ndim))
    parts = parts.reshape(-1, *parts.shape[len(axes) :])
    for k in sequence:
        parts = lax.psum_scatter(parts, axes[k], scatter_dimension=0, tiled=True)
    return parts[0]


def split_up(value, dim, peers):
    lengths = value.shape
    parts = value.reshape(*lengths[:dim], peers, lengths[dim] // peers, *lengths[dim + 1 :])
    return jnp.moveaxis(parts, dim, 0)


def summed_rows(value, axes, sequence, dim):
    peers = lax.axis_size(axes)
    return sum_in_order(split_up(value, dim, peers), axes, sequence)


def back_project(grad, weight):
    return lax.dot_general(
        grad, weight, (((1,), (1,)), ((), ())), preferred_element_type=jnp.float32
    )


def attention_kernel(
    span_ref, block_ref, first_ref, start_ref, q_ref, g_ref, kv_ref,
    dq_ref, dkv_ref,
    kvs, qs, gs, s_buf, d_buf, acc, dqt,
):
    exponent = LOG2E / math.sqrt(CHANNEL_DIM)
    scale = 1.0 / math.sqrt(CHANNEL_DIM)
    spans = span_ref.shape[0]

    @pl.loop(0, spans)
    def _(r):
        p = span_ref[r]
        kvs[pl.ds(pl.multiple_of(p * HALF, HALF), HALF), :] = kv_ref[
            pl.ds(pl.multiple_of(r * HALF, HALF), HALF), :
        ]
        acc[pl.ds(pl.multiple_of(r * HALF, HALF), HALF), :] = jnp.zeros((HALF, 2 * CHANNEL_DIM), jnp.float32)

    lanes = BUNDLE * HALF
    for b in range(2):
        rows = slice(b * HALF, (b + 1) * HALF)
        for h in range(BUNDLE):
            cols = slice(h * CHANNEL_DIM, (h + 1) * CHANNEL_DIM)
            qs[h * HALF : (h + 1) * HALF, :] = q_ref[rows, cols]
            gs[h * HALF : (h + 1) * HALF, :] = g_ref[rows, cols]
        c = block_ref[b]
        low = first_ref[b] // (TILE // HALF)
        high = c // (TILE // HALF) + 1
        start = start_ref[b : b + 1, :]
        position = c * HALF + lax.broadcasted_iota(jnp.int32, (1, HALF), 1)

        def gather_stats(t, carry):
            top, total, inner = carry
            at = pl.ds(pl.multiple_of(t * TILE, TILE), TILE)
            keys = kvs[at, :CHANNEL_DIM]
            values = kvs[at, CHANNEL_DIM:]
            key_position = t * TILE + lax.broadcasted_iota(jnp.int32, (TILE, HALF), 0)
            bias = jnp.where(
                (key_position <= position) & (key_position >= start), 0.0, MASKED
            )
            bias = jnp.concatenate([bias] * BUNDLE, axis=1)
            s = lax.dot_general(
                keys, qs[...], (((1,), (1,)), ((), ())), preferred_element_type=jnp.float32
            )
            s = s * exponent + bias
            s_buf[at, :] = s
            fresh = jnp.maximum(top, jnp.max(s, axis=0, keepdims=True))
            factor = jnp.exp2(top - fresh)
            e = jnp.exp2(s - fresh)
            slopes = lax.dot_general(
                values, gs[...], (((1,), (1,)), ((), ())), preferred_element_type=jnp.float32
            )
            d_buf[at, :] = slopes
            total = total * factor + jnp.sum(e, axis=0, keepdims=True)
            inner = inner * factor + jnp.sum(e * slopes, axis=0, keepdims=True)
            return fresh, total, inner

        zero = jnp.zeros((1, lanes), jnp.float32)
        top, total, inner = lax.fori_loop(
            low, high, gather_stats, (jnp.full((1, lanes), MASKED, jnp.float32), zero, zero)
        )
        delta = inner / total
        level = top + jnp.log2(total)
        dqt[...] = jnp.zeros_like(dqt)

        @pl.loop(low, high)
        def _(t):
            at = pl.ds(pl.multiple_of(t * TILE, TILE), TILE)
            probability = jnp.exp2(s_buf[at, :] - level)
            score_grad = (probability * (d_buf[at, :] - delta)).astype(jnp.bfloat16)
            rounded = probability.astype(jnp.bfloat16)
            acc[at, CHANNEL_DIM:] += jnp.dot(rounded, gs[...], preferred_element_type=jnp.float32)
            acc[at, :CHANNEL_DIM] += jnp.dot(score_grad, qs[...], preferred_element_type=jnp.float32)
            dqt[...] += lax.dot_general(
                kvs[at, :CHANNEL_DIM], score_grad, (((0,), (0,)), ((), ())),
                preferred_element_type=jnp.float32,
            )

        for h in range(BUNDLE):
            dq_ref[rows, h * CHANNEL_DIM : (h + 1) * CHANNEL_DIM] = (
                (dqt[:, h * HALF : (h + 1) * HALF] * scale).T.astype(jnp.bfloat16)
            )

    @pl.loop(0, spans)
    def _(r):
        p = span_ref[r]
        at = pl.ds(pl.multiple_of(p * HALF, HALF), HALF)
        to = pl.ds(pl.multiple_of(r * HALF, HALF), HALF)
        dkv_ref[to, :CHANNEL_DIM] = (acc[at, :CHANNEL_DIM] * scale).astype(jnp.bfloat16)
        dkv_ref[to, CHANNEL_DIM:] = acc[at, CHANNEL_DIM:].astype(jnp.bfloat16)


def attention(q, g, kv, span_order, doc_lengths):
    tokens = q.shape[0]
    length = kv.shape[0]
    ends = jnp.cumsum(doc_lengths)
    mine = lax.axis_index("ctx")
    blocks = lax.dynamic_slice_in_dim(span_order, mine * 2, 2)
    positions = blocks[:, None] * HALF + jnp.arange(HALF, dtype=jnp.int32)[None, :]
    starts = jnp.max(
        jnp.where(positions[:, :, None] >= ends[None, None, :], ends[None, None, :], 0), axis=2
    ).astype(jnp.int32)
    first = (starts[:, 0] // HALF).astype(jnp.int32)
    smem = pl.BlockSpec(memory_space=pltpu.SMEM)
    vmem = pl.BlockSpec(memory_space=pltpu.VMEM)
    lanes = BUNDLE * HALF
    return pl.pallas_call(
        attention_kernel,
        out_shape=(
            jax.ShapeDtypeStruct((tokens, lanes), jnp.bfloat16),
            jax.ShapeDtypeStruct((length, 2 * CHANNEL_DIM), jnp.bfloat16),
        ),
        in_specs=[smem, smem, smem, vmem, vmem, vmem, vmem],
        out_specs=(vmem, vmem),
        scratch_shapes=[
            pltpu.VMEM((length, 2 * CHANNEL_DIM), jnp.bfloat16),
            pltpu.VMEM((lanes, CHANNEL_DIM), jnp.bfloat16),
            pltpu.VMEM((lanes, CHANNEL_DIM), jnp.bfloat16),
            pltpu.VMEM((length, lanes), jnp.float32),
            pltpu.VMEM((length, lanes), jnp.float32),
            pltpu.VMEM((length, 2 * CHANNEL_DIM), jnp.float32),
            pltpu.VMEM((CHANNEL_DIM, lanes), jnp.float32),
        ],
        compiler_params=pltpu.CompilerParams(vmem_limit_bytes=40 * 1024 * 1024),
        name="attention",
    )(span_order, blocks, first, starts, q, g, kv)


def shards(inputs, out_grad, w_query, w_key, value_projection, w_out, doc_lengths, span_order):
    width = w_key.shape[1]
    query = jnp.dot(inputs, w_query, preferred_element_type=jnp.float32).astype(jnp.bfloat16)
    keys = jnp.dot(inputs, w_key, preferred_element_type=jnp.float32).astype(jnp.bfloat16)
    values = jnp.dot(inputs, value_projection, preferred_element_type=jnp.float32).astype(
        jnp.bfloat16
    )
    context_grad = back_project(gathered_copies(out_grad, HEAD, 1), w_out).astype(jnp.bfloat16)
    gathered = lax.all_gather(jnp.concatenate([keys, values], axis=1), "ctx", axis=0, tiled=True)
    query_grad, pieces = attention(query, context_grad, gathered, span_order, doc_lengths)
    owned = lax.psum_scatter(pieces, "ctx", scatter_dimension=0, tiled=True)
    partial_value = (
        back_project(query_grad, w_query)
        + back_project(owned[:, :width], w_key)
        + back_project(owned[:, width:], value_projection)
    )
    return summed_rows(partial_value, HEAD, (1, 0), 1).astype(jnp.bfloat16)


def solution(mesh):
    split = Mesh(mesh.devices.reshape(2, 4, mesh.shape["ctx"]), ("head_0", "head_1", "ctx"))
    in_specs = (
        P("ctx", None),
        P("ctx", HEAD),
        P(None, HEAD),
        P(None, HEAD),
        P(None, HEAD),
        P(HEAD, None),
        P(),
        P(),
    )
    out_specs = P("ctx", HEAD)
    return jax.shard_map(
        shards, mesh=split, in_specs=in_specs, out_specs=out_specs, check_vma=False
    )
```

```python
import math

import jax
import jax.numpy as jnp
from jax import lax
from jax.experimental import pallas as pl
from jax.experimental.pallas import tpu as pltpu
from jax.sharding import PartitionSpec as P

ASKER_NUM = 32
SHARED_KV_NUM = 8
CHANNEL_DIM = 128
BUNDLE = ASKER_NUM // SHARED_KV_NUM
HALF = 128
TILE = 256
RING = 4
FEATURES = 512
CHUNKS = 2
LOG2E = 1.4426950408889634
MASKED = -1e30
MESH = pl.DeviceIdType.MESH


def remote(src, dst, send, receive, place):
    return pltpu.make_async_remote_copy(
        src_ref=src, dst_ref=dst, send_sem=send, recv_sem=receive,
        device_id=place, device_id_type=MESH,
    )


def greet(places):
    barrier = pltpu.get_barrier_semaphore()
    for place in places:
        pl.semaphore_signal(barrier, inc=1, device_id=place, device_id_type=MESH)
    pl.semaphore_wait(barrier, len(places))


def neighbours():
    head = lax.axis_index("head")
    ctx = lax.axis_index("ctx")
    far, depth = head // RING, head % RING
    line, near, core = ctx // 4, (ctx // 2) % 2, ctx % 2

    def head_of(f, d):
        return f * RING + d

    def ctx_of(r, n, c):
        return r * 4 + n * 2 + c

    places = {
        "head_up": (head_of(far, (depth + 1) % RING), ctx),
        "head_down": (head_of(far, (depth + 3) % RING), ctx),
        "head_pair": (head_of(1 - far, depth), ctx),
        "ctx_up": (head, ctx_of((line + 1) % RING, near, core)),
        "ctx_down": (head, ctx_of((line + 3) % RING, near, core)),
        "ctx_pair": (head, ctx_of(line, 1 - near, core)),
        "sibling": (head, ctx_of(line, near, 1 - core)),
    }
    return places, (far, depth), (line, near, core)


class Gather:
    def __init__(self, source, block, half, pair, ring, sends, receives, up, down, across):
        other = 1 - pair
        before, after, opposite = (ring + 3) % RING, (ring + 1) % RING, (ring + 2) % RING
        self.copies = []
        plan = [
            (source, block(pair, ring), block(pair, before), up),
            (source, block(pair, ring), block(pair, after), down),
            (source, block(pair, ring), block(other, ring), across),
            (half(pair, before, 0), half(pair, before, 0), half(pair, opposite, 0), up),
            (half(pair, after, 1), half(pair, after, 1), half(pair, opposite, 1), down),
            (block(other, ring), block(other, ring), block(other, before), up),
            (block(other, ring), block(other, ring), block(other, after), down),
            (half(other, before, 0), half(other, before, 0), half(other, opposite, 0), up),
            (half(other, after, 1), half(other, after, 1), half(other, opposite, 1), down),
        ]
        for k, (src, dst, landed, place) in enumerate(plan):
            self.copies.append(
                (
                    remote(src, dst, sends.at[k], receives.at[k], place),
                    remote(landed, landed, sends.at[k], receives.at[k], place),
                )
            )

    def start(self, *which):
        for k in which:
            self.copies[k][0].start()

    def arrive(self, *which):
        for k in which:
            self.copies[k][1].wait_recv()

    def drain(self):
        for sent, landed in self.copies:
            sent.wait_send()


def front_kernel(
    x_hbm, og_hbm, wq_hbm, wk_hbm, wv_hbm, wo_hbm,
    q_ref, g_ref, kv_ref,
    x, wq, wkv, wo, og, acc,
    loads, head_send, head_receive, ctx_send, ctx_receive, sibling_send, sibling_receive,
):
    places, (far, depth), (line, near, core) = neighbours()
    me = far * RING + depth
    local = [
        pltpu.make_async_copy(x_hbm, x, loads.at[0]),
        pltpu.make_async_copy(wk_hbm, wkv.at[:, :CHANNEL_DIM], loads.at[1]),
        pltpu.make_async_copy(wv_hbm, wkv.at[:, CHANNEL_DIM:], loads.at[2]),
        pltpu.make_async_copy(wq_hbm, wq, loads.at[3]),
        pltpu.make_async_copy(og_hbm, og.at[me], loads.at[4]),
        pltpu.make_async_copy(wo_hbm, wo, loads.at[5]),
    ]
    for copy in local:
        copy.start()
    greet(list(places.values()))

    heads = Gather(
        og_hbm,
        lambda p, r: og.at[p * RING + r],
        lambda p, r, k: og.at[p * RING + r, pl.ds(k * HALF, HALF), :],
        far, depth, head_send, head_receive,
        places["head_up"], places["head_down"], places["head_pair"],
    )
    heads.start(0, 1, 2)

    def slot(p, r, c=core):
        return r * 4 + p * 2 + c

    spread = Gather(
        kv_ref.at[slot(near, line)],
        lambda p, r: kv_ref.at[slot(p, r)],
        lambda p, r, k: kv_ref.at[slot(p, r), pl.ds(k * HALF, HALF), :],
        near, line, ctx_send, ctx_receive,
        places["ctx_up"], places["ctx_down"], places["ctx_pair"],
    )
    turns = [(p, (line + d) % RING) for p in (near, 1 - near) for d in (0, 3, 1, 2)]
    passed = [
        (
            remote(
                kv_ref.at[slot(p, r)], kv_ref.at[slot(p, r)],
                sibling_send.at[k], sibling_receive.at[k], places["sibling"],
            ),
            remote(
                kv_ref.at[slot(p, r, 1 - core)], kv_ref.at[slot(p, r, 1 - core)],
                sibling_send.at[k], sibling_receive.at[k], places["sibling"],
            ),
        )
        for k, (p, r) in enumerate(turns)
    ]

    def features(p, r):
        f = p * RING + r
        return lax.dot_general(
            og[f], wo[:, pl.ds(pl.multiple_of(f * FEATURES, FEATURES), FEATURES)],
            (((1,), (1,)), ((), ())), preferred_element_type=jnp.float32,
        )

    for k in (0, 1, 2):
        local[k].wait()
    kv_ref[slot(near, line)] = jnp.dot(
        x[...], wkv[...], preferred_element_type=jnp.float32
    ).astype(jnp.bfloat16)
    local[3].wait()
    q_ref[...] = jnp.dot(x[...], wq[...], preferred_element_type=jnp.float32).astype(jnp.bfloat16)
    spread.start(0, 1, 2)
    passed[0][0].start()
    local[4].wait()
    local[5].wait()
    acc[...] = features(far, depth)

    before, after, opposite = (depth + 3) % RING, (depth + 1) % RING, (depth + 2) % RING
    heads.arrive(0)
    heads.start(3)
    heads.arrive(1)
    heads.start(4)
    acc[...] += features(far, before)
    spread.arrive(0)
    spread.start(3)
    passed[1][0].start()
    spread.arrive(1)
    spread.start(4)
    passed[2][0].start()
    spread.arrive(2)
    spread.start(5, 6)
    passed[4][0].start()
    acc[...] += features(far, after)
    heads.arrive(2)
    heads.start(5, 6)
    acc[...] += features(1 - far, depth)
    spread.arrive(3, 4)
    passed[3][0].start()
    spread.arrive(5)
    spread.start(7)
    passed[5][0].start()
    spread.arrive(6)
    spread.start(8)
    passed[6][0].start()
    heads.arrive(3, 4)
    acc[...] += features(far, opposite)
    heads.arrive(5)
    heads.start(7)
    heads.arrive(6)
    heads.start(8)
    acc[...] += features(1 - far, before)
    acc[...] += features(1 - far, after)
    spread.arrive(7, 8)
    passed[7][0].start()
    heads.arrive(7, 8)
    g_ref[...] = (acc[...] + features(1 - far, opposite)).astype(jnp.bfloat16)
    for sent, landed in passed:
        landed.wait_recv()
    heads.drain()
    spread.drain()
    for sent, landed in passed:
        sent.wait_send()


def front(inputs, out_grad, w_query, w_key, value_projection, w_out, peers):
    tokens, width = inputs.shape
    lanes = w_query.shape[1]
    hbm = pl.BlockSpec(memory_space=pl.ANY)
    vmem = pl.BlockSpec(memory_space=pltpu.VMEM)
    return pl.pallas_call(
        front_kernel,
        out_shape=(
            jax.ShapeDtypeStruct((tokens, lanes), jnp.bfloat16),
            jax.ShapeDtypeStruct((tokens, lanes), jnp.bfloat16),
            jax.ShapeDtypeStruct((peers, tokens, 2 * CHANNEL_DIM), jnp.bfloat16),
        ),
        in_specs=[hbm] * 6,
        out_specs=(vmem, vmem, vmem),
        scratch_shapes=[
            pltpu.VMEM((tokens, width), jnp.bfloat16),
            pltpu.VMEM((width, lanes), jnp.bfloat16),
            pltpu.VMEM((width, 2 * CHANNEL_DIM), jnp.bfloat16),
            pltpu.VMEM((lanes, width), jnp.bfloat16),
            pltpu.VMEM((2 * RING, tokens, FEATURES), jnp.bfloat16),
            pltpu.VMEM((tokens, lanes), jnp.float32),
            pltpu.SemaphoreType.DMA((6,)),
            pltpu.SemaphoreType.DMA((9,)),
            pltpu.SemaphoreType.DMA((9,)),
            pltpu.SemaphoreType.DMA((9,)),
            pltpu.SemaphoreType.DMA((9,)),
            pltpu.SemaphoreType.DMA((8,)),
            pltpu.SemaphoreType.DMA((8,)),
        ],
        compiler_params=pltpu.CompilerParams(
            collective_id=0, has_side_effects=True, vmem_limit_bytes=32 * 1024 * 1024
        ),
        name="front",
    )(inputs, out_grad, w_query, w_key, value_projection, w_out)


class Reduce:
    def __init__(self, held, gone_up, gone_down, up_sum, down_sum, ring, sends, receives, up, down):
        self.held, self.gone_up, self.gone_down = held, gone_up, gone_down
        self.up_sum, self.down_sum = up_sum, down_sum
        self.before, self.after = (ring + 3) % RING, (ring + 1) % RING
        opposite = (ring + 2) % RING
        low, high = pl.ds(0, HALF), pl.ds(HALF, HALF)
        plan = [
            (held.at[opposite, :, low], gone_up, up),
            (held.at[opposite, :, high], gone_down, down),
            (held.at[self.after, :, high], up_sum.at[:, high], up),
            (held.at[self.before, :, low], down_sum.at[:, low], down),
            (held.at[self.after, :, low], up_sum.at[:, low], up),
            (held.at[self.before, :, high], down_sum.at[:, high], down),
        ]
        self.copies = [
            remote(src, dst, sends.at[k], receives.at[k], place)
            for k, (src, dst, place) in enumerate(plan)
        ]

    def start(self, *which):
        for k in which:
            self.copies[k].start()

    def relay(self):
        low, high = slice(0, HALF), slice(HALF, 2 * HALF)
        self.copies[0].wait_recv()
        for p in range(2):
            self.held[self.after, p, low] = (
                self.held[self.after, p, low].astype(jnp.float32)
                + self.gone_up[p].astype(jnp.float32)
            ).astype(jnp.bfloat16)
        self.start(4)
        self.copies[1].wait_recv()
        for p in range(2):
            self.held[self.before, p, high] = (
                self.held[self.before, p, high].astype(jnp.float32)
                + self.gone_down[p].astype(jnp.float32)
            ).astype(jnp.bfloat16)
        self.start(5)

    def arrive(self):
        for k in (2, 3, 4, 5):
            self.copies[k].wait_recv()

    def total(self, p):
        return self.up_sum[p].astype(jnp.float32) + self.down_sum[p].astype(jnp.float32)

    def drain(self):
        for copy in self.copies:
            copy.wait_send()


def back_kernel(
    dq_ref, p_ref, wq_hbm, wk_hbm, wv_hbm,
    out_ref,
    wq, wkv, side, held, crossing, crossed, gone, sums, kept, dkv,
    parts, leaving, left, far_gone, far_sums, far_crossing, far_crossed,
    loads, side_send, side_receive, ctx_send, ctx_receive, head_send, head_receive,
    pair_send, pair_receive,
):
    places, (far, depth), (line, near, core) = neighbours()
    local = [
        pltpu.make_async_copy(wq_hbm, wq, loads.at[0]),
        pltpu.make_async_copy(wk_hbm, wkv.at[:, :CHANNEL_DIM], loads.at[1]),
        pltpu.make_async_copy(wv_hbm, wkv.at[:, CHANNEL_DIM:], loads.at[2]),
    ]
    for copy in local:
        copy.start()
    greet(list(places.values()))

    turns = [(line + d) % RING for d in (2, 1, 3, 0)]
    swaps = [
        remote(
            p_ref.at[r, :, 1 - core], side.at[r],
            side_send.at[k], side_receive.at[k], places["sibling"],
        )
        for k, r in enumerate(turns)
    ]
    for copy in swaps:
        copy.start()
    rows = Reduce(
        held, gone.at[0], gone.at[1], sums.at[0], sums.at[1], line,
        ctx_send, ctx_receive, places["ctx_up"], places["ctx_down"],
    )

    def join(k, p):
        r = turns[k]
        return p_ref[r, p, core].astype(jnp.float32) + side[r, p].astype(jnp.float32)

    for k, ready in enumerate(((0, 1), (2,), (3,))):
        swaps[k].wait_recv()
        for p in range(2):
            held[turns[k], p] = join(k, p).astype(jnp.bfloat16)
        rows.start(*ready)

    local[0].wait()

    def query_part(f):
        return lax.dot_general(
            dq_ref[...], wq[pl.ds(pl.multiple_of(f * FEATURES, FEATURES), FEATURES), :],
            (((1,), (1,)), ((), ())), preferred_element_type=jnp.float32,
        )

    @pl.loop(0, RING)
    def _(f):
        parts[f] = query_part(f)

    swaps[3].wait_recv()
    for p in range(2):
        kept[p] = join(3, p)
    rows.relay()

    @pl.loop(RING, 2 * RING)
    def _(f):
        parts[f] = query_part(f)

    rows.arrive()
    crossing[...] = (kept[1 - near] + rows.total(1 - near)).astype(jnp.bfloat16)
    swap = remote(
        crossing, crossed, pair_send.at[0], pair_receive.at[0], places["ctx_pair"]
    )
    swap.start()
    kept[near] = kept[near] + rows.total(near)
    local[1].wait()
    local[2].wait()
    swap.wait_recv()
    dkv[...] = (kept[near] + crossed[...].astype(jnp.float32)).astype(jnp.bfloat16)

    columns = FEATURES // CHUNKS
    turns = [(depth + d) % RING for d in (2, 1, 3, 0)]
    rounds = [
        Reduce(
            leaving.at[c], far_gone.at[c, 0], far_gone.at[c, 1],
            far_sums.at[c, 0], far_sums.at[c, 1], depth,
            head_send.at[c], head_receive.at[c], places["head_up"], places["head_down"],
        )
        for c in range(CHUNKS)
    ]
    across = [
        remote(
            far_crossing.at[c], far_crossed.at[c],
            pair_send.at[1 + c], pair_receive.at[1 + c], places["head_pair"],
        )
        for c in range(CHUNKS)
    ]

    def term(c, f):
        return parts[f, :, c * columns : (c + 1) * columns] + lax.dot_general(
            dkv[...], wkv[pl.ds(pl.multiple_of(f * FEATURES + c * columns, columns), columns), :],
            (((1,), (1,)), ((), ())), preferred_element_type=jnp.float32,
        )

    for c in range(CHUNKS):
        for k, ready in enumerate(((0, 1), (2,), (3,))):
            for p in range(2):
                leaving[c, turns[k], p] = term(c, p * RING + turns[k]).astype(jnp.bfloat16)
            rounds[c].start(*ready)
    for c in range(CHUNKS):
        rounds[c].relay()
    for c in range(CHUNKS):
        for p in range(2):
            left[c, p] = term(c, p * RING + turns[3])
        rounds[c].arrive()
        far_crossing[c] = (left[c, 1 - far] + rounds[c].total(1 - far)).astype(jnp.bfloat16)
        across[c].start()
        left[c, far] = left[c, far] + rounds[c].total(far)
    for c in range(CHUNKS):
        across[c].wait_recv()
        out_ref[:, c * columns : (c + 1) * columns] = (
            left[c, far] + far_crossed[c].astype(jnp.float32)
        ).astype(jnp.bfloat16)
    for copy in (*swaps, swap, *across):
        copy.wait_send()
    rows.drain()
    for c in range(CHUNKS):
        rounds[c].drain()


def back(query_grad, pieces, w_query, w_key, value_projection):
    tokens, lanes = query_grad.shape
    width = w_query.shape[0]
    columns = FEATURES // CHUNKS
    hbm = pl.BlockSpec(memory_space=pl.ANY)
    vmem = pl.BlockSpec(memory_space=pltpu.VMEM)
    wide = 2 * CHANNEL_DIM
    bf16, f32 = jnp.bfloat16, jnp.float32
    return pl.pallas_call(
        back_kernel,
        out_shape=jax.ShapeDtypeStruct((tokens, FEATURES), bf16),
        in_specs=[vmem, vmem, hbm, hbm, hbm],
        out_specs=vmem,
        scratch_shapes=[
            pltpu.VMEM((width, lanes), bf16),
            pltpu.VMEM((width, wide), bf16),
            pltpu.VMEM((RING, 2, tokens, wide), bf16),
            pltpu.VMEM((RING, 2, tokens, wide), bf16),
            pltpu.VMEM((tokens, wide), bf16),
            pltpu.VMEM((tokens, wide), bf16),
            pltpu.VMEM((2, 2, HALF, wide), bf16),
            pltpu.VMEM((2, 2, tokens, wide), bf16),
            pltpu.VMEM((2, tokens, wide), f32),
            pltpu.VMEM((tokens, wide), bf16),
            pltpu.VMEM((2 * RING, tokens, FEATURES), f32),
            pltpu.VMEM((CHUNKS, RING, 2, tokens, columns), bf16),
            pltpu.VMEM((CHUNKS, 2, tokens, columns), f32),
            pltpu.VMEM((CHUNKS, 2, 2, HALF, columns), bf16),
            pltpu.VMEM((CHUNKS, 2, 2, tokens, columns), bf16),
            pltpu.VMEM((CHUNKS, tokens, columns), bf16),
            pltpu.VMEM((CHUNKS, tokens, columns), bf16),
            pltpu.SemaphoreType.DMA((3,)),
            pltpu.SemaphoreType.DMA((4,)),
            pltpu.SemaphoreType.DMA((4,)),
            pltpu.SemaphoreType.DMA((6,)),
            pltpu.SemaphoreType.DMA((6,)),
            pltpu.SemaphoreType.DMA((CHUNKS, 6)),
            pltpu.SemaphoreType.DMA((CHUNKS, 6)),
            pltpu.SemaphoreType.DMA((1 + CHUNKS,)),
            pltpu.SemaphoreType.DMA((1 + CHUNKS,)),
        ],
        compiler_params=pltpu.CompilerParams(
            collective_id=1, has_side_effects=True, vmem_limit_bytes=40 * 1024 * 1024
        ),
        name="back",
    )(query_grad, pieces, w_query, w_key, value_projection)


def attention_kernel(
    span_ref, block_ref, first_ref, start_ref, q_ref, g_ref, kv_ref,
    dq_ref, dkv_ref,
    kvs, qs, gs, s_buf, d_buf, acc, dqt,
):
    exponent = LOG2E / math.sqrt(CHANNEL_DIM)
    scale = 1.0 / math.sqrt(CHANNEL_DIM)
    spans = span_ref.shape[0]

    @pl.loop(0, spans)
    def _(r):
        p = span_ref[r]
        kvs[pl.ds(pl.multiple_of(p * HALF, HALF), HALF), :] = kv_ref[
            pl.ds(pl.multiple_of(r * HALF, HALF), HALF), :
        ]
        acc[pl.ds(pl.multiple_of(r * HALF, HALF), HALF), :] = jnp.zeros((HALF, 2 * CHANNEL_DIM), jnp.float32)

    lanes = BUNDLE * HALF
    for b in range(2):
        rows = slice(b * HALF, (b + 1) * HALF)
        for h in range(BUNDLE):
            cols = slice(h * CHANNEL_DIM, (h + 1) * CHANNEL_DIM)
            qs[h * HALF : (h + 1) * HALF, :] = q_ref[rows, cols]
            gs[h * HALF : (h + 1) * HALF, :] = g_ref[rows, cols]
        c = block_ref[b]
        low = first_ref[b] // (TILE // HALF)
        high = c // (TILE // HALF) + 1
        start = start_ref[b : b + 1, :]
        position = c * HALF + lax.broadcasted_iota(jnp.int32, (1, HALF), 1)

        def gather_stats(t, carry):
            top, total, inner = carry
            at = pl.ds(pl.multiple_of(t * TILE, TILE), TILE)
            keys = kvs[at, :CHANNEL_DIM]
            values = kvs[at, CHANNEL_DIM:]
            key_position = t * TILE + lax.broadcasted_iota(jnp.int32, (TILE, HALF), 0)
            bias = jnp.where(
                (key_position <= position) & (key_position >= start), 0.0, MASKED
            )
            bias = jnp.concatenate([bias] * BUNDLE, axis=1)
            s = lax.dot_general(
                keys, qs[...], (((1,), (1,)), ((), ())), preferred_element_type=jnp.float32
            )
            s = s * exponent + bias
            s_buf[at, :] = s
            fresh = jnp.maximum(top, jnp.max(s, axis=0, keepdims=True))
            factor = jnp.exp2(top - fresh)
            e = jnp.exp2(s - fresh)
            slopes = lax.dot_general(
                values, gs[...], (((1,), (1,)), ((), ())), preferred_element_type=jnp.float32
            )
            d_buf[at, :] = slopes
            total = total * factor + jnp.sum(e, axis=0, keepdims=True)
            inner = inner * factor + jnp.sum(e * slopes, axis=0, keepdims=True)
            return fresh, total, inner

        zero = jnp.zeros((1, lanes), jnp.float32)
        top, total, inner = lax.fori_loop(
            low, high, gather_stats, (jnp.full((1, lanes), MASKED, jnp.float32), zero, zero)
        )
        delta = inner / total
        level = top + jnp.log2(total)
        dqt[...] = jnp.zeros_like(dqt)

        @pl.loop(low, high)
        def _(t):
            at = pl.ds(pl.multiple_of(t * TILE, TILE), TILE)
            probability = jnp.exp2(s_buf[at, :] - level)
            score_grad = (probability * (d_buf[at, :] - delta)).astype(jnp.bfloat16)
            rounded = probability.astype(jnp.bfloat16)
            acc[at, CHANNEL_DIM:] += jnp.dot(rounded, gs[...], preferred_element_type=jnp.float32)
            acc[at, :CHANNEL_DIM] += jnp.dot(score_grad, qs[...], preferred_element_type=jnp.float32)
            dqt[...] += lax.dot_general(
                kvs[at, :CHANNEL_DIM], score_grad, (((0,), (0,)), ((), ())),
                preferred_element_type=jnp.float32,
            )

        for h in range(BUNDLE):
            dq_ref[rows, h * CHANNEL_DIM : (h + 1) * CHANNEL_DIM] = (
                (dqt[:, h * HALF : (h + 1) * HALF] * scale).T.astype(jnp.bfloat16)
            )

    @pl.loop(0, spans)
    def _(r):
        p = span_ref[r]
        at = pl.ds(pl.multiple_of(p * HALF, HALF), HALF)
        to = pl.ds(pl.multiple_of(r * HALF, HALF), HALF)
        dkv_ref[to, :CHANNEL_DIM] = (acc[at, :CHANNEL_DIM] * scale).astype(jnp.bfloat16)
        dkv_ref[to, CHANNEL_DIM:] = acc[at, CHANNEL_DIM:].astype(jnp.bfloat16)


def attention(q, g, kv, span_order, doc_lengths):
    tokens = q.shape[0]
    length = kv.shape[0]
    ends = jnp.cumsum(doc_lengths)
    mine = lax.axis_index("ctx")
    blocks = lax.dynamic_slice_in_dim(span_order, mine * 2, 2)
    positions = blocks[:, None] * HALF + jnp.arange(HALF, dtype=jnp.int32)[None, :]
    starts = jnp.max(
        jnp.where(positions[:, :, None] >= ends[None, None, :], ends[None, None, :], 0), axis=2
    ).astype(jnp.int32)
    first = (starts[:, 0] // HALF).astype(jnp.int32)
    smem = pl.BlockSpec(memory_space=pltpu.SMEM)
    vmem = pl.BlockSpec(memory_space=pltpu.VMEM)
    lanes = BUNDLE * HALF
    return pl.pallas_call(
        attention_kernel,
        out_shape=(
            jax.ShapeDtypeStruct((tokens, lanes), jnp.bfloat16),
            jax.ShapeDtypeStruct((length, 2 * CHANNEL_DIM), jnp.bfloat16),
        ),
        in_specs=[smem, smem, smem, vmem, vmem, vmem, vmem],
        out_specs=(vmem, vmem),
        scratch_shapes=[
            pltpu.VMEM((length, 2 * CHANNEL_DIM), jnp.bfloat16),
            pltpu.VMEM((lanes, CHANNEL_DIM), jnp.bfloat16),
            pltpu.VMEM((lanes, CHANNEL_DIM), jnp.bfloat16),
            pltpu.VMEM((length, lanes), jnp.float32),
            pltpu.VMEM((length, lanes), jnp.float32),
            pltpu.VMEM((length, 2 * CHANNEL_DIM), jnp.float32),
            pltpu.VMEM((CHANNEL_DIM, lanes), jnp.float32),
        ],
        compiler_params=pltpu.CompilerParams(vmem_limit_bytes=40 * 1024 * 1024),
        name="attention",
    )(span_order, blocks, first, starts, q, g, kv)


def shards(inputs, out_grad, w_query, w_key, value_projection, w_out, doc_lengths, span_order):
    tokens = inputs.shape[0]
    peers = lax.axis_size("ctx")
    query, context_grad, gathered = front(
        inputs, out_grad, w_query, w_key, value_projection, w_out, peers
    )
    query_grad, pieces = attention(
        query, context_grad, gathered.reshape(peers * tokens, -1), span_order, doc_lengths
    )
    pieces = pieces.reshape(RING, 2, 2, tokens, -1)
    return back(query_grad, pieces, w_query, w_key, value_projection)


def solution(mesh):
    in_specs = (
        P("ctx", None),
        P("ctx", "head"),
        P(None, "head"),
        P(None, "head"),
        P(None, "head"),
        P("head", None),
        P(),
        P(),
    )
    return jax.shard_map(
        shards, mesh=mesh, in_specs=in_specs, out_specs=P("ctx", "head"), check_vma=False
    )
```

```python
import math

import jax
import jax.numpy as jnp
from jax import lax
from jax.experimental import pallas as pl
from jax.experimental.pallas import tpu as pltpu
from jax.sharding import PartitionSpec as P

ASKER_NUM = 32
SHARED_KV_NUM = 8
CHANNEL_DIM = 128
BUNDLE = ASKER_NUM // SHARED_KV_NUM
HALF = 128
TILE = 256
RING = 4
FEATURES = 512
CHUNKS = 4
OFFSETS = ((2, 1), (2, 0), (1, 1), (3, 1), (1, 0), (3, 0), (0, 1))
LOG2E = 1.4426950408889634
MASKED = -1e30
MESH = pl.DeviceIdType.MESH


def remote(src, dst, send, receive, place):
    return pltpu.make_async_remote_copy(
        src_ref=src, dst_ref=dst, send_sem=send, recv_sem=receive,
        device_id=place, device_id_type=MESH,
    )


def greet(places):
    barrier = pltpu.get_barrier_semaphore()
    for place in places:
        pl.semaphore_signal(barrier, inc=1, device_id=place, device_id_type=MESH)
    pl.semaphore_wait(barrier, len(places))


def neighbours():
    head = lax.axis_index("head")
    ctx = lax.axis_index("ctx")
    far, depth = head // RING, head % RING
    line, near, core = ctx // 4, (ctx // 2) % 2, ctx % 2

    def head_of(f, d):
        return f * RING + d

    def ctx_of(r, n, c):
        return r * 4 + n * 2 + c

    places = {
        "head_up": (head_of(far, (depth + 1) % RING), ctx),
        "head_down": (head_of(far, (depth + 3) % RING), ctx),
        "head_pair": (head_of(1 - far, depth), ctx),
        "ctx_up": (head, ctx_of((line + 1) % RING, near, core)),
        "ctx_down": (head, ctx_of((line + 3) % RING, near, core)),
        "ctx_pair": (head, ctx_of(line, 1 - near, core)),
        "sibling": (head, ctx_of(line, near, 1 - core)),
    }
    return places, (far, depth), (line, near, core)


class Gather:
    def __init__(self, source, block, half, pair, ring, sends, receives, up, down, across):
        other = 1 - pair
        before, after, opposite = (ring + 3) % RING, (ring + 1) % RING, (ring + 2) % RING
        self.copies = []
        own = block(pair, ring)
        plan = [
            (source(0), half(pair, ring, 0), half(pair, before, 0), up),
            (source(1), half(pair, ring, 1), half(pair, after, 1), down),
            (source(None), own, block(other, ring), across),
            (source(1), half(pair, ring, 1), half(pair, before, 1), up),
            (source(0), half(pair, ring, 0), half(pair, after, 0), down),
            (half(pair, before, 0), half(pair, before, 0), half(pair, opposite, 0), up),
            (half(pair, after, 1), half(pair, after, 1), half(pair, opposite, 1), down),
            (half(other, ring, 0), half(other, ring, 0), half(other, before, 0), up),
            (half(other, ring, 1), half(other, ring, 1), half(other, after, 1), down),
            (half(other, ring, 1), half(other, ring, 1), half(other, before, 1), up),
            (half(other, ring, 0), half(other, ring, 0), half(other, after, 0), down),
            (half(other, before, 0), half(other, before, 0), half(other, opposite, 0), up),
            (half(other, after, 1), half(other, after, 1), half(other, opposite, 1), down),
        ]
        for k, (src, dst, landed, place) in enumerate(plan):
            self.copies.append(
                (
                    remote(src, dst, sends.at[k], receives.at[k], place),
                    remote(landed, landed, sends.at[k], receives.at[k], place),
                )
            )

    def start(self, *which):
        for k in which:
            self.copies[k][0].start()

    def arrive(self, *which):
        for k in which:
            self.copies[k][1].wait_recv()

    def drain(self):
        for sent, landed in self.copies:
            sent.wait_send()


def front_kernel(
    x_hbm, og_hbm, wq_hbm, wk_hbm, wv_hbm, wo_hbm,
    q_ref, g_ref, kv_ref,
    x, wq, wkv, wo, og, acc,
    loads, head_send, head_receive, ctx_send, ctx_receive, sibling_send, sibling_receive,
):
    places, (far, depth), (line, near, core) = neighbours()
    me = far * RING + depth
    local = [
        pltpu.make_async_copy(x_hbm, x, loads.at[0]),
        pltpu.make_async_copy(wk_hbm, wkv.at[:, :CHANNEL_DIM], loads.at[1]),
        pltpu.make_async_copy(wv_hbm, wkv.at[:, CHANNEL_DIM:], loads.at[2]),
        pltpu.make_async_copy(wq_hbm, wq, loads.at[3]),
        pltpu.make_async_copy(og_hbm, og.at[me], loads.at[4]),
        pltpu.make_async_copy(wo_hbm, wo, loads.at[5]),
    ]
    for copy in local:
        copy.start()
    greet(list(places.values()))

    heads = Gather(
        lambda k: og_hbm if k is None else og_hbm.at[pl.ds(k * HALF, HALF), :],
        lambda p, r: og.at[p * RING + r],
        lambda p, r, k: og.at[p * RING + r, pl.ds(k * HALF, HALF), :],
        far, depth, head_send, head_receive,
        places["head_up"], places["head_down"], places["head_pair"],
    )
    heads.start(0, 1, 2, 3, 4)

    def slot(p, r, c=core):
        return r * 4 + p * 2 + c

    spread = Gather(
        lambda k: kv_ref.at[slot(near, line)]
        if k is None
        else kv_ref.at[slot(near, line), pl.ds(k * HALF, HALF), :],
        lambda p, r: kv_ref.at[slot(p, r)],
        lambda p, r, k: kv_ref.at[slot(p, r), pl.ds(k * HALF, HALF), :],
        near, line, ctx_send, ctx_receive,
        places["ctx_up"], places["ctx_down"], places["ctx_pair"],
    )
    turns = [(p, (line + d) % RING) for p in (near, 1 - near) for d in (0, 3, 1, 2)]
    passed = [
        (
            remote(
                kv_ref.at[slot(p, r)], kv_ref.at[slot(p, r)],
                sibling_send.at[k], sibling_receive.at[k], places["sibling"],
            ),
            remote(
                kv_ref.at[slot(p, r, 1 - core)], kv_ref.at[slot(p, r, 1 - core)],
                sibling_send.at[k], sibling_receive.at[k], places["sibling"],
            ),
        )
        for k, (p, r) in enumerate(turns)
    ]

    def features(p, r):
        f = p * RING + r
        return lax.dot_general(
            og[f], wo[:, pl.ds(pl.multiple_of(f * FEATURES, FEATURES), FEATURES)],
            (((1,), (1,)), ((), ())), preferred_element_type=jnp.float32,
        )

    for k in (0, 1, 2):
        local[k].wait()
    kv_ref[slot(near, line)] = jnp.dot(
        x[...], wkv[...], preferred_element_type=jnp.float32
    ).astype(jnp.bfloat16)
    local[3].wait()
    q_ref[...] = jnp.dot(x[...], wq[...], preferred_element_type=jnp.float32).astype(jnp.bfloat16)
    spread.start(0, 1, 2, 3, 4)
    passed[0][0].start()
    heads.arrive(0)
    heads.start(5)
    heads.arrive(1)
    heads.start(6)
    local[4].wait()
    local[5].wait()
    acc[...] = features(far, depth)

    before, after, opposite = (depth + 3) % RING, (depth + 1) % RING, (depth + 2) % RING
    spread.arrive(2)
    spread.start(7, 8, 9, 10)
    passed[4][0].start()
    spread.arrive(0)
    spread.start(5)
    spread.arrive(1)
    spread.start(6)
    heads.arrive(2)
    heads.start(7, 8, 9, 10)
    heads.arrive(3)
    acc[...] += features(far, before)
    heads.arrive(4)
    acc[...] += features(far, after)
    spread.arrive(3)
    passed[1][0].start()
    spread.arrive(4)
    passed[2][0].start()
    spread.arrive(7)
    spread.start(11)
    spread.arrive(8)
    spread.start(12)
    acc[...] += features(1 - far, depth)
    heads.arrive(5, 6)
    acc[...] += features(far, opposite)
    spread.arrive(5, 6)
    passed[3][0].start()
    spread.arrive(9)
    passed[5][0].start()
    spread.arrive(10)
    passed[6][0].start()
    heads.arrive(7)
    heads.start(11)
    heads.arrive(8)
    heads.start(12)
    spread.arrive(11, 12)
    passed[7][0].start()
    heads.arrive(9)
    acc[...] += features(1 - far, before)
    heads.arrive(10)
    acc[...] += features(1 - far, after)
    heads.arrive(11, 12)
    g_ref[...] = (acc[...] + features(1 - far, opposite)).astype(jnp.bfloat16)
    for sent, landed in passed:
        landed.wait_recv()
    heads.drain()
    spread.drain()
    for sent, landed in passed:
        sent.wait_send()


def front(inputs, out_grad, w_query, w_key, value_projection, w_out, peers):
    tokens, width = inputs.shape
    lanes = w_query.shape[1]
    hbm = pl.BlockSpec(memory_space=pltpu.HBM)
    vmem = pl.BlockSpec(memory_space=pltpu.VMEM)
    return pl.pallas_call(
        front_kernel,
        out_shape=(
            jax.ShapeDtypeStruct((tokens, lanes), jnp.bfloat16),
            jax.ShapeDtypeStruct((tokens, lanes), jnp.bfloat16),
            jax.ShapeDtypeStruct((peers, tokens, 2 * CHANNEL_DIM), jnp.bfloat16),
        ),
        in_specs=[hbm] * 6,
        out_specs=(vmem, vmem, vmem),
        scratch_shapes=[
            pltpu.VMEM((tokens, width), jnp.bfloat16),
            pltpu.VMEM((width, lanes), jnp.bfloat16),
            pltpu.VMEM((width, 2 * CHANNEL_DIM), jnp.bfloat16),
            pltpu.VMEM((lanes, width), jnp.bfloat16),
            pltpu.VMEM((2 * RING, tokens, FEATURES), jnp.bfloat16),
            pltpu.VMEM((tokens, lanes), jnp.float32),
            pltpu.SemaphoreType.DMA((6,)),
            pltpu.SemaphoreType.DMA((13,)),
            pltpu.SemaphoreType.DMA((13,)),
            pltpu.SemaphoreType.DMA((13,)),
            pltpu.SemaphoreType.DMA((13,)),
            pltpu.SemaphoreType.DMA((8,)),
            pltpu.SemaphoreType.DMA((8,)),
        ],
        compiler_params=pltpu.CompilerParams(
            collective_id=0, has_side_effects=True, vmem_limit_bytes=60 * 1024 * 1024
        ),
        name="front",
    )(inputs, out_grad, w_query, w_key, value_projection, w_out)


class Reduce:
    def __init__(self, held, gone, sums, ring, sends, receives, up, down):
        self.held, self.gone, self.sums = held, gone, sums
        self.before, self.after = (ring + 3) % RING, (ring + 1) % RING
        opposite = (ring + 2) % RING
        self.cut = held.shape[2] // 2
        low, high = pl.ds(0, self.cut), pl.ds(self.cut, self.cut)
        plan = [
            (held.at[opposite, :, low], gone.at[0], up),
            (held.at[opposite, :, high], gone.at[1], down),
            (held.at[self.after, :, high], sums.at[0, :, high], up),
            (held.at[self.before, :, low], sums.at[1, :, low], down),
            (held.at[self.after, :, low], sums.at[0, :, low], up),
            (held.at[self.before, :, high], sums.at[1, :, high], down),
        ]
        self.copies = [
            remote(src, dst, sends.at[k], receives.at[k], place)
            for k, (src, dst, place) in enumerate(plan)
        ]

    def start(self, *which):
        for k in which:
            self.copies[k].start()

    def relay(self):
        low, high = slice(0, self.cut), slice(self.cut, 2 * self.cut)
        for k, r, rows in ((0, self.after, low), (1, self.before, high)):
            self.copies[k].wait_recv()
            for p in range(2):
                self.held[r, p, rows] = (
                    self.held[r, p, rows].astype(jnp.float32)
                    + self.gone[k, p].astype(jnp.float32)
                ).astype(jnp.bfloat16)
            self.start(4 + k)

    def arrive(self):
        for k in (2, 3, 4, 5):
            self.copies[k].wait_recv()

    def total(self, p):
        return self.sums[0, p].astype(jnp.float32) + self.sums[1, p].astype(jnp.float32)

    def drain(self):
        for copy in self.copies:
            copy.wait_send()


def back_kernel(
    dq_ref, p_ref, wq, wk, wv,
    out_ref,
    wkv, side, held, inbox, dkv, parts, leaving, left, gone, sums, crossing, crossed,
    loads, side_send, side_receive, ctx_send, ctx_receive, head_send, head_receive,
    pair_send, pair_receive,
):
    places, (far, depth), (line, near, core) = neighbours()
    head, ctx = lax.axis_index("head"), lax.axis_index("ctx")
    others = [
        ((line + d) % RING, (near + n) % 2) for d, n in OFFSETS
    ]
    around = [(head, r * 4 + p * 2 + core) for r, p in others]
    local = [
        pltpu.make_async_copy(wk, wkv.at[:, :CHANNEL_DIM], loads.at[0]),
        pltpu.make_async_copy(wv, wkv.at[:, CHANNEL_DIM:], loads.at[1]),
    ]
    for copy in local:
        copy.start()
    greet([places["sibling"], places["head_up"], places["head_down"], places["head_pair"], *around])

    rows = p_ref.shape[4]
    swaps = [
        remote(
            p_ref.at[:, :, 1 - core, c], side.at[c],
            side_send.at[c], side_receive.at[c], places["sibling"],
        )
        for c in range(CHUNKS)
    ]
    for copy in swaps:
        copy.start()
    sends = [
        [
            remote(
                held.at[c, r, p], inbox.at[c, k],
                ctx_send.at[c, k], ctx_receive.at[c, k], around[k],
            )
            for k, (r, p) in enumerate(others)
        ]
        for c in range(CHUNKS)
    ]
    rounds = [
        Reduce(
            leaving.at[c], gone.at[c], sums.at[c], depth,
            head_send.at[c], head_receive.at[c], places["head_up"], places["head_down"],
        )
        for c in range(CHUNKS)
    ]
    across = [
        remote(
            crossing.at[c], crossed.at[c],
            pair_send.at[c], pair_receive.at[c], places["head_pair"],
        )
        for c in range(CHUNKS)
    ]

    def join(c, r, p):
        return p_ref[r, p, core, c].astype(jnp.float32) + side[c, r, p].astype(jnp.float32)

    for c in range(CHUNKS):
        swaps[c].wait_recv()
        for k, (r, p) in enumerate(others):
            held[c, r, p] = join(c, r, p).astype(jnp.bfloat16)
        for copy in sends[c]:
            copy.start()

    @pl.loop(0, 2 * RING)
    def _(f):
        parts[f] = lax.dot_general(
            dq_ref[...], wq[pl.ds(pl.multiple_of(f * FEATURES, FEATURES), FEATURES), :],
            (((1,), (1,)), ((), ())), preferred_element_type=jnp.float32,
        )

    for copy in local:
        copy.wait()

    def term(c, f):
        return parts[f, c * rows : (c + 1) * rows, :] + lax.dot_general(
            dkv[c], wkv[pl.ds(pl.multiple_of(f * FEATURES, FEATURES), FEATURES), :],
            (((1,), (1,)), ((), ())), preferred_element_type=jnp.float32,
        )

    def issue(c):
        mine = join(c, line, near)
        for k in range(len(sends[c])):
            sends[c][k].wait_recv()
            mine = mine + inbox[c, k].astype(jnp.float32)
        dkv[c] = mine.astype(jnp.bfloat16)
        for d, ready in ((2, (0, 1)), (1, (2,)), (3, (3,))):
            r = (depth + d) % RING
            for p in range(2):
                leaving[c, r, p] = term(c, p * RING + r).astype(jnp.bfloat16)
            rounds[c].start(*ready)
        for p in range(2):
            left[c, p] = term(c, p * RING + depth)

    def cross(c):
        rounds[c].arrive()
        crossing[c] = (left[c, 1 - far] + rounds[c].total(1 - far)).astype(jnp.bfloat16)
        across[c].start()
        left[c, far] = left[c, far] + rounds[c].total(far)

    issue(0)
    for c in range(1, CHUNKS):
        issue(c)
        rounds[c - 1].relay()
        if c > 1:
            cross(c - 2)
    rounds[CHUNKS - 1].relay()
    cross(CHUNKS - 2)
    cross(CHUNKS - 1)
    for c in range(CHUNKS):
        across[c].wait_recv()
        out_ref[c * rows : (c + 1) * rows, :] = (
            left[c, far] + crossed[c].astype(jnp.float32)
        ).astype(jnp.bfloat16)
    for c in range(CHUNKS):
        swaps[c].wait_send()
        across[c].wait_send()
        rounds[c].drain()
        for copy in sends[c]:
            copy.wait_send()


def back(query_grad, pieces, w_query, w_key, value_projection):
    tokens, lanes = query_grad.shape
    width = w_query.shape[0]
    rows = tokens // CHUNKS
    vmem = pl.BlockSpec(memory_space=pltpu.VMEM)
    wide = 2 * CHANNEL_DIM
    bf16, f32 = jnp.bfloat16, jnp.float32
    dma = pltpu.SemaphoreType.DMA
    return pl.pallas_call(
        back_kernel,
        out_shape=jax.ShapeDtypeStruct((tokens, FEATURES), bf16),
        in_specs=[vmem] * 5,
        out_specs=vmem,
        scratch_shapes=[
            pltpu.VMEM((width, wide), bf16),
            pltpu.VMEM((CHUNKS, RING, 2, rows, wide), bf16),
            pltpu.VMEM((CHUNKS, RING, 2, rows, wide), bf16),
            pltpu.VMEM((CHUNKS, len(OFFSETS), rows, wide), bf16),
            pltpu.VMEM((CHUNKS, rows, wide), bf16),
            pltpu.VMEM((2 * RING, tokens, FEATURES), f32),
            pltpu.VMEM((CHUNKS, RING, 2, rows, FEATURES), bf16),
            pltpu.VMEM((CHUNKS, 2, rows, FEATURES), f32),
            pltpu.VMEM((CHUNKS, 2, 2, rows // 2, FEATURES), bf16),
            pltpu.VMEM((CHUNKS, 2, 2, rows, FEATURES), bf16),
            pltpu.VMEM((CHUNKS, rows, FEATURES), bf16),
            pltpu.VMEM((CHUNKS, rows, FEATURES), bf16),
            dma((2,)),
            dma((CHUNKS,)),
            dma((CHUNKS,)),
            dma((CHUNKS, len(OFFSETS))),
            dma((CHUNKS, len(OFFSETS))),
            dma((CHUNKS, 6)),
            dma((CHUNKS, 6)),
            dma((CHUNKS,)),
            dma((CHUNKS,)),
        ],
        compiler_params=pltpu.CompilerParams(
            collective_id=1, has_side_effects=True, vmem_limit_bytes=32 * 1024 * 1024
        ),
        name="back",
    )(query_grad, pieces, w_query, w_key, value_projection)


def attention_kernel(
    span_ref, length_ref, q_ref, g_ref, kv_ref,
    dq_ref, dkv_ref,
    kvs, qs, gs, s_buf, d_buf, acc, dqt,
):
    exponent = LOG2E / math.sqrt(CHANNEL_DIM)
    scale = 1.0 / math.sqrt(CHANNEL_DIM)
    spans = span_ref.shape[0]

    @pl.loop(0, spans)
    def _(r):
        p = span_ref[r]
        kvs[pl.ds(pl.multiple_of(p * HALF, HALF), HALF), :] = kv_ref[
            pl.ds(pl.multiple_of(r * HALF, HALF), HALF), :
        ]
        acc[pl.ds(pl.multiple_of(r * HALF, HALF), HALF), :] = jnp.zeros((HALF, 2 * CHANNEL_DIM), jnp.float32)

    lanes = BUNDLE * HALF
    for b in range(2):
        rows = slice(b * HALF, (b + 1) * HALF)
        for h in range(BUNDLE):
            cols = slice(h * CHANNEL_DIM, (h + 1) * CHANNEL_DIM)
            qs[h * HALF : (h + 1) * HALF, :] = q_ref[rows, cols]
            gs[h * HALF : (h + 1) * HALF, :] = g_ref[rows, cols]
        c = span_ref[2 * lax.axis_index("ctx") + b]
        position = c * HALF + lax.broadcasted_iota(jnp.int32, (1, HALF), 1)
        start = jnp.zeros((1, HALF), jnp.int32)
        first = 0
        end = 0
        for k in range(length_ref.shape[0]):
            end = end + length_ref[k]
            start = jnp.where(position >= end, end, start)
            first = jnp.where(c * HALF >= end, end, first)
        low = first // TILE
        high = c // (TILE // HALF) + 1

        def gather_stats(t, carry):
            top, total, inner = carry
            at = pl.ds(pl.multiple_of(t * TILE, TILE), TILE)
            keys = kvs[at, :CHANNEL_DIM]
            values = kvs[at, CHANNEL_DIM:]
            key_position = t * TILE + lax.broadcasted_iota(jnp.int32, (TILE, HALF), 0)
            bias = jnp.where(
                (key_position <= position) & (key_position >= start), 0.0, MASKED
            )
            bias = jnp.concatenate([bias] * BUNDLE, axis=1)
            s = lax.dot_general(
                keys, qs[...], (((1,), (1,)), ((), ())), preferred_element_type=jnp.float32
            )
            s = s * exponent + bias
            s_buf[at, :] = s
            fresh = jnp.maximum(top, jnp.max(s, axis=0, keepdims=True))
            factor = jnp.exp2(top - fresh)
            e = jnp.exp2(s - fresh)
            slopes = lax.dot_general(
                values, gs[...], (((1,), (1,)), ((), ())), preferred_element_type=jnp.float32
            )
            d_buf[at, :] = slopes
            total = total * factor + jnp.sum(e, axis=0, keepdims=True)
            inner = inner * factor + jnp.sum(e * slopes, axis=0, keepdims=True)
            return fresh, total, inner

        zero = jnp.zeros((1, lanes), jnp.float32)
        top, total, inner = lax.fori_loop(
            low, high, gather_stats, (jnp.full((1, lanes), MASKED, jnp.float32), zero, zero)
        )
        delta = inner / total
        level = top + jnp.log2(total)
        dqt[...] = jnp.zeros_like(dqt)

        @pl.loop(low, high)
        def _(t):
            at = pl.ds(pl.multiple_of(t * TILE, TILE), TILE)
            probability = jnp.exp2(s_buf[at, :] - level)
            score_grad = (probability * (d_buf[at, :] - delta)).astype(jnp.bfloat16)
            rounded = probability.astype(jnp.bfloat16)
            acc[at, CHANNEL_DIM:] += jnp.dot(rounded, gs[...], preferred_element_type=jnp.float32)
            acc[at, :CHANNEL_DIM] += jnp.dot(score_grad, qs[...], preferred_element_type=jnp.float32)
            dqt[...] += lax.dot_general(
                kvs[at, :CHANNEL_DIM], score_grad, (((0,), (0,)), ((), ())),
                preferred_element_type=jnp.float32,
            )

        for h in range(BUNDLE):
            dq_ref[rows, h * CHANNEL_DIM : (h + 1) * CHANNEL_DIM] = (
                (dqt[:, h * HALF : (h + 1) * HALF] * scale).T.astype(jnp.bfloat16)
            )

    @pl.loop(0, spans)
    def _(r):
        p = span_ref[r]
        at = pl.ds(pl.multiple_of(p * HALF, HALF), HALF)
        to = pl.ds(pl.multiple_of(r * HALF, HALF), HALF)
        dkv_ref[to, :CHANNEL_DIM] = (acc[at, :CHANNEL_DIM] * scale).astype(jnp.bfloat16)
        dkv_ref[to, CHANNEL_DIM:] = acc[at, CHANNEL_DIM:].astype(jnp.bfloat16)


def attention(q, g, kv, span_order, doc_lengths):
    tokens = q.shape[0]
    length = kv.shape[0]
    smem = pl.BlockSpec(memory_space=pltpu.SMEM)
    vmem = pl.BlockSpec(memory_space=pltpu.VMEM)
    lanes = BUNDLE * HALF
    return pl.pallas_call(
        attention_kernel,
        out_shape=(
            jax.ShapeDtypeStruct((tokens, lanes), jnp.bfloat16),
            jax.ShapeDtypeStruct((length, 2 * CHANNEL_DIM), jnp.bfloat16),
        ),
        in_specs=[smem, smem, vmem, vmem, vmem],
        out_specs=(vmem, vmem),
        scratch_shapes=[
            pltpu.VMEM((length, 2 * CHANNEL_DIM), jnp.bfloat16),
            pltpu.VMEM((lanes, CHANNEL_DIM), jnp.bfloat16),
            pltpu.VMEM((lanes, CHANNEL_DIM), jnp.bfloat16),
            pltpu.VMEM((length, lanes), jnp.float32),
            pltpu.VMEM((length, lanes), jnp.float32),
            pltpu.VMEM((length, 2 * CHANNEL_DIM), jnp.float32),
            pltpu.VMEM((CHANNEL_DIM, lanes), jnp.float32),
        ],
        compiler_params=pltpu.CompilerParams(vmem_limit_bytes=40 * 1024 * 1024),
        name="attention",
    )(span_order, doc_lengths, q, g, kv)


def shards(inputs, out_grad, w_query, w_key, value_projection, w_out, doc_lengths, span_order):
    tokens = inputs.shape[0]
    peers = lax.axis_size("ctx")
    query, context_grad, gathered = front(
        inputs, out_grad, w_query, w_key, value_projection, w_out, peers
    )
    query_grad, pieces = attention(
        query, context_grad, gathered.reshape(peers * tokens, -1), span_order, doc_lengths
    )
    pieces = pieces.reshape(RING, 2, 2, CHUNKS, tokens // CHUNKS, -1)
    return back(query_grad, pieces, w_query, w_key, value_projection)


def solution(mesh):
    in_specs = (
        P("ctx", None),
        P("ctx", "head"),
        P(None, "head"),
        P(None, "head"),
        P(None, "head"),
        P("head", None),
        P(),
        P(),
    )
    return jax.shard_map(
        shards, mesh=mesh, in_specs=in_specs, out_specs=P("ctx", "head"), check_vma=False
    )
```

```python
import math

import jax
import jax.numpy as jnp
from jax import lax
from jax.experimental import pallas as pl
from jax.experimental.pallas import tpu as pltpu
from jax.sharding import PartitionSpec as P

ASKER_NUM = 32
SHARED_KV_NUM = 8
CHANNEL_DIM = 128
BUNDLE = ASKER_NUM // SHARED_KV_NUM
HALF = 128
TILE = 256
RING = 4
FEATURES = 512
CHUNKS = 4
OFFSETS = ((2, 1), (2, 0), (1, 1), (3, 1), (1, 0), (3, 0), (0, 1))
LOG2E = 1.4426950408889634
MASKED = -1e30
GRANT = 60 * 1024 * 1024
MESH = pl.DeviceIdType.MESH


def remote(src, dst, send, receive, place):
    return pltpu.make_async_remote_copy(
        src_ref=src, dst_ref=dst, send_sem=send, recv_sem=receive,
        device_id=place, device_id_type=MESH,
    )


def greet(places):
    barrier = pltpu.get_barrier_semaphore()
    for place in places:
        pl.semaphore_signal(barrier, inc=1, device_id=place, device_id_type=MESH)
    pl.semaphore_wait(barrier, len(places))


def neighbours():
    head = lax.axis_index("head")
    ctx = lax.axis_index("ctx")
    far, depth = head // RING, head % RING
    line, near, core = ctx // 4, (ctx // 2) % 2, ctx % 2

    def head_of(f, d):
        return f * RING + d

    def ctx_of(r, n, c):
        return r * 4 + n * 2 + c

    places = {
        "head_up": (head_of(far, (depth + 1) % RING), ctx),
        "head_down": (head_of(far, (depth + 3) % RING), ctx),
        "head_pair": (head_of(1 - far, depth), ctx),
        "ctx_up": (head, ctx_of((line + 1) % RING, near, core)),
        "ctx_down": (head, ctx_of((line + 3) % RING, near, core)),
        "ctx_pair": (head, ctx_of(line, 1 - near, core)),
        "sibling": (head, ctx_of(line, near, 1 - core)),
    }
    return places, (far, depth), (line, near, core)


class Gather:
    def __init__(self, source, block, half, pair, ring, sends, receives, up, down, across):
        other = 1 - pair
        before, after, opposite = (ring + 3) % RING, (ring + 1) % RING, (ring + 2) % RING
        self.copies = []
        own = block(pair, ring)
        plan = [
            (source(0), half(pair, ring, 0), half(pair, before, 0), up),
            (source(1), half(pair, ring, 1), half(pair, after, 1), down),
            (source(None), own, block(other, ring), across),
            (source(1), half(pair, ring, 1), half(pair, before, 1), up),
            (source(0), half(pair, ring, 0), half(pair, after, 0), down),
            (half(pair, before, 0), half(pair, before, 0), half(pair, opposite, 0), up),
            (half(pair, after, 1), half(pair, after, 1), half(pair, opposite, 1), down),
            (half(other, ring, 0), half(other, ring, 0), half(other, before, 0), up),
            (half(other, ring, 1), half(other, ring, 1), half(other, after, 1), down),
            (half(other, ring, 1), half(other, ring, 1), half(other, before, 1), up),
            (half(other, ring, 0), half(other, ring, 0), half(other, after, 0), down),
            (half(other, before, 0), half(other, before, 0), half(other, opposite, 0), up),
            (half(other, after, 1), half(other, after, 1), half(other, opposite, 1), down),
        ]
        for k, (src, dst, landed, place) in enumerate(plan):
            self.copies.append(
                (
                    remote(src, dst, sends.at[k], receives.at[k], place),
                    remote(landed, landed, sends.at[k], receives.at[k], place),
                )
            )

    def start(self, *which):
        for k in which:
            self.copies[k][0].start()

    def arrive(self, *which):
        for k in which:
            self.copies[k][1].wait_recv()

    def drain(self):
        for sent, landed in self.copies:
            sent.wait_send()


def front_kernel(
    x_hbm, og_hbm, wq_hbm, wk_hbm, wv_hbm, wo_hbm,
    q_hbm, g_hbm, kv_hbm,
    x, wq, wkv, wo, og, acc, q_ref, g_ref, kv_ref,
    loads, stores, head_send, head_receive, ctx_send, ctx_receive, sibling_send, sibling_receive,
):
    places, (far, depth), (line, near, core) = neighbours()
    me = far * RING + depth
    local = [
        pltpu.make_async_copy(x_hbm, x, loads.at[0]),
        pltpu.make_async_copy(wk_hbm, wkv.at[:, :CHANNEL_DIM], loads.at[1]),
        pltpu.make_async_copy(wv_hbm, wkv.at[:, CHANNEL_DIM:], loads.at[2]),
        pltpu.make_async_copy(wq_hbm, wq, loads.at[3]),
        pltpu.make_async_copy(og_hbm, og.at[me], loads.at[4]),
        pltpu.make_async_copy(wo_hbm, wo, loads.at[5]),
    ]
    for copy in local:
        copy.start()
    saved = [
        pltpu.make_async_copy(q_ref, q_hbm, stores.at[0]),
        pltpu.make_async_copy(kv_ref, kv_hbm, stores.at[1]),
        pltpu.make_async_copy(g_ref, g_hbm, stores.at[2]),
    ]
    greet(list(places.values()))

    heads = Gather(
        lambda k: og_hbm if k is None else og_hbm.at[pl.ds(k * HALF, HALF), :],
        lambda p, r: og.at[p * RING + r],
        lambda p, r, k: og.at[p * RING + r, pl.ds(k * HALF, HALF), :],
        far, depth, head_send, head_receive,
        places["head_up"], places["head_down"], places["head_pair"],
    )
    heads.start(0, 1, 2, 3, 4)

    def slot(p, r, c=core):
        return r * 4 + p * 2 + c

    spread = Gather(
        lambda k: kv_ref.at[slot(near, line)]
        if k is None
        else kv_ref.at[slot(near, line), pl.ds(k * HALF, HALF), :],
        lambda p, r: kv_ref.at[slot(p, r)],
        lambda p, r, k: kv_ref.at[slot(p, r), pl.ds(k * HALF, HALF), :],
        near, line, ctx_send, ctx_receive,
        places["ctx_up"], places["ctx_down"], places["ctx_pair"],
    )
    turns = [(p, (line + d) % RING) for p in (near, 1 - near) for d in (0, 3, 1, 2)]
    passed = [
        (
            remote(
                kv_ref.at[slot(p, r)], kv_ref.at[slot(p, r)],
                sibling_send.at[k], sibling_receive.at[k], places["sibling"],
            ),
            remote(
                kv_ref.at[slot(p, r, 1 - core)], kv_ref.at[slot(p, r, 1 - core)],
                sibling_send.at[k], sibling_receive.at[k], places["sibling"],
            ),
        )
        for k, (p, r) in enumerate(turns)
    ]

    def features(p, r):
        f = p * RING + r
        return lax.dot_general(
            og[f], wo[:, pl.ds(pl.multiple_of(f * FEATURES, FEATURES), FEATURES)],
            (((1,), (1,)), ((), ())), preferred_element_type=jnp.float32,
        )

    for k in (0, 1, 2):
        local[k].wait()
    kv_ref[slot(near, line)] = jnp.dot(
        x[...], wkv[...], preferred_element_type=jnp.float32
    ).astype(jnp.bfloat16)
    local[3].wait()
    q_ref[...] = jnp.dot(x[...], wq[...], preferred_element_type=jnp.float32).astype(jnp.bfloat16)
    spread.start(0, 1, 2, 3, 4)
    passed[0][0].start()
    saved[0].start()
    heads.arrive(0)
    heads.start(5)
    heads.arrive(1)
    heads.start(6)
    local[4].wait()
    local[5].wait()
    acc[...] = features(far, depth)

    before, after, opposite = (depth + 3) % RING, (depth + 1) % RING, (depth + 2) % RING
    spread.arrive(2)
    spread.start(7, 8, 9, 10)
    passed[4][0].start()
    spread.arrive(0)
    spread.start(5)
    spread.arrive(1)
    spread.start(6)
    heads.arrive(2)
    heads.start(7, 8, 9, 10)
    heads.arrive(3)
    acc[...] += features(far, before)
    heads.arrive(4)
    acc[...] += features(far, after)
    spread.arrive(3)
    passed[1][0].start()
    spread.arrive(4)
    passed[2][0].start()
    spread.arrive(7)
    spread.start(11)
    spread.arrive(8)
    spread.start(12)
    acc[...] += features(1 - far, depth)
    heads.arrive(5, 6)
    acc[...] += features(far, opposite)
    spread.arrive(5, 6)
    passed[3][0].start()
    spread.arrive(9)
    passed[5][0].start()
    spread.arrive(10)
    passed[6][0].start()
    heads.arrive(7)
    heads.start(11)
    heads.arrive(8)
    heads.start(12)
    spread.arrive(11, 12)
    passed[7][0].start()
    heads.arrive(9)
    acc[...] += features(1 - far, before)
    heads.arrive(10)
    acc[...] += features(1 - far, after)
    for sent, landed in passed:
        landed.wait_recv()
    saved[1].start()
    heads.arrive(11, 12)
    g_ref[...] = (acc[...] + features(1 - far, opposite)).astype(jnp.bfloat16)
    saved[2].start()
    heads.drain()
    spread.drain()
    for sent, landed in passed:
        sent.wait_send()
    for copy in saved:
        copy.wait()


def front(inputs, out_grad, w_query, w_key, value_projection, w_out, peers):
    tokens, width = inputs.shape
    lanes = w_query.shape[1]
    hbm = pl.BlockSpec(memory_space=pl.ANY)
    return pl.pallas_call(
        front_kernel,
        out_shape=(
            jax.ShapeDtypeStruct((tokens, lanes), jnp.bfloat16),
            jax.ShapeDtypeStruct((tokens, lanes), jnp.bfloat16),
            jax.ShapeDtypeStruct((peers, tokens, 2 * CHANNEL_DIM), jnp.bfloat16),
        ),
        in_specs=[hbm] * 6,
        out_specs=(hbm, hbm, hbm),
        scratch_shapes=[
            pltpu.VMEM((tokens, width), jnp.bfloat16),
            pltpu.VMEM((width, lanes), jnp.bfloat16),
            pltpu.VMEM((width, 2 * CHANNEL_DIM), jnp.bfloat16),
            pltpu.VMEM((lanes, width), jnp.bfloat16),
            pltpu.VMEM((2 * RING, tokens, FEATURES), jnp.bfloat16),
            pltpu.VMEM((tokens, lanes), jnp.float32),
            pltpu.VMEM((tokens, lanes), jnp.bfloat16),
            pltpu.VMEM((tokens, lanes), jnp.bfloat16),
            pltpu.VMEM((peers, tokens, 2 * CHANNEL_DIM), jnp.bfloat16),
            pltpu.SemaphoreType.DMA((6,)),
            pltpu.SemaphoreType.DMA((3,)),
            pltpu.SemaphoreType.DMA((13,)),
            pltpu.SemaphoreType.DMA((13,)),
            pltpu.SemaphoreType.DMA((13,)),
            pltpu.SemaphoreType.DMA((13,)),
            pltpu.SemaphoreType.DMA((8,)),
            pltpu.SemaphoreType.DMA((8,)),
        ],
        compiler_params=pltpu.CompilerParams(
            collective_id=0, has_side_effects=True, vmem_limit_bytes=GRANT
        ),
        name="front",
    )(inputs, out_grad, w_query, w_key, value_projection, w_out)


class Reduce:
    def __init__(self, held, gone, sums, ring, sends, receives, up, down):
        self.held, self.gone, self.sums = held, gone, sums
        self.before, self.after = (ring + 3) % RING, (ring + 1) % RING
        opposite = (ring + 2) % RING
        self.cut = held.shape[2] // 2
        low, high = pl.ds(0, self.cut), pl.ds(self.cut, self.cut)
        plan = [
            (held.at[opposite, :, low], gone.at[0], up),
            (held.at[opposite, :, high], gone.at[1], down),
            (held.at[self.after, :, high], sums.at[0, :, high], up),
            (held.at[self.before, :, low], sums.at[1, :, low], down),
            (held.at[self.after, :, low], sums.at[0, :, low], up),
            (held.at[self.before, :, high], sums.at[1, :, high], down),
        ]
        self.copies = [
            remote(src, dst, sends.at[k], receives.at[k], place)
            for k, (src, dst, place) in enumerate(plan)
        ]

    def start(self, *which):
        for k in which:
            self.copies[k].start()

    def relay(self):
        low, high = slice(0, self.cut), slice(self.cut, 2 * self.cut)
        for k, r, rows in ((0, self.after, low), (1, self.before, high)):
            self.copies[k].wait_recv()
            for p in range(2):
                self.held[r, p, rows] = (
                    self.held[r, p, rows].astype(jnp.float32)
                    + self.gone[k, p].astype(jnp.float32)
                ).astype(jnp.bfloat16)
            self.start(4 + k)

    def arrive(self):
        for k in (2, 3, 4, 5):
            self.copies[k].wait_recv()

    def total(self, p):
        return self.sums[0, p].astype(jnp.float32) + self.sums[1, p].astype(jnp.float32)

    def drain(self):
        for copy in self.copies:
            copy.wait_send()


def back_kernel(
    dq_hbm, p_hbm, wq_hbm, wk_hbm, wv_hbm,
    out_ref,
    dq, mine, wq, wkv, side, held, inbox, dkv, parts, leaving, left, gone, sums, crossing, crossed,
    loads, side_send, side_receive, ctx_send, ctx_receive, head_send, head_receive,
    pair_send, pair_receive,
):
    places, (far, depth), (line, near, core) = neighbours()
    head, ctx = lax.axis_index("head"), lax.axis_index("ctx")
    others = [
        ((line + d) % RING, (near + n) % 2) for d, n in OFFSETS
    ]
    around = [(head, r * 4 + p * 2 + core) for r, p in others]
    local = [
        pltpu.make_async_copy(p_hbm.at[:, :, core], mine, loads.at[0]),
        pltpu.make_async_copy(dq_hbm, dq, loads.at[1]),
        pltpu.make_async_copy(wq_hbm, wq, loads.at[2]),
        pltpu.make_async_copy(wk_hbm, wkv.at[:, :CHANNEL_DIM], loads.at[3]),
        pltpu.make_async_copy(wv_hbm, wkv.at[:, CHANNEL_DIM:], loads.at[4]),
    ]
    for copy in local:
        copy.start()
    greet([places["sibling"], places["head_up"], places["head_down"], places["head_pair"], *around])

    rows = mine.shape[3]
    swaps = [
        remote(
            p_hbm.at[:, :, 1 - core, c], side.at[c],
            side_send.at[c], side_receive.at[c], places["sibling"],
        )
        for c in range(CHUNKS)
    ]
    for copy in swaps:
        copy.start()
    sends = [
        [
            remote(
                held.at[c, r, p], inbox.at[c, k],
                ctx_send.at[c, k], ctx_receive.at[c, k], around[k],
            )
            for k, (r, p) in enumerate(others)
        ]
        for c in range(CHUNKS)
    ]
    rounds = [
        Reduce(
            leaving.at[c], gone.at[c], sums.at[c], depth,
            head_send.at[c], head_receive.at[c], places["head_up"], places["head_down"],
        )
        for c in range(CHUNKS)
    ]
    across = [
        remote(
            crossing.at[c], crossed.at[c],
            pair_send.at[c], pair_receive.at[c], places["head_pair"],
        )
        for c in range(CHUNKS)
    ]

    def join(c, r, p):
        return mine[r, p, c].astype(jnp.float32) + side[c, r, p].astype(jnp.float32)

    local[0].wait()
    for c in range(CHUNKS):
        swaps[c].wait_recv()
        for k, (r, p) in enumerate(others):
            held[c, r, p] = join(c, r, p).astype(jnp.bfloat16)
        for copy in sends[c]:
            copy.start()

    local[1].wait()
    local[2].wait()

    @pl.loop(0, 2 * RING)
    def _(f):
        parts[f] = lax.dot_general(
            dq[...], wq[pl.ds(pl.multiple_of(f * FEATURES, FEATURES), FEATURES), :],
            (((1,), (1,)), ((), ())), preferred_element_type=jnp.float32,
        )

    local[3].wait()
    local[4].wait()

    def term(c, f):
        return parts[f, c * rows : (c + 1) * rows, :] + lax.dot_general(
            dkv[c], wkv[pl.ds(pl.multiple_of(f * FEATURES, FEATURES), FEATURES), :],
            (((1,), (1,)), ((), ())), preferred_element_type=jnp.float32,
        )

    def issue(c):
        total = join(c, line, near)
        for k in range(len(sends[c])):
            sends[c][k].wait_recv()
            total = total + inbox[c, k].astype(jnp.float32)
        dkv[c] = total.astype(jnp.bfloat16)
        for d, ready in ((2, (0, 1)), (1, (2,)), (3, (3,))):
            r = (depth + d) % RING
            for p in range(2):
                leaving[c, r, p] = term(c, p * RING + r).astype(jnp.bfloat16)
            rounds[c].start(*ready)
        for p in range(2):
            left[c, p] = term(c, p * RING + depth)

    def cross(c):
        rounds[c].arrive()
        crossing[c] = (left[c, 1 - far] + rounds[c].total(1 - far)).astype(jnp.bfloat16)
        across[c].start()
        left[c, far] = left[c, far] + rounds[c].total(far)

    issue(0)
    for c in range(1, CHUNKS):
        issue(c)
        rounds[c - 1].relay()
        if c > 1:
            cross(c - 2)
    rounds[CHUNKS - 1].relay()
    cross(CHUNKS - 2)
    cross(CHUNKS - 1)
    for c in range(CHUNKS):
        across[c].wait_recv()
        out_ref[c * rows : (c + 1) * rows, :] = (
            left[c, far] + crossed[c].astype(jnp.float32)
        ).astype(jnp.bfloat16)
    for c in range(CHUNKS):
        swaps[c].wait_send()
        across[c].wait_send()
        rounds[c].drain()
        for copy in sends[c]:
            copy.wait_send()


def back(query_grad, pieces, w_query, w_key, value_projection):
    tokens, lanes = query_grad.shape
    width = w_query.shape[0]
    rows = tokens // CHUNKS
    vmem = pl.BlockSpec(memory_space=pltpu.VMEM)
    hbm = pl.BlockSpec(memory_space=pl.ANY)
    wide = 2 * CHANNEL_DIM
    bf16, f32 = jnp.bfloat16, jnp.float32
    dma = pltpu.SemaphoreType.DMA
    return pl.pallas_call(
        back_kernel,
        out_shape=jax.ShapeDtypeStruct((tokens, FEATURES), bf16),
        in_specs=[hbm] * 5,
        out_specs=vmem,
        scratch_shapes=[
            pltpu.VMEM((tokens, lanes), bf16),
            pltpu.VMEM((RING, 2, CHUNKS, rows, wide), bf16),
            pltpu.VMEM((width, lanes), bf16),
            pltpu.VMEM((width, wide), bf16),
            pltpu.VMEM((CHUNKS, RING, 2, rows, wide), bf16),
            pltpu.VMEM((CHUNKS, RING, 2, rows, wide), bf16),
            pltpu.VMEM((CHUNKS, len(OFFSETS), rows, wide), bf16),
            pltpu.VMEM((CHUNKS, rows, wide), bf16),
            pltpu.VMEM((2 * RING, tokens, FEATURES), f32),
            pltpu.VMEM((CHUNKS, RING, 2, rows, FEATURES), bf16),
            pltpu.VMEM((CHUNKS, 2, rows, FEATURES), f32),
            pltpu.VMEM((CHUNKS, 2, 2, rows // 2, FEATURES), bf16),
            pltpu.VMEM((CHUNKS, 2, 2, rows, FEATURES), bf16),
            pltpu.VMEM((CHUNKS, rows, FEATURES), bf16),
            pltpu.VMEM((CHUNKS, rows, FEATURES), bf16),
            dma((5,)),
            dma((CHUNKS,)),
            dma((CHUNKS,)),
            dma((CHUNKS, len(OFFSETS))),
            dma((CHUNKS, len(OFFSETS))),
            dma((CHUNKS, 6)),
            dma((CHUNKS, 6)),
            dma((CHUNKS,)),
            dma((CHUNKS,)),
        ],
        compiler_params=pltpu.CompilerParams(
            collective_id=1, has_side_effects=True, vmem_limit_bytes=GRANT
        ),
        name="back",
    )(query_grad, pieces, w_query, w_key, value_projection)


def attention_kernel(
    span_ref, length_ref, q_hbm, g_hbm, kv_hbm,
    dq_hbm, dkv_hbm,
    kvs, qs, gs, s_buf, d_buf, acc, dqt, q_ref, g_ref, dq_ref, dkv_ref,
    loads, stores,
):
    exponent = LOG2E / math.sqrt(CHANNEL_DIM)
    scale = 1.0 / math.sqrt(CHANNEL_DIM)
    spans = span_ref.shape[0]

    local = [
        pltpu.make_async_copy(q_hbm, q_ref, loads.at[0]),
        pltpu.make_async_copy(g_hbm, g_ref, loads.at[1]),
    ]
    for copy in local:
        copy.start()

    @pl.loop(0, spans)
    def _(r):
        p = span_ref[r]
        pltpu.make_async_copy(
            kv_hbm.at[pl.ds(pl.multiple_of(r * HALF, HALF), HALF), :],
            kvs.at[pl.ds(pl.multiple_of(p * HALF, HALF), HALF), :],
            loads.at[2],
        ).start()

    @pl.loop(0, spans)
    def _(r):
        acc[pl.ds(pl.multiple_of(r * HALF, HALF), HALF), :] = jnp.zeros((HALF, 2 * CHANNEL_DIM), jnp.float32)

    for copy in local:
        copy.wait()
    pltpu.make_async_copy(kv_hbm, kvs, loads.at[2]).wait()
    lanes = BUNDLE * HALF
    for b in range(2):
        rows = slice(b * HALF, (b + 1) * HALF)
        for h in range(BUNDLE):
            cols = slice(h * CHANNEL_DIM, (h + 1) * CHANNEL_DIM)
            qs[h * HALF : (h + 1) * HALF, :] = q_ref[rows, cols]
            gs[h * HALF : (h + 1) * HALF, :] = g_ref[rows, cols]
        c = span_ref[2 * lax.axis_index("ctx") + b]
        position = c * HALF + lax.broadcasted_iota(jnp.int32, (1, HALF), 1)
        start = jnp.zeros((1, HALF), jnp.int32)
        first = 0
        end = 0
        for k in range(length_ref.shape[0]):
            end = end + length_ref[k]
            start = jnp.where(position >= end, end, start)
            first = jnp.where(c * HALF >= end, end, first)
        low = first // TILE
        high = c // (TILE // HALF) + 1

        def gather_stats(t, carry):
            top, total, inner = carry
            at = pl.ds(pl.multiple_of(t * TILE, TILE), TILE)
            keys = kvs[at, :CHANNEL_DIM]
            values = kvs[at, CHANNEL_DIM:]
            key_position = t * TILE + lax.broadcasted_iota(jnp.int32, (TILE, HALF), 0)
            bias = jnp.where(
                (key_position <= position) & (key_position >= start), 0.0, MASKED
            )
            bias = jnp.concatenate([bias] * BUNDLE, axis=1)
            s = lax.dot_general(
                keys, qs[...], (((1,), (1,)), ((), ())), preferred_element_type=jnp.float32
            )
            s = s * exponent + bias
            s_buf[at, :] = s
            fresh = jnp.maximum(top, jnp.max(s, axis=0, keepdims=True))
            factor = jnp.exp2(top - fresh)
            e = jnp.exp2(s - fresh)
            slopes = lax.dot_general(
                values, gs[...], (((1,), (1,)), ((), ())), preferred_element_type=jnp.float32
            )
            d_buf[at, :] = slopes
            total = total * factor + jnp.sum(e, axis=0, keepdims=True)
            inner = inner * factor + jnp.sum(e * slopes, axis=0, keepdims=True)
            return fresh, total, inner

        zero = jnp.zeros((1, lanes), jnp.float32)
        top, total, inner = lax.fori_loop(
            low, high, gather_stats, (jnp.full((1, lanes), MASKED, jnp.float32), zero, zero)
        )
        delta = inner / total
        level = top + jnp.log2(total)
        dqt[...] = jnp.zeros_like(dqt)

        @pl.loop(low, high)
        def _(t):
            at = pl.ds(pl.multiple_of(t * TILE, TILE), TILE)
            probability = jnp.exp2(s_buf[at, :] - level)
            score_grad = (probability * (d_buf[at, :] - delta)).astype(jnp.bfloat16)
            rounded = probability.astype(jnp.bfloat16)
            acc[at, CHANNEL_DIM:] += jnp.dot(rounded, gs[...], preferred_element_type=jnp.float32)
            acc[at, :CHANNEL_DIM] += jnp.dot(score_grad, qs[...], preferred_element_type=jnp.float32)
            dqt[...] += lax.dot_general(
                kvs[at, :CHANNEL_DIM], score_grad, (((0,), (0,)), ((), ())),
                preferred_element_type=jnp.float32,
            )

        for h in range(BUNDLE):
            dq_ref[rows, h * CHANNEL_DIM : (h + 1) * CHANNEL_DIM] = (
                (dqt[:, h * HALF : (h + 1) * HALF] * scale).T.astype(jnp.bfloat16)
            )

    grads = pltpu.make_async_copy(dq_ref, dq_hbm, stores.at[0])
    grads.start()

    @pl.loop(0, spans)
    def _(r):
        p = span_ref[r]
        at = pl.ds(pl.multiple_of(p * HALF, HALF), HALF)
        to = pl.ds(pl.multiple_of(r * HALF, HALF), HALF)
        dkv_ref[to, :CHANNEL_DIM] = (acc[at, :CHANNEL_DIM] * scale).astype(jnp.bfloat16)
        dkv_ref[to, CHANNEL_DIM:] = acc[at, CHANNEL_DIM:].astype(jnp.bfloat16)
        pltpu.make_async_copy(dkv_ref.at[to, :], dkv_hbm.at[to, :], stores.at[1]).start()

    grads.wait()
    pltpu.make_async_copy(dkv_ref, dkv_hbm, stores.at[1]).wait()


def attention(q, g, kv, span_order, doc_lengths):
    tokens = q.shape[0]
    length = kv.shape[0]
    smem = pl.BlockSpec(memory_space=pltpu.SMEM)
    hbm = pl.BlockSpec(memory_space=pl.ANY)
    lanes = BUNDLE * HALF
    return pl.pallas_call(
        attention_kernel,
        out_shape=(
            jax.ShapeDtypeStruct((tokens, lanes), jnp.bfloat16),
            jax.ShapeDtypeStruct((length, 2 * CHANNEL_DIM), jnp.bfloat16),
        ),
        in_specs=[smem, smem, hbm, hbm, hbm],
        out_specs=(hbm, hbm),
        scratch_shapes=[
            pltpu.VMEM((length, 2 * CHANNEL_DIM), jnp.bfloat16),
            pltpu.VMEM((lanes, CHANNEL_DIM), jnp.bfloat16),
            pltpu.VMEM((lanes, CHANNEL_DIM), jnp.bfloat16),
            pltpu.VMEM((length, lanes), jnp.float32),
            pltpu.VMEM((length, lanes), jnp.float32),
            pltpu.VMEM((length, 2 * CHANNEL_DIM), jnp.float32),
            pltpu.VMEM((CHANNEL_DIM, lanes), jnp.float32),
            pltpu.VMEM((tokens, lanes), jnp.bfloat16),
            pltpu.VMEM((tokens, lanes), jnp.bfloat16),
            pltpu.VMEM((tokens, lanes), jnp.bfloat16),
            pltpu.VMEM((length, 2 * CHANNEL_DIM), jnp.bfloat16),
            pltpu.SemaphoreType.DMA((3,)),
            pltpu.SemaphoreType.DMA((2,)),
        ],
        compiler_params=pltpu.CompilerParams(vmem_limit_bytes=GRANT),
        name="attention",
    )(span_order, doc_lengths, q, g, kv)


def shards(inputs, out_grad, w_query, w_key, value_projection, w_out, doc_lengths, span_order):
    tokens = inputs.shape[0]
    peers = lax.axis_size("ctx")
    query, context_grad, gathered = front(
        inputs, out_grad, w_query, w_key, value_projection, w_out, peers
    )
    query_grad, pieces = attention(
        query, context_grad, gathered.reshape(peers * tokens, -1), span_order, doc_lengths
    )
    pieces = pieces.reshape(RING, 2, 2, CHUNKS, tokens // CHUNKS, -1)
    return back(query_grad, pieces, w_query, w_key, value_projection)


def solution(mesh):
    in_specs = (
        P("ctx", None),
        P("ctx", "head"),
        P(None, "head"),
        P(None, "head"),
        P(None, "head"),
        P("head", None),
        P(),
        P(),
    )
    return jax.shard_map(
        shards, mesh=mesh, in_specs=in_specs, out_specs=P("ctx", "head"), check_vma=False
    )
```

```python
import math

import jax
import jax.numpy as jnp
from jax import lax
from jax.experimental import pallas as pl
from jax.experimental.pallas import tpu as pltpu
from jax.sharding import PartitionSpec as P

ASKER_NUM = 32
SHARED_KV_NUM = 8
CHANNEL_DIM = 128
BUNDLE = ASKER_NUM // SHARED_KV_NUM
HALF = 128
TILE = 256
RING = 4
FEATURES = 512
CHUNKS = 4
OFFSETS = ((2, 1), (2, 0), (1, 1), (3, 1), (1, 0), (3, 0), (0, 1))
LOG2E = 1.4426950408889634
MASKED = -1e30
GRANT = 60 * 1024 * 1024
MESH = pl.DeviceIdType.MESH


def remote(src, dst, send, receive, place):
    return pltpu.make_async_remote_copy(
        src_ref=src, dst_ref=dst, send_sem=send, recv_sem=receive,
        device_id=place, device_id_type=MESH,
    )


def greet(places):
    barrier = pltpu.get_barrier_semaphore()
    for place in places:
        pl.semaphore_signal(barrier, inc=1, device_id=place, device_id_type=MESH)
    pl.semaphore_wait(barrier, len(places))


def neighbours():
    head = lax.axis_index("head")
    ctx = lax.axis_index("ctx")
    far, depth = head // RING, head % RING
    line, near, core = ctx // 4, (ctx // 2) % 2, ctx % 2

    def head_of(f, d):
        return f * RING + d

    def ctx_of(r, n, c):
        return r * 4 + n * 2 + c

    places = {
        "head_up": (head_of(far, (depth + 1) % RING), ctx),
        "head_down": (head_of(far, (depth + 3) % RING), ctx),
        "head_pair": (head_of(1 - far, depth), ctx),
        "ctx_up": (head, ctx_of((line + 1) % RING, near, core)),
        "ctx_down": (head, ctx_of((line + 3) % RING, near, core)),
        "ctx_pair": (head, ctx_of(line, 1 - near, core)),
        "sibling": (head, ctx_of(line, near, 1 - core)),
    }
    return places, (far, depth), (line, near, core)


class Gather:
    def __init__(self, source, block, half, pair, ring, sends, receives, up, down, across):
        other = 1 - pair
        before, after, opposite = (ring + 3) % RING, (ring + 1) % RING, (ring + 2) % RING
        self.copies = []
        own = block(pair, ring)
        plan = [
            (source(0), half(pair, ring, 0), half(pair, before, 0), up),
            (source(1), half(pair, ring, 1), half(pair, after, 1), down),
            (source(None), own, block(other, ring), across),
            (source(1), half(pair, ring, 1), half(pair, before, 1), up),
            (source(0), half(pair, ring, 0), half(pair, after, 0), down),
            (half(pair, before, 0), half(pair, before, 0), half(pair, opposite, 0), up),
            (half(pair, after, 1), half(pair, after, 1), half(pair, opposite, 1), down),
            (half(other, ring, 0), half(other, ring, 0), half(other, before, 0), up),
            (half(other, ring, 1), half(other, ring, 1), half(other, after, 1), down),
            (half(other, ring, 1), half(other, ring, 1), half(other, before, 1), up),
            (half(other, ring, 0), half(other, ring, 0), half(other, after, 0), down),
            (half(other, before, 0), half(other, before, 0), half(other, opposite, 0), up),
            (half(other, after, 1), half(other, after, 1), half(other, opposite, 1), down),
        ]
        for k, (src, dst, landed, place) in enumerate(plan):
            self.copies.append(
                (
                    remote(src, dst, sends.at[k], receives.at[k], place),
                    remote(landed, landed, sends.at[k], receives.at[k], place),
                )
            )

    def start(self, *which):
        for k in which:
            self.copies[k][0].start()

    def arrive(self, *which):
        for k in which:
            self.copies[k][1].wait_recv()

    def drain(self):
        for sent, landed in self.copies:
            sent.wait_send()


def front_kernel(
    x_hbm, og_hbm, wq_hbm, wk_hbm, wv_hbm, wo_hbm,
    q_hbm, g_hbm, kv_hbm,
    x, wq, wkv, wo, og, acc, q_ref, g_ref, kv_ref,
    loads, stores, head_send, head_receive, ctx_send, ctx_receive, sibling_send, sibling_receive,
):
    places, (far, depth), (line, near, core) = neighbours()
    me = far * RING + depth
    local = [
        pltpu.make_async_copy(x_hbm, x, loads.at[0]),
        pltpu.make_async_copy(wk_hbm, wkv.at[:, :CHANNEL_DIM], loads.at[1]),
        pltpu.make_async_copy(wv_hbm, wkv.at[:, CHANNEL_DIM:], loads.at[2]),
        pltpu.make_async_copy(wq_hbm, wq, loads.at[3]),
        pltpu.make_async_copy(og_hbm, og.at[me], loads.at[4]),
        pltpu.make_async_copy(wo_hbm, wo, loads.at[5]),
    ]
    for copy in local:
        copy.start()
    saved = [
        pltpu.make_async_copy(q_ref, q_hbm, stores.at[0]),
        pltpu.make_async_copy(kv_ref, kv_hbm, stores.at[1]),
        pltpu.make_async_copy(g_ref, g_hbm, stores.at[2]),
    ]
    greet(list(places.values()))

    heads = Gather(
        lambda k: og_hbm if k is None else og_hbm.at[pl.ds(k * HALF, HALF), :],
        lambda p, r: og.at[p * RING + r],
        lambda p, r, k: og.at[p * RING + r, pl.ds(k * HALF, HALF), :],
        far, depth, head_send, head_receive,
        places["head_up"], places["head_down"], places["head_pair"],
    )
    heads.start(0, 1, 2, 3, 4)

    def slot(p, r, c=core):
        return r * 4 + p * 2 + c

    spread = Gather(
        lambda k: kv_ref.at[slot(near, line)]
        if k is None
        else kv_ref.at[slot(near, line), pl.ds(k * HALF, HALF), :],
        lambda p, r: kv_ref.at[slot(p, r)],
        lambda p, r, k: kv_ref.at[slot(p, r), pl.ds(k * HALF, HALF), :],
        near, line, ctx_send, ctx_receive,
        places["ctx_up"], places["ctx_down"], places["ctx_pair"],
    )
    turns = [(p, (line + d) % RING) for p in (near, 1 - near) for d in (0, 3, 1, 2)]
    passed = [
        (
            remote(
                kv_ref.at[slot(p, r)], kv_ref.at[slot(p, r)],
                sibling_send.at[k], sibling_receive.at[k], places["sibling"],
            ),
            remote(
                kv_ref.at[slot(p, r, 1 - core)], kv_ref.at[slot(p, r, 1 - core)],
                sibling_send.at[k], sibling_receive.at[k], places["sibling"],
            ),
        )
        for k, (p, r) in enumerate(turns)
    ]

    def features(p, r):
        f = p * RING + r
        return lax.dot_general(
            og[f], wo[:, pl.ds(pl.multiple_of(f * FEATURES, FEATURES), FEATURES)],
            (((1,), (1,)), ((), ())), preferred_element_type=jnp.float32,
        )

    for k in (0, 1, 2):
        local[k].wait()
    kv_ref[slot(near, line)] = jnp.dot(
        x[...], wkv[...], preferred_element_type=jnp.float32
    ).astype(jnp.bfloat16)
    local[3].wait()
    q_ref[...] = jnp.dot(x[...], wq[...], preferred_element_type=jnp.float32).astype(jnp.bfloat16)
    spread.start(0, 1, 2, 3, 4)
    passed[0][0].start()
    saved[0].start()
    heads.arrive(0)
    heads.start(5)
    heads.arrive(1)
    heads.start(6)
    local[4].wait()
    local[5].wait()
    acc[...] = features(far, depth)

    before, after, opposite = (depth + 3) % RING, (depth + 1) % RING, (depth + 2) % RING
    spread.arrive(2)
    spread.start(7, 8, 9, 10)
    passed[4][0].start()
    spread.arrive(0)
    spread.start(5)
    spread.arrive(1)
    spread.start(6)
    heads.arrive(2)
    heads.start(7, 8, 9, 10)
    heads.arrive(3)
    acc[...] += features(far, before)
    heads.arrive(4)
    acc[...] += features(far, after)
    spread.arrive(3)
    passed[1][0].start()
    spread.arrive(4)
    passed[2][0].start()
    spread.arrive(7)
    spread.start(11)
    spread.arrive(8)
    spread.start(12)
    acc[...] += features(1 - far, depth)
    heads.arrive(5, 6)
    acc[...] += features(far, opposite)
    spread.arrive(5, 6)
    passed[3][0].start()
    spread.arrive(9)
    passed[5][0].start()
    spread.arrive(10)
    passed[6][0].start()
    heads.arrive(7)
    heads.start(11)
    heads.arrive(8)
    heads.start(12)
    spread.arrive(11, 12)
    passed[7][0].start()
    heads.arrive(9)
    acc[...] += features(1 - far, before)
    heads.arrive(10)
    acc[...] += features(1 - far, after)
    for sent, landed in passed:
        landed.wait_recv()
    saved[1].start()
    heads.arrive(11, 12)
    g_ref[...] = (acc[...] + features(1 - far, opposite)).astype(jnp.bfloat16)
    saved[2].start()
    heads.drain()
    spread.drain()
    for sent, landed in passed:
        sent.wait_send()
    for copy in saved:
        copy.wait()


def front(inputs, out_grad, w_query, w_key, value_projection, w_out, peers):
    tokens, width = inputs.shape
    lanes = w_query.shape[1]
    hbm = pl.BlockSpec(memory_space=pl.ANY)
    return pl.pallas_call(
        front_kernel,
        out_shape=(
            jax.ShapeDtypeStruct((tokens, lanes), jnp.bfloat16),
            jax.ShapeDtypeStruct((tokens, lanes), jnp.bfloat16),
            jax.ShapeDtypeStruct((peers, tokens, 2 * CHANNEL_DIM), jnp.bfloat16),
        ),
        in_specs=[hbm] * 6,
        out_specs=(hbm, hbm, hbm),
        scratch_shapes=[
            pltpu.VMEM((tokens, width), jnp.bfloat16),
            pltpu.VMEM((width, lanes), jnp.bfloat16),
            pltpu.VMEM((width, 2 * CHANNEL_DIM), jnp.bfloat16),
            pltpu.VMEM((lanes, width), jnp.bfloat16),
            pltpu.VMEM((2 * RING, tokens, FEATURES), jnp.bfloat16),
            pltpu.VMEM((tokens, lanes), jnp.float32),
            pltpu.VMEM((tokens, lanes), jnp.bfloat16),
            pltpu.VMEM((tokens, lanes), jnp.bfloat16),
            pltpu.VMEM((peers, tokens, 2 * CHANNEL_DIM), jnp.bfloat16),
            pltpu.SemaphoreType.DMA((6,)),
            pltpu.SemaphoreType.DMA((3,)),
            pltpu.SemaphoreType.DMA((13,)),
            pltpu.SemaphoreType.DMA((13,)),
            pltpu.SemaphoreType.DMA((13,)),
            pltpu.SemaphoreType.DMA((13,)),
            pltpu.SemaphoreType.DMA((8,)),
            pltpu.SemaphoreType.DMA((8,)),
        ],
        compiler_params=pltpu.CompilerParams(
            collective_id=0, has_side_effects=True, vmem_limit_bytes=GRANT
        ),
        name="front",
    )(inputs, out_grad, w_query, w_key, value_projection, w_out)


class Reduce:
    def __init__(self, held, gone, sums, ring, sends, receives, up, down):
        self.held, self.gone, self.sums = held, gone, sums
        self.before, self.after = (ring + 3) % RING, (ring + 1) % RING
        opposite = (ring + 2) % RING
        self.cut = held.shape[2] // 2
        low, high = pl.ds(0, self.cut), pl.ds(self.cut, self.cut)
        plan = [
            (held.at[opposite, :, low], gone.at[0], up),
            (held.at[opposite, :, high], gone.at[1], down),
            (held.at[self.after, :, high], sums.at[0, :, high], up),
            (held.at[self.before, :, low], sums.at[1, :, low], down),
            (held.at[self.after, :, low], sums.at[0, :, low], up),
            (held.at[self.before, :, high], sums.at[1, :, high], down),
        ]
        self.copies = [
            remote(src, dst, sends.at[k], receives.at[k], place)
            for k, (src, dst, place) in enumerate(plan)
        ]

    def start(self, *which):
        for k in which:
            self.copies[k].start()

    def relay(self):
        low, high = slice(0, self.cut), slice(self.cut, 2 * self.cut)
        for k, r, rows in ((0, self.after, low), (1, self.before, high)):
            self.copies[k].wait_recv()
            for p in range(2):
                self.held[r, p, rows] = (
                    self.held[r, p, rows].astype(jnp.float32)
                    + self.gone[k, p].astype(jnp.float32)
                ).astype(jnp.bfloat16)
            self.start(4 + k)

    def arrive(self):
        for k in (2, 3, 4, 5):
            self.copies[k].wait_recv()

    def total(self, p):
        return self.sums[0, p].astype(jnp.float32) + self.sums[1, p].astype(jnp.float32)

    def drain(self):
        for copy in self.copies:
            copy.wait_send()


def back_kernel(
    p_hbm, wq_hbm, wk_hbm, wv_hbm,
    out_ref,
    dq, mine, wq, wkv, side, held, inbox, dkv, parts, leaving, left, gone, sums, crossing, crossed,
    loads, side_send, side_receive, ctx_send, ctx_receive, head_send, head_receive,
    pair_send, pair_receive,
):
    places, (far, depth), (line, near, core) = neighbours()
    head, ctx = lax.axis_index("head"), lax.axis_index("ctx")
    others = [
        ((line + d) % RING, (near + n) % 2) for d, n in OFFSETS
    ]
    around = [(head, r * 4 + p * 2 + core) for r, p in others]
    local = [
        pltpu.make_async_copy(p_hbm.at[pl.ds(1, 2 * RING), core], mine, loads.at[0]),
        pltpu.make_async_copy(p_hbm.at[0], dq, loads.at[1]),
        pltpu.make_async_copy(wq_hbm, wq, loads.at[2]),
        pltpu.make_async_copy(wk_hbm, wkv.at[:, :CHANNEL_DIM], loads.at[3]),
        pltpu.make_async_copy(wv_hbm, wkv.at[:, CHANNEL_DIM:], loads.at[4]),
    ]
    for copy in local:
        copy.start()
    greet([places["sibling"], places["head_up"], places["head_down"], places["head_pair"], *around])

    rows = mine.shape[2]
    swaps = [
        remote(
            p_hbm.at[pl.ds(1, 2 * RING), 1 - core, c], side.at[c],
            side_send.at[c], side_receive.at[c], places["sibling"],
        )
        for c in range(CHUNKS)
    ]
    for copy in swaps:
        copy.start()
    sends = [
        [
            remote(
                held.at[c, r, p], inbox.at[c, k],
                ctx_send.at[c, k], ctx_receive.at[c, k], around[k],
            )
            for k, (r, p) in enumerate(others)
        ]
        for c in range(CHUNKS)
    ]
    rounds = [
        Reduce(
            leaving.at[c], gone.at[c], sums.at[c], depth,
            head_send.at[c], head_receive.at[c], places["head_up"], places["head_down"],
        )
        for c in range(CHUNKS)
    ]
    across = [
        remote(
            crossing.at[c], crossed.at[c],
            pair_send.at[c], pair_receive.at[c], places["head_pair"],
        )
        for c in range(CHUNKS)
    ]

    def join(c, r, p):
        return mine[2 * r + p, c].astype(jnp.float32) + side[c, 2 * r + p].astype(jnp.float32)

    local[0].wait()
    for c in range(CHUNKS):
        swaps[c].wait_recv()
        for k, (r, p) in enumerate(others):
            held[c, r, p] = join(c, r, p).astype(jnp.bfloat16)
        for copy in sends[c]:
            copy.start()

    local[1].wait()
    local[2].wait()

    @pl.loop(0, 2 * RING)
    def _(f):
        at = pl.ds(pl.multiple_of(f * FEATURES, FEATURES), FEATURES)
        query_grad = jnp.concatenate(
            [dq[k].reshape(dq.shape[1] * dq.shape[2], dq.shape[3]) for k in range(2)], axis=1
        )
        parts[f] = lax.dot_general(
            query_grad, wq[at, :], (((1,), (1,)), ((), ())), preferred_element_type=jnp.float32
        )

    local[3].wait()
    local[4].wait()

    def term(c, f):
        return parts[f, c * rows : (c + 1) * rows, :] + lax.dot_general(
            dkv[c], wkv[pl.ds(pl.multiple_of(f * FEATURES, FEATURES), FEATURES), :],
            (((1,), (1,)), ((), ())), preferred_element_type=jnp.float32,
        )

    def issue(c):
        total = join(c, line, near)
        for k in range(len(sends[c])):
            sends[c][k].wait_recv()
            total = total + inbox[c, k].astype(jnp.float32)
        dkv[c] = total.astype(jnp.bfloat16)
        for d, ready in ((2, (0, 1)), (1, (2,)), (3, (3,))):
            r = (depth + d) % RING
            for p in range(2):
                leaving[c, r, p] = term(c, p * RING + r).astype(jnp.bfloat16)
            rounds[c].start(*ready)
        for p in range(2):
            left[c, p] = term(c, p * RING + depth)

    def cross(c):
        rounds[c].arrive()
        crossing[c] = (left[c, 1 - far] + rounds[c].total(1 - far)).astype(jnp.bfloat16)
        across[c].start()
        left[c, far] = left[c, far] + rounds[c].total(far)

    issue(0)
    for c in range(1, CHUNKS):
        issue(c)
        rounds[c - 1].relay()
        if c > 1:
            cross(c - 2)
    rounds[CHUNKS - 1].relay()
    cross(CHUNKS - 2)
    cross(CHUNKS - 1)
    for c in range(CHUNKS):
        across[c].wait_recv()
        out_ref[c * rows : (c + 1) * rows, :] = (
            left[c, far] + crossed[c].astype(jnp.float32)
        ).astype(jnp.bfloat16)
    for c in range(CHUNKS):
        swaps[c].wait_send()
        across[c].wait_send()
        rounds[c].drain()
        for copy in sends[c]:
            copy.wait_send()


def back(pieces, w_query, w_key, value_projection):
    rows = pieces.shape[3]
    tokens = rows * CHUNKS
    width, lanes = w_query.shape
    vmem = pl.BlockSpec(memory_space=pltpu.VMEM)
    hbm = pl.BlockSpec(memory_space=pl.ANY)
    wide = 2 * CHANNEL_DIM
    bf16, f32 = jnp.bfloat16, jnp.float32
    dma = pltpu.SemaphoreType.DMA
    return pl.pallas_call(
        back_kernel,
        out_shape=jax.ShapeDtypeStruct((tokens, FEATURES), bf16),
        in_specs=[hbm] * 4,
        out_specs=vmem,
        scratch_shapes=[
            pltpu.VMEM((2, CHUNKS, rows, wide), bf16),
            pltpu.VMEM((2 * RING, CHUNKS, rows, wide), bf16),
            pltpu.VMEM((width, lanes), bf16),
            pltpu.VMEM((width, wide), bf16),
            pltpu.VMEM((CHUNKS, 2 * RING, rows, wide), bf16),
            pltpu.VMEM((CHUNKS, RING, 2, rows, wide), bf16),
            pltpu.VMEM((CHUNKS, len(OFFSETS), rows, wide), bf16),
            pltpu.VMEM((CHUNKS, rows, wide), bf16),
            pltpu.VMEM((2 * RING, tokens, FEATURES), f32),
            pltpu.VMEM((CHUNKS, RING, 2, rows, FEATURES), bf16),
            pltpu.VMEM((CHUNKS, 2, rows, FEATURES), f32),
            pltpu.VMEM((CHUNKS, 2, 2, rows // 2, FEATURES), bf16),
            pltpu.VMEM((CHUNKS, 2, 2, rows, FEATURES), bf16),
            pltpu.VMEM((CHUNKS, rows, FEATURES), bf16),
            pltpu.VMEM((CHUNKS, rows, FEATURES), bf16),
            dma((5,)),
            dma((CHUNKS,)),
            dma((CHUNKS,)),
            dma((CHUNKS, len(OFFSETS))),
            dma((CHUNKS, len(OFFSETS))),
            dma((CHUNKS, 6)),
            dma((CHUNKS, 6)),
            dma((CHUNKS,)),
            dma((CHUNKS,)),
        ],
        compiler_params=pltpu.CompilerParams(
            collective_id=1, has_side_effects=True, vmem_limit_bytes=54000 * 1024
        ),
        name="back",
    )(pieces, w_query, w_key, value_projection)


def attention_kernel(
    span_ref, length_ref, q_hbm, g_hbm, kv_hbm,
    out_hbm,
    kvs, qs, gs, s_buf, d_buf, acc, dqt, q_ref, g_ref, dq_ref, dkv_ref, blank, row_of,
    loads, stores,
):
    exponent = LOG2E / math.sqrt(CHANNEL_DIM)
    scale = 1.0 / math.sqrt(CHANNEL_DIM)
    spans = span_ref.shape[0]
    tokens, wide = q_ref.shape[0], 2 * CHANNEL_DIM
    local = [
        pltpu.make_async_copy(q_hbm, q_ref, loads.at[0]),
        pltpu.make_async_copy(g_hbm, g_ref, loads.at[1]),
    ]
    for copy in local:
        copy.start()
    blank[...] = jnp.zeros_like(blank)

    places = []
    for b in range(2):
        c = span_ref[2 * lax.axis_index("ctx") + b]
        first = 0
        end = 0
        for k in range(length_ref.shape[0]):
            end = end + length_ref[k]
            first = jnp.where(c * HALF >= end, end, first)
        places.append((c, first // TILE, c // (TILE // HALF) + 1))

    def reached(p):
        t = p // (TILE // HALF)
        return jnp.logical_or(
            *[jnp.logical_and(t >= low, t < high) for c, low, high in places]
        )

    def rows_at(n):
        return pl.ds(pl.multiple_of(n * HALF, HALF), HALF)

    def block_in(r, p):
        return pltpu.make_async_copy(
            kv_hbm.at[rows_at(r), :], kvs.at[rows_at(p), :], loads.at[2]
        )

    def block_out(block, r):
        return pltpu.make_async_copy(
            block, out_hbm.at[rows_at(r + 2 * tokens // HALF), :], stores.at[1]
        )

    @pl.loop(0, spans)
    def _(r):
        p = span_ref[r]
        row_of[p] = r

        @pl.when(reached(p))
        def _():
            block_in(r, p).start()

        @pl.when(jnp.logical_not(reached(p)))
        def _():
            block_out(blank, r).start()

    for c, low, high in places:

        @pl.loop(low, high)
        def _(t):
            acc[pl.ds(pl.multiple_of(t * TILE, TILE), TILE), :] = jnp.zeros((TILE, wide), jnp.float32)

    for copy in local:
        copy.wait()

    @pl.loop(0, spans)
    def _(r):
        p = span_ref[r]

        @pl.when(reached(p))
        def _():
            block_in(r, p).wait()

    lanes = BUNDLE * HALF
    for b in range(2):
        rows = slice(b * HALF, (b + 1) * HALF)
        for h in range(BUNDLE):
            cols = slice(h * CHANNEL_DIM, (h + 1) * CHANNEL_DIM)
            qs[h * HALF : (h + 1) * HALF, :] = q_ref[rows, cols]
            gs[h * HALF : (h + 1) * HALF, :] = g_ref[rows, cols]
        c, low, high = places[b]
        position = c * HALF + lax.broadcasted_iota(jnp.int32, (1, HALF), 1)
        start = jnp.zeros((1, HALF), jnp.int32)
        end = 0
        for k in range(length_ref.shape[0]):
            end = end + length_ref[k]
            start = jnp.where(position >= end, end, start)

        def gather_stats(t, carry):
            top, total, inner = carry
            at = pl.ds(pl.multiple_of(t * TILE, TILE), TILE)
            keys = kvs[at, :CHANNEL_DIM]
            values = kvs[at, CHANNEL_DIM:]
            key_position = t * TILE + lax.broadcasted_iota(jnp.int32, (TILE, HALF), 0)
            bias = jnp.where(
                (key_position <= position) & (key_position >= start), 0.0, MASKED
            )
            bias = jnp.concatenate([bias] * BUNDLE, axis=1)
            s = lax.dot_general(
                keys, qs[...], (((1,), (1,)), ((), ())), preferred_element_type=jnp.float32
            )
            s = s * exponent + bias
            s_buf[at, :] = s
            fresh = jnp.maximum(top, jnp.max(s, axis=0, keepdims=True))
            factor = jnp.exp2(top - fresh)
            e = jnp.exp2(s - fresh)
            slopes = lax.dot_general(
                values, gs[...], (((1,), (1,)), ((), ())), preferred_element_type=jnp.float32
            )
            d_buf[at, :] = slopes
            total = total * factor + jnp.sum(e, axis=0, keepdims=True)
            inner = inner * factor + jnp.sum(e * slopes, axis=0, keepdims=True)
            return fresh, total, inner

        zero = jnp.zeros((1, lanes), jnp.float32)
        top, total, inner = lax.fori_loop(
            low, high, gather_stats, (jnp.full((1, lanes), MASKED, jnp.float32), zero, zero)
        )
        delta = inner / total
        level = top + jnp.log2(total)
        dqt[...] = jnp.zeros_like(dqt)

        @pl.loop(low, high)
        def _(t):
            at = pl.ds(pl.multiple_of(t * TILE, TILE), TILE)
            probability = jnp.exp2(s_buf[at, :] - level)
            score_grad = (probability * (d_buf[at, :] - delta)).astype(jnp.bfloat16)
            rounded = probability.astype(jnp.bfloat16)
            acc[at, CHANNEL_DIM:] += jnp.dot(rounded, gs[...], preferred_element_type=jnp.float32)
            acc[at, :CHANNEL_DIM] += jnp.dot(score_grad, qs[...], preferred_element_type=jnp.float32)
            dqt[...] += lax.dot_general(
                kvs[at, :CHANNEL_DIM], score_grad, (((0,), (0,)), ((), ())),
                preferred_element_type=jnp.float32,
            )

        for h in range(BUNDLE):
            to = slice(h // 2 * tokens + b * HALF, h // 2 * tokens + (b + 1) * HALF)
            dq_ref[to, h % 2 * CHANNEL_DIM : (h % 2 + 1) * CHANNEL_DIM] = (
                (dqt[:, h * HALF : (h + 1) * HALF] * scale).T.astype(jnp.bfloat16)
            )

    grads = pltpu.make_async_copy(dq_ref, out_hbm.at[pl.ds(0, 2 * tokens), :], stores.at[0])
    grads.start()

    def finish(p):
        r = row_of[p]
        at, to = rows_at(p), rows_at(r)
        dkv_ref[to, :CHANNEL_DIM] = (acc[at, :CHANNEL_DIM] * scale).astype(jnp.bfloat16)
        dkv_ref[to, CHANNEL_DIM:] = acc[at, CHANNEL_DIM:].astype(jnp.bfloat16)
        block_out(dkv_ref.at[to, :], r).start()

    for b, (c, low, high) in enumerate(places):

        @pl.loop(low, high)
        def _(t):
            fresh = True
            if b:
                fresh = jnp.logical_or(t < places[0][1], t >= places[0][2])

            @pl.when(fresh)
            def _():
                for k in range(TILE // HALF):
                    finish(t * (TILE // HALF) + k)

    grads.wait()
    pltpu.make_async_copy(
        dkv_ref, out_hbm.at[pl.ds(2 * tokens, dkv_ref.shape[0]), :], stores.at[1]
    ).wait()


def attention(q, g, kv, span_order, doc_lengths):
    tokens = q.shape[0]
    length = kv.shape[0]
    smem = pl.BlockSpec(memory_space=pltpu.SMEM)
    hbm = pl.BlockSpec(memory_space=pl.ANY)
    lanes = BUNDLE * HALF
    return pl.pallas_call(
        attention_kernel,
        out_shape=jax.ShapeDtypeStruct((2 * tokens + length, 2 * CHANNEL_DIM), jnp.bfloat16),
        in_specs=[smem, smem, hbm, hbm, hbm],
        out_specs=hbm,
        scratch_shapes=[
            pltpu.VMEM((length, 2 * CHANNEL_DIM), jnp.bfloat16),
            pltpu.VMEM((lanes, CHANNEL_DIM), jnp.bfloat16),
            pltpu.VMEM((lanes, CHANNEL_DIM), jnp.bfloat16),
            pltpu.VMEM((length, lanes), jnp.float32),
            pltpu.VMEM((length, lanes), jnp.float32),
            pltpu.VMEM((length, 2 * CHANNEL_DIM), jnp.float32),
            pltpu.VMEM((CHANNEL_DIM, lanes), jnp.float32),
            pltpu.VMEM((tokens, lanes), jnp.bfloat16),
            pltpu.VMEM((tokens, lanes), jnp.bfloat16),
            pltpu.VMEM((2 * tokens, 2 * CHANNEL_DIM), jnp.bfloat16),
            pltpu.VMEM((length, 2 * CHANNEL_DIM), jnp.bfloat16),
            pltpu.VMEM((HALF, 2 * CHANNEL_DIM), jnp.bfloat16),
            pltpu.SMEM((length // HALF,), jnp.int32),
            pltpu.SemaphoreType.DMA((3,)),
            pltpu.SemaphoreType.DMA((2,)),
        ],
        compiler_params=pltpu.CompilerParams(vmem_limit_bytes=GRANT),
        name="attention",
    )(span_order, doc_lengths, q, g, kv)


def shards(inputs, out_grad, w_query, w_key, value_projection, w_out, doc_lengths, span_order):
    tokens = inputs.shape[0]
    peers = lax.axis_size("ctx")
    query, context_grad, gathered = front(
        inputs, out_grad, w_query, w_key, value_projection, w_out, peers
    )
    pieces = attention(
        query, context_grad, gathered.reshape(peers * tokens, -1), span_order, doc_lengths
    )
    pieces = pieces.reshape(1 + 2 * RING, 2, CHUNKS, tokens // CHUNKS, -1)
    return back(pieces, w_query, w_key, value_projection)


def solution(mesh):
    in_specs = (
        P("ctx", None),
        P("ctx", "head"),
        P(None, "head"),
        P(None, "head"),
        P(None, "head"),
        P("head", None),
        P(),
        P(),
    )
    return jax.shard_map(
        shards, mesh=mesh, in_specs=in_specs, out_specs=P("ctx", "head"), check_vma=False
    )
```

```python
import math

import jax
import jax.numpy as jnp
from jax import lax
from jax.experimental import pallas as pl
from jax.experimental.pallas import tpu as pltpu
from jax.sharding import PartitionSpec as P

ASKER_NUM = 32
SHARED_KV_NUM = 8
CHANNEL_DIM = 128
BUNDLE = ASKER_NUM // SHARED_KV_NUM
HALF = 128
TILE = 256
RING = 4
FEATURES = 512
PARTS = tuple(pl.ds(*cut) for cut in ((0, 64), (64, 64), (128, 64), (192, 64)))
OFFSETS = ((2, 1), (2, 0), (1, 1), (3, 1), (1, 0), (3, 0), (0, 1))
LOG2E = 1.4426950408889634
MASKED = -1e30
GRANT = 60 * 1024 * 1024
MESH = pl.DeviceIdType.MESH


def remote(src, dst, send, receive, place):
    return pltpu.make_async_remote_copy(
        src_ref=src, dst_ref=dst, send_sem=send, recv_sem=receive,
        device_id=place, device_id_type=MESH,
    )


def greet(places):
    barrier = pltpu.get_barrier_semaphore()
    for place in places:
        pl.semaphore_signal(barrier, inc=1, device_id=place, device_id_type=MESH)
    pl.semaphore_wait(barrier, len(places))


def neighbours():
    head = lax.axis_index("head")
    ctx = lax.axis_index("ctx")
    far, depth = head // RING, head % RING
    line, near, core = ctx // 4, (ctx // 2) % 2, ctx % 2

    def head_of(f, d):
        return f * RING + d

    def ctx_of(r, n, c):
        return r * 4 + n * 2 + c

    places = {
        "head_up": (head_of(far, (depth + 1) % RING), ctx),
        "head_down": (head_of(far, (depth + 3) % RING), ctx),
        "head_pair": (head_of(1 - far, depth), ctx),
        "ctx_up": (head, ctx_of((line + 1) % RING, near, core)),
        "ctx_down": (head, ctx_of((line + 3) % RING, near, core)),
        "ctx_pair": (head, ctx_of(line, 1 - near, core)),
        "sibling": (head, ctx_of(line, near, 1 - core)),
    }
    return places, (far, depth), (line, near, core)


class Gather:
    def __init__(self, source, block, pair, ring, sends, receives, up, down, across):
        other = 1 - pair
        before, after, opposite = (ring + 3) % RING, (ring + 1) % RING, (ring + 2) % RING
        self.copies = []
        own = block(pair, ring)

        def half(p, r, k, start=0, size=HALF):
            return block(p, r).at[pl.ds(k * HALF + start, size), :]

        def quarter(p, r, k, q):
            return half(p, r, k, q * HALF // 2, HALF // 2)

        plan = [
            (source(0), half(pair, ring, 0), half(pair, before, 0), up),
            (source(1), half(pair, ring, 1), half(pair, after, 1), down),
            (source(None), own, block(other, ring), across),
            (source(1), half(pair, ring, 1), half(pair, before, 1), up),
            (source(0), half(pair, ring, 0), half(pair, after, 0), down),
            (half(pair, before, 0), half(pair, before, 0), half(pair, opposite, 0), up),
            (half(pair, after, 1), half(pair, after, 1), half(pair, opposite, 1), down),
            (half(other, ring, 0), half(other, ring, 0), half(other, before, 0), up),
            (half(other, ring, 1), half(other, ring, 1), half(other, after, 1), down),
            (half(other, ring, 1), half(other, ring, 1), half(other, before, 1), up),
            (half(other, ring, 0), half(other, ring, 0), half(other, after, 0), down),
            (
                quarter(other, before, 0, 0), quarter(other, before, 0, 0),
                quarter(other, opposite, 0, 0), up,
            ),
            (
                quarter(other, after, 1, 0), quarter(other, after, 1, 0),
                quarter(other, opposite, 1, 0), down,
            ),
            (
                quarter(pair, opposite, 0, 1), quarter(pair, opposite, 0, 1),
                quarter(other, opposite, 0, 1), across,
            ),
            (
                quarter(pair, opposite, 1, 1), quarter(pair, opposite, 1, 1),
                quarter(other, opposite, 1, 1), across,
            ),
        ]
        for k, (src, dst, landed, place) in enumerate(plan):
            self.copies.append(
                (
                    remote(src, dst, sends.at[k], receives.at[k], place),
                    remote(landed, landed, sends.at[k], receives.at[k], place),
                )
            )

    def start(self, *which):
        for k in which:
            self.copies[k][0].start()

    def arrive(self, *which):
        for k in which:
            self.copies[k][1].wait_recv()

    def drain(self):
        for sent, landed in self.copies:
            sent.wait_send()


def front_kernel(
    x_hbm, og_hbm, wq_hbm, wk_hbm, wv_hbm, wo_hbm,
    q_hbm, g_hbm, kv_hbm,
    x, wq, wkv, wo, og, acc, q_ref, g_ref, kv_ref,
    loads, stores, head_send, head_receive, ctx_send, ctx_receive, sibling_send, sibling_receive,
):
    places, (far, depth), (line, near, core) = neighbours()
    me = far * RING + depth
    local = [
        pltpu.make_async_copy(x_hbm, x, loads.at[0]),
        pltpu.make_async_copy(wk_hbm, wkv.at[:, :CHANNEL_DIM], loads.at[1]),
        pltpu.make_async_copy(wv_hbm, wkv.at[:, CHANNEL_DIM:], loads.at[2]),
        pltpu.make_async_copy(wq_hbm, wq, loads.at[3]),
        pltpu.make_async_copy(og_hbm, og.at[me], loads.at[4]),
        pltpu.make_async_copy(wo_hbm, wo, loads.at[5]),
    ]
    for copy in local[:3]:
        copy.start()
    saved = [
        pltpu.make_async_copy(q_ref, q_hbm, stores.at[0]),
        pltpu.make_async_copy(kv_ref, kv_hbm, stores.at[1]),
        pltpu.make_async_copy(g_ref, g_hbm, stores.at[2]),
    ]
    greet(list(places.values()))

    heads = Gather(
        lambda k: og_hbm if k is None else og_hbm.at[pl.ds(k * HALF, HALF), :],
        lambda p, r: og.at[p * RING + r],
        far, depth, head_send, head_receive,
        places["head_up"], places["head_down"], places["head_pair"],
    )
    heads.start(0, 1, 2, 3, 4)
    for copy in local[3:]:
        copy.start()

    def slot(p, r, c=core):
        return r * 4 + p * 2 + c

    spread = Gather(
        lambda k: kv_ref.at[slot(near, line)]
        if k is None
        else kv_ref.at[slot(near, line), pl.ds(k * HALF, HALF), :],
        lambda p, r: kv_ref.at[slot(p, r)],
        near, line, ctx_send, ctx_receive,
        places["ctx_up"], places["ctx_down"], places["ctx_pair"],
    )
    turns = [(p, (line + d) % RING) for p in (near, 1 - near) for d in (0, 3, 1, 2)]
    passed = [
        (
            remote(
                kv_ref.at[slot(p, r)], kv_ref.at[slot(p, r)],
                sibling_send.at[k], sibling_receive.at[k], places["sibling"],
            ),
            remote(
                kv_ref.at[slot(p, r, 1 - core)], kv_ref.at[slot(p, r, 1 - core)],
                sibling_send.at[k], sibling_receive.at[k], places["sibling"],
            ),
        )
        for k, (p, r) in enumerate(turns)
    ]

    def features(p, r):
        f = p * RING + r
        return lax.dot_general(
            og[f], wo[:, pl.ds(pl.multiple_of(f * FEATURES, FEATURES), FEATURES)],
            (((1,), (1,)), ((), ())), preferred_element_type=jnp.float32,
        )

    for k in (0, 1, 2):
        local[k].wait()
    kv_ref[slot(near, line)] = jnp.dot(
        x[...], wkv[...], preferred_element_type=jnp.float32
    ).astype(jnp.bfloat16)
    def query(k):
        columns = slice(k * wq.shape[1] // 2, (k + 1) * wq.shape[1] // 2)
        q_ref[:, columns] = jnp.dot(
            x[...], wq[:, columns], preferred_element_type=jnp.float32
        ).astype(jnp.bfloat16)

    def keep(at):
        pltpu.make_async_copy(kv_ref.at[at], kv_hbm.at[at], stores.at[1]).start()

    def share(k):
        passed[k][0].start()
        keep(slot(*turns[k]))

    local[3].wait()
    query(0)
    spread.start(0, 1, 2, 3, 4)
    share(0)
    query(1)
    saved[0].start()
    before, after, opposite = (depth + 3) % RING, (depth + 1) % RING, (depth + 2) % RING
    heads.arrive(0)
    heads.start(5)
    heads.arrive(1)
    heads.start(6)
    local[4].wait()
    local[5].wait()
    acc[...] = features(far, depth)
    spread.arrive(0)
    spread.start(5)
    spread.arrive(1)
    spread.start(6)
    heads.arrive(3)
    acc[...] += features(far, before)
    spread.arrive(2)
    spread.start(7, 8, 9, 10)
    share(4)
    heads.arrive(4)
    acc[...] += features(far, after)
    spread.arrive(3)
    share(1)
    spread.arrive(4)
    share(2)
    heads.arrive(2)
    heads.start(7, 8, 9, 10)
    acc[...] += features(1 - far, depth)
    spread.arrive(5)
    spread.start(13)
    spread.arrive(6)
    spread.start(14)
    share(3)
    heads.arrive(5)
    heads.start(13)
    heads.arrive(6)
    heads.start(14)
    acc[...] += features(far, opposite)
    spread.arrive(7)
    spread.start(11)
    spread.arrive(8)
    spread.start(12)
    spread.arrive(9)
    share(5)
    spread.arrive(10)
    share(6)
    heads.arrive(7)
    heads.start(11)
    heads.arrive(8)
    heads.start(12)
    spread.arrive(11, 12, 13, 14)
    share(7)
    heads.arrive(9)
    acc[...] += features(1 - far, before)
    heads.arrive(10)
    acc[...] += features(1 - far, after)
    for k, (sent, landed) in enumerate(passed):
        landed.wait_recv()
        keep(slot(*turns[k], 1 - core))
    heads.arrive(11, 12, 13, 14)
    g_ref[...] = (acc[...] + features(1 - far, opposite)).astype(jnp.bfloat16)
    saved[2].start()
    heads.drain()
    spread.drain()
    for sent, landed in passed:
        sent.wait_send()
    for copy in saved:
        copy.wait()


def front(inputs, out_grad, w_query, w_key, value_projection, w_out, peers):
    tokens, width = inputs.shape
    lanes = w_query.shape[1]
    hbm = pl.BlockSpec(memory_space=pl.ANY)
    return pl.pallas_call(
        front_kernel,
        out_shape=(
            jax.ShapeDtypeStruct((tokens, lanes), jnp.bfloat16),
            jax.ShapeDtypeStruct((tokens, lanes), jnp.bfloat16),
            jax.ShapeDtypeStruct((peers, tokens, 2 * CHANNEL_DIM), jnp.bfloat16),
        ),
        in_specs=[hbm] * 6,
        out_specs=(hbm, hbm, hbm),
        scratch_shapes=[
            pltpu.VMEM((tokens, width), jnp.bfloat16),
            pltpu.VMEM((width, lanes), jnp.bfloat16),
            pltpu.VMEM((width, 2 * CHANNEL_DIM), jnp.bfloat16),
            pltpu.VMEM((lanes, width), jnp.bfloat16),
            pltpu.VMEM((2 * RING, tokens, FEATURES), jnp.bfloat16),
            pltpu.VMEM((tokens, lanes), jnp.float32),
            pltpu.VMEM((tokens, lanes), jnp.bfloat16),
            pltpu.VMEM((tokens, lanes), jnp.bfloat16),
            pltpu.VMEM((peers, tokens, 2 * CHANNEL_DIM), jnp.bfloat16),
            pltpu.SemaphoreType.DMA((6,)),
            pltpu.SemaphoreType.DMA((3,)),
            pltpu.SemaphoreType.DMA((15,)),
            pltpu.SemaphoreType.DMA((15,)),
            pltpu.SemaphoreType.DMA((15,)),
            pltpu.SemaphoreType.DMA((15,)),
            pltpu.SemaphoreType.DMA((8,)),
            pltpu.SemaphoreType.DMA((8,)),
        ],
        compiler_params=pltpu.CompilerParams(
            collective_id=0, has_side_effects=True, vmem_limit_bytes=GRANT
        ),
        name="front",
    )(inputs, out_grad, w_query, w_key, value_projection, w_out)


class Reduce:
    def __init__(self, held, gone, sums, ring, sends, receives, up, down):
        self.held, self.gone, self.sums = held, gone, sums
        self.before, self.after = (ring + 3) % RING, (ring + 1) % RING
        opposite = (ring + 2) % RING
        self.cut = held.shape[2] // 2
        low, high = pl.ds(0, self.cut), pl.ds(self.cut, self.cut)
        plan = [
            (held.at[opposite, :, low], gone.at[0], up),
            (held.at[opposite, :, high], gone.at[1], down),
            (held.at[self.after, :, high], sums.at[0, :, high], up),
            (held.at[self.before, :, low], sums.at[1, :, low], down),
            (held.at[self.after, :, low], sums.at[0, :, low], up),
            (held.at[self.before, :, high], sums.at[1, :, high], down),
        ]
        self.copies = [
            remote(src, dst, sends.at[k], receives.at[k], place)
            for k, (src, dst, place) in enumerate(plan)
        ]

    def start(self, *which):
        for k in which:
            self.copies[k].start()

    def relay(self):
        low, high = slice(0, self.cut), slice(self.cut, 2 * self.cut)
        for k, r, rows in ((0, self.after, low), (1, self.before, high)):
            self.copies[k].wait_recv()
            for p in range(2):
                self.held[r, p, rows] = (
                    self.held[r, p, rows].astype(jnp.float32)
                    + self.gone[k, p].astype(jnp.float32)
                ).astype(jnp.bfloat16)
            self.start(4 + k)

    def arrive(self):
        for k in (2, 3, 4, 5):
            self.copies[k].wait_recv()

    def total(self, p):
        return self.sums[0, p].astype(jnp.float32) + self.sums[1, p].astype(jnp.float32)

    def drain(self):
        for copy in self.copies:
            copy.wait_send()


def back_kernel(
    p_hbm, wq_hbm, wk_hbm, wv_hbm,
    out_ref,
    dq, mine, wq, wkv, side, held, inbox, dkv, parts, leaving, left, gone, sums, crossing, crossed,
    loads, side_send, side_receive, ctx_send, ctx_receive, head_send, head_receive,
    pair_send, pair_receive,
):
    places, (far, depth), (line, near, core) = neighbours()
    head, ctx = lax.axis_index("head"), lax.axis_index("ctx")
    others = [
        ((line + d) % RING, (near + n) % 2) for d, n in OFFSETS
    ]
    around = [(head, r * 4 + p * 2 + core) for r, p in others]
    local = [
        pltpu.make_async_copy(p_hbm.at[pl.ds(1, 2 * RING), core], mine, loads.at[0]),
        pltpu.make_async_copy(p_hbm.at[0], dq, loads.at[1]),
        pltpu.make_async_copy(wq_hbm, wq, loads.at[2]),
        pltpu.make_async_copy(wk_hbm, wkv.at[:, :CHANNEL_DIM], loads.at[3]),
        pltpu.make_async_copy(wv_hbm, wkv.at[:, CHANNEL_DIM:], loads.at[4]),
    ]
    for copy in local:
        copy.start()
    greet([places["sibling"], places["head_up"], places["head_down"], places["head_pair"], *around])

    swaps = [
        remote(
            p_hbm.at[pl.ds(1, 2 * RING), 1 - core, rows], side.at[:, rows],
            side_send.at[c], side_receive.at[c], places["sibling"],
        )
        for c, rows in enumerate(PARTS)
    ]
    swaps[0].start()
    sends = [
        [
            remote(
                held.at[r, p, rows], inbox.at[k, rows],
                ctx_send.at[c, k], ctx_receive.at[c, k], around[k],
            )
            for k, (r, p) in enumerate(others)
        ]
        for c, rows in enumerate(PARTS)
    ]
    rounds = [
        Reduce(
            leaving.at[:, :, rows],
            gone.at[:, :, pl.ds(rows.start // 2, rows.size // 2)],
            sums.at[:, :, rows],
            depth, head_send.at[c], head_receive.at[c], places["head_up"], places["head_down"],
        )
        for c, rows in enumerate(PARTS)
    ]
    across = [
        remote(
            crossing.at[rows], crossed.at[rows],
            pair_send.at[c], pair_receive.at[c], places["head_pair"],
        )
        for c, rows in enumerate(PARTS)
    ]

    def join(rows, r, p):
        return mine[2 * r + p, rows].astype(jnp.float32) + side[2 * r + p, rows].astype(jnp.float32)

    def pass_on(c):
        rows = PARTS[c]
        swaps[c].wait_recv()
        if c + 1 < len(PARTS):
            swaps[c + 1].start()
        for k, (r, p) in enumerate(others):
            held[r, p, rows] = join(rows, r, p).astype(jnp.bfloat16)
        for copy in sends[c]:
            copy.start()

    def query_parts(low, high):
        @pl.loop(low, high)
        def _(f):
            at = pl.ds(pl.multiple_of(f * FEATURES, FEATURES), FEATURES)
            query_grad = jnp.concatenate([dq[0], dq[1]], axis=1)
            parts[f] = lax.dot_general(
                query_grad, wq[at, :], (((1,), (1,)), ((), ())),
                preferred_element_type=jnp.float32,
            )

    def term(rows, f):
        return parts[f, rows, :] + lax.dot_general(
            dkv[rows], wkv[pl.ds(pl.multiple_of(f * FEATURES, FEATURES), FEATURES), :],
            (((1,), (1,)), ((), ())), preferred_element_type=jnp.float32,
        )

    def issue(c):
        rows = PARTS[c]
        total = join(rows, line, near)
        for k in range(len(sends[c])):
            sends[c][k].wait_recv()
            total = total + inbox[k, rows].astype(jnp.float32)
        dkv[rows] = total.astype(jnp.bfloat16)
        for d, ready in ((2, (0, 1)), (1, (2,)), (3, (3,))):
            r = (depth + d) % RING
            for p in range(2):
                leaving[r, p, rows] = term(rows, p * RING + r).astype(jnp.bfloat16)
            rounds[c].start(*ready)
        for p in range(2):
            left[p, rows] = term(rows, p * RING + depth)

    def cross(c):
        rows = PARTS[c]
        rounds[c].arrive()
        crossing[rows] = (left[1 - far, rows] + rounds[c].total(1 - far)).astype(jnp.bfloat16)
        across[c].start()
        left[far, rows] = left[far, rows] + rounds[c].total(far)

    last = len(PARTS) - 1
    local[0].wait()
    pass_on(0)
    local[1].wait()
    local[2].wait()
    query_parts(0, RING)
    pass_on(1)
    query_parts(RING, 2 * RING)
    pass_on(2)
    local[3].wait()
    local[4].wait()
    issue(0)
    for c in range(3, len(PARTS)):
        pass_on(c)
    for c in range(1, len(PARTS)):
        issue(c)
        rounds[c - 1].relay()
        if c > 1:
            cross(c - 2)
    rounds[last].relay()
    cross(last - 1)
    cross(last)
    for c, rows in enumerate(PARTS):
        across[c].wait_recv()
        out_ref[rows, :] = (
            left[far, rows] + crossed[rows].astype(jnp.float32)
        ).astype(jnp.bfloat16)
    for c in range(len(PARTS)):
        swaps[c].wait_send()
        across[c].wait_send()
        rounds[c].drain()
        for copy in sends[c]:
            copy.wait_send()


def back(pieces, w_query, w_key, value_projection):
    tokens = pieces.shape[2]
    chunks = len(PARTS)
    width, lanes = w_query.shape
    vmem = pl.BlockSpec(memory_space=pltpu.VMEM)
    hbm = pl.BlockSpec(memory_space=pl.ANY)
    wide = 2 * CHANNEL_DIM
    bf16, f32 = jnp.bfloat16, jnp.float32
    dma = pltpu.SemaphoreType.DMA
    return pl.pallas_call(
        back_kernel,
        out_shape=jax.ShapeDtypeStruct((tokens, FEATURES), bf16),
        in_specs=[hbm] * 4,
        out_specs=vmem,
        scratch_shapes=[
            pltpu.VMEM((2, tokens, wide), bf16),
            pltpu.VMEM((2 * RING, tokens, wide), bf16),
            pltpu.VMEM((width, lanes), bf16),
            pltpu.VMEM((width, wide), bf16),
            pltpu.VMEM((2 * RING, tokens, wide), bf16),
            pltpu.VMEM((RING, 2, tokens, wide), bf16),
            pltpu.VMEM((len(OFFSETS), tokens, wide), bf16),
            pltpu.VMEM((tokens, wide), bf16),
            pltpu.VMEM((2 * RING, tokens, FEATURES), f32),
            pltpu.VMEM((RING, 2, tokens, FEATURES), bf16),
            pltpu.VMEM((2, tokens, FEATURES), f32),
            pltpu.VMEM((2, 2, tokens // 2, FEATURES), bf16),
            pltpu.VMEM((2, 2, tokens, FEATURES), bf16),
            pltpu.VMEM((tokens, FEATURES), bf16),
            pltpu.VMEM((tokens, FEATURES), bf16),
            dma((5,)),
            dma((chunks,)),
            dma((chunks,)),
            dma((chunks, len(OFFSETS))),
            dma((chunks, len(OFFSETS))),
            dma((chunks, 6)),
            dma((chunks, 6)),
            dma((chunks,)),
            dma((chunks,)),
        ],
        compiler_params=pltpu.CompilerParams(
            collective_id=1, has_side_effects=True, vmem_limit_bytes=54000 * 1024
        ),
        name="back",
    )(pieces, w_query, w_key, value_projection)


def attention_kernel(
    span_ref, length_ref, q_hbm, g_hbm, kv_hbm,
    out_hbm,
    kvs, qs, gs, s_buf, d_buf, acc, dqt, q_ref, g_ref, dq_ref, dkv_ref, blank, row_of,
    loads, stores,
):
    exponent = LOG2E / math.sqrt(CHANNEL_DIM)
    scale = 1.0 / math.sqrt(CHANNEL_DIM)
    spans = span_ref.shape[0]
    tokens, wide = q_ref.shape[0], 2 * CHANNEL_DIM
    local = [
        pltpu.make_async_copy(q_hbm, q_ref, loads.at[0]),
        pltpu.make_async_copy(g_hbm, g_ref, loads.at[1]),
    ]
    for copy in local:
        copy.start()
    blank[...] = jnp.zeros_like(blank)

    places = []
    for b in range(2):
        c = span_ref[2 * lax.axis_index("ctx") + b]
        first = 0
        end = 0
        for k in range(length_ref.shape[0]):
            end = end + length_ref[k]
            first = jnp.where(c * HALF >= end, end, first)
        places.append((c, first // TILE, c // (TILE // HALF) + 1))

    def reached(p):
        t = p // (TILE // HALF)
        return jnp.logical_or(
            *[jnp.logical_and(t >= low, t < high) for c, low, high in places]
        )

    def rows_at(n):
        return pl.ds(pl.multiple_of(n * HALF, HALF), HALF)

    def block_in(r, p):
        return pltpu.make_async_copy(
            kv_hbm.at[rows_at(r), :], kvs.at[rows_at(p), :], loads.at[2]
        )

    def block_out(block, r):
        return pltpu.make_async_copy(
            block, out_hbm.at[rows_at(r + 2 * tokens // HALF), :], stores.at[1]
        )

    @pl.loop(0, spans)
    def _(r):
        p = span_ref[r]
        row_of[p] = r

        @pl.when(reached(p))
        def _():
            block_in(r, p).start()

        @pl.when(jnp.logical_not(reached(p)))
        def _():
            block_out(blank, r).start()

    for c, low, high in places:

        @pl.loop(low, high)
        def _(t):
            acc[pl.ds(pl.multiple_of(t * TILE, TILE), TILE), :] = jnp.zeros((TILE, wide), jnp.float32)

    for copy in local:
        copy.wait()

    @pl.loop(0, spans)
    def _(r):
        p = span_ref[r]

        @pl.when(reached(p))
        def _():
            block_in(r, p).wait()

    lanes = BUNDLE * HALF
    for b in range(2):
        rows = slice(b * HALF, (b + 1) * HALF)
        for h in range(BUNDLE):
            cols = slice(h * CHANNEL_DIM, (h + 1) * CHANNEL_DIM)
            qs[h * HALF : (h + 1) * HALF, :] = q_ref[rows, cols]
            gs[h * HALF : (h + 1) * HALF, :] = g_ref[rows, cols]
        c, low, high = places[b]
        position = c * HALF + lax.broadcasted_iota(jnp.int32, (1, HALF), 1)
        start = jnp.zeros((1, HALF), jnp.int32)
        end = 0
        for k in range(length_ref.shape[0]):
            end = end + length_ref[k]
            start = jnp.where(position >= end, end, start)

        def gather_stats(t, carry):
            top, total, inner = carry
            at = pl.ds(pl.multiple_of(t * TILE, TILE), TILE)
            keys = kvs[at, :CHANNEL_DIM]
            values = kvs[at, CHANNEL_DIM:]
            key_position = t * TILE + lax.broadcasted_iota(jnp.int32, (TILE, HALF), 0)
            bias = jnp.where(
                (key_position <= position) & (key_position >= start), 0.0, MASKED
            )
            bias = jnp.concatenate([bias] * BUNDLE, axis=1)
            s = lax.dot_general(
                keys, qs[...], (((1,), (1,)), ((), ())), preferred_element_type=jnp.float32
            )
            s = s * exponent + bias
            s_buf[at, :] = s
            fresh = jnp.maximum(top, jnp.max(s, axis=0, keepdims=True))
            factor = jnp.exp2(top - fresh)
            e = jnp.exp2(s - fresh)
            slopes = lax.dot_general(
                values, gs[...], (((1,), (1,)), ((), ())), preferred_element_type=jnp.float32
            )
            d_buf[at, :] = slopes
            total = total * factor + jnp.sum(e, axis=0, keepdims=True)
            inner = inner * factor + jnp.sum(e * slopes, axis=0, keepdims=True)
            return fresh, total, inner

        zero = jnp.zeros((1, lanes), jnp.float32)
        pairs = (high - low) // 2
        odd = low + 2 * pairs
        top, total, inner = lax.fori_loop(
            odd,
            high,
            gather_stats,
            lax.fori_loop(
                0,
                pairs,
                lambda k, carry: gather_stats(
                    low + 2 * k + 1, gather_stats(low + 2 * k, carry)
                ),
                (jnp.full((1, lanes), MASKED, jnp.float32), zero, zero),
            ),
        )
        delta = inner / total
        level = top + jnp.log2(total)
        dqt[...] = jnp.zeros_like(dqt)

        def spread_grads(t):
            at = pl.ds(pl.multiple_of(t * TILE, TILE), TILE)
            probability = jnp.exp2(s_buf[at, :] - level)
            score_grad = (probability * (d_buf[at, :] - delta)).astype(jnp.bfloat16)
            rounded = probability.astype(jnp.bfloat16)
            acc[at, CHANNEL_DIM:] += jnp.dot(rounded, gs[...], preferred_element_type=jnp.float32)
            acc[at, :CHANNEL_DIM] += jnp.dot(score_grad, qs[...], preferred_element_type=jnp.float32)
            dqt[...] += lax.dot_general(
                kvs[at, :CHANNEL_DIM], score_grad, (((0,), (0,)), ((), ())),
                preferred_element_type=jnp.float32,
            )

        @pl.loop(0, pairs)
        def _(k):
            spread_grads(low + 2 * k)
            spread_grads(low + 2 * k + 1)

        @pl.loop(odd, high)
        def _(t):
            spread_grads(t)

        for h in range(BUNDLE):
            to = slice(h // 2 * tokens + b * HALF, h // 2 * tokens + (b + 1) * HALF)
            dq_ref[to, h % 2 * CHANNEL_DIM : (h % 2 + 1) * CHANNEL_DIM] = (
                (dqt[:, h * HALF : (h + 1) * HALF] * scale).T.astype(jnp.bfloat16)
            )

    grads = pltpu.make_async_copy(dq_ref, out_hbm.at[pl.ds(0, 2 * tokens), :], stores.at[0])
    grads.start()

    def finish(p):
        r = row_of[p]
        at, to = rows_at(p), rows_at(r)
        dkv_ref[to, :CHANNEL_DIM] = (acc[at, :CHANNEL_DIM] * scale).astype(jnp.bfloat16)
        dkv_ref[to, CHANNEL_DIM:] = acc[at, CHANNEL_DIM:].astype(jnp.bfloat16)
        block_out(dkv_ref.at[to, :], r).start()

    for b, (c, low, high) in enumerate(places):

        @pl.loop(low, high)
        def _(t):
            fresh = True
            if b:
                fresh = jnp.logical_or(t < places[0][1], t >= places[0][2])

            @pl.when(fresh)
            def _():
                for k in range(TILE // HALF):
                    finish(t * (TILE // HALF) + k)

    grads.wait()
    pltpu.make_async_copy(
        dkv_ref, out_hbm.at[pl.ds(2 * tokens, dkv_ref.shape[0]), :], stores.at[1]
    ).wait()


def attention(q, g, kv, span_order, doc_lengths):
    tokens = q.shape[0]
    length = kv.shape[0]
    smem = pl.BlockSpec(memory_space=pltpu.SMEM)
    hbm = pl.BlockSpec(memory_space=pl.ANY)
    lanes = BUNDLE * HALF
    return pl.pallas_call(
        attention_kernel,
        out_shape=jax.ShapeDtypeStruct((2 * tokens + length, 2 * CHANNEL_DIM), jnp.bfloat16),
        in_specs=[smem, smem, hbm, hbm, hbm],
        out_specs=hbm,
        scratch_shapes=[
            pltpu.VMEM((length, 2 * CHANNEL_DIM), jnp.bfloat16),
            pltpu.VMEM((lanes, CHANNEL_DIM), jnp.bfloat16),
            pltpu.VMEM((lanes, CHANNEL_DIM), jnp.bfloat16),
            pltpu.VMEM((length, lanes), jnp.float32),
            pltpu.VMEM((length, lanes), jnp.float32),
            pltpu.VMEM((length, 2 * CHANNEL_DIM), jnp.float32),
            pltpu.VMEM((CHANNEL_DIM, lanes), jnp.float32),
            pltpu.VMEM((tokens, lanes), jnp.bfloat16),
            pltpu.VMEM((tokens, lanes), jnp.bfloat16),
            pltpu.VMEM((2 * tokens, 2 * CHANNEL_DIM), jnp.bfloat16),
            pltpu.VMEM((length, 2 * CHANNEL_DIM), jnp.bfloat16),
            pltpu.VMEM((HALF, 2 * CHANNEL_DIM), jnp.bfloat16),
            pltpu.SMEM((length // HALF,), jnp.int32),
            pltpu.SemaphoreType.DMA((3,)),
            pltpu.SemaphoreType.DMA((2,)),
        ],
        compiler_params=pltpu.CompilerParams(vmem_limit_bytes=GRANT),
        name="attention",
    )(span_order, doc_lengths, q, g, kv)


def shards(inputs, out_grad, w_query, w_key, value_projection, w_out, doc_lengths, span_order):
    tokens = inputs.shape[0]
    peers = lax.axis_size("ctx")
    query, context_grad, gathered = front(
        inputs, out_grad, w_query, w_key, value_projection, w_out, peers
    )
    pieces = attention(
        query, context_grad, gathered.reshape(peers * tokens, -1), span_order, doc_lengths
    )
    pieces = pieces.reshape(1 + 2 * RING, 2, tokens, -1)
    return back(pieces, w_query, w_key, value_projection)


def solution(mesh):
    in_specs = (
        P("ctx", None),
        P("ctx", "head"),
        P(None, "head"),
        P(None, "head"),
        P(None, "head"),
        P("head", None),
        P(),
        P(),
    )
    return jax.shard_map(
        shards, mesh=mesh, in_specs=in_specs, out_specs=P("ctx", "head"), check_vma=False
    )
```

```python
import math

import jax
import jax.numpy as jnp
from jax import lax
from jax.experimental import pallas as pl
from jax.experimental.pallas import tpu as pltpu
from jax.sharding import PartitionSpec as P

ASKER_NUM = 32
SHARED_KV_NUM = 8
CHANNEL_DIM = 128
BUNDLE = ASKER_NUM // SHARED_KV_NUM
HALF = 128
TILE = 256
RING = 4
FEATURES = 512
PARTS = tuple(pl.ds(*cut) for cut in ((0, 64), (64, 64), (128, 64), (192, 64)))
OFFSETS = ((2, 1), (2, 0), (1, 1), (3, 1), (1, 0), (3, 0), (0, 1))
LOG2E = 1.4426950408889634
MASKED = -1e30
OWN = ("u0", "d1", "x0", "x2", "u1", "d0", "x1", "x3")
GRANT = 60 * 1024 * 1024
MESH = pl.DeviceIdType.MESH


def remote(src, dst, send, receive, place):
    return pltpu.make_async_remote_copy(
        src_ref=src, dst_ref=dst, send_sem=send, recv_sem=receive,
        device_id=place, device_id_type=MESH,
    )


def greet(places):
    barrier = pltpu.get_barrier_semaphore()
    for place in places:
        pl.semaphore_signal(barrier, inc=1, device_id=place, device_id_type=MESH)
    pl.semaphore_wait(barrier, len(places))


def neighbours():
    head = lax.axis_index("head")
    ctx = lax.axis_index("ctx")
    far, depth = head // RING, head % RING
    line, near, core = ctx // 4, (ctx // 2) % 2, ctx % 2

    def head_of(f, d):
        return f * RING + d

    def ctx_of(r, n, c):
        return r * 4 + n * 2 + c

    places = {
        "head_up": (head_of(far, (depth + 1) % RING), ctx),
        "head_down": (head_of(far, (depth + 3) % RING), ctx),
        "head_pair": (head_of(1 - far, depth), ctx),
        "ctx_up": (head, ctx_of((line + 1) % RING, near, core)),
        "ctx_down": (head, ctx_of((line + 3) % RING, near, core)),
        "ctx_pair": (head, ctx_of(line, 1 - near, core)),
        "ctx_far": (head, ctx_of((line + 2) % RING, near, core)),
        "sibling": (head, ctx_of(line, near, 1 - core)),
    }
    return places, (far, depth), (line, near, core)


class Gather:
    def __init__(self, source, block, pair, ring, sends, receives, up, down, across, opposed=None):
        other = 1 - pair
        before, after, opposite = (ring + 3) % RING, (ring + 1) % RING, (ring + 2) % RING
        cut = HALF // 2

        def part(p, r, start, size):
            return block(p, r).at[pl.ds(start * cut, size * cut), :]

        own, facing = (pair, ring), (other, ring)
        plan = {
            "u0": (own, (pair, before), 0, 2, up),
            "d1": (own, (pair, after), 2, 2, down),
            "x0": (own, facing, 0, 1, across),
            "x2": (own, facing, 2, 1, across),
            "u1": (own, (pair, before), 2, 2, up),
            "d0": (own, (pair, after), 0, 2, down),
            "x1": (own, facing, 1, 1, across),
            "x3": (own, facing, 3, 1, across),
            "ru": ((pair, before), (pair, opposite), 0, 2, up),
            "rd": ((pair, after), (pair, opposite), 2, 2, down),
            "ou0": (facing, (other, before), 0, 1, up),
            "od2": (facing, (other, after), 2, 1, down),
            "ou1": (facing, (other, before), 1, 2, up),
            "od0": (facing, (other, after), 0, 1, down),
            "od3": (facing, (other, after), 3, 1, down),
            "xb": ((pair, before), (other, before), 3, 1, across),
            "xa": ((pair, after), (other, after), 1, 1, across),
            "rou": ((other, before), (other, opposite), 0, 1, up),
            "rod": ((other, after), (other, opposite), 2, 1, down),
            "xo1": ((pair, opposite), (other, opposite), 1, 1, across),
            "xo3": ((pair, opposite), (other, opposite), 3, 1, across),
        }
        if opposed is not None:
            plan["ou0"] = (facing, (other, before), 0, 2, up)
            plan["ou1"] = (facing, (other, before), 2, 2, up)
            plan["od0"] = (facing, (other, after), 0, 2, down)
            plan["od2"] = (facing, (other, after), 2, 2, down)
            plan["oo"] = (facing, (other, opposite), 0, 4, opposed)
            for name in ("od3", "xb", "xa", "xo1", "xo3", "rou", "rod"):
                del plan[name]
        self.copies = {}
        for k, (name, (at, to, start, size, place)) in enumerate(plan.items()):
            there, here = part(*at, start, size), part(*to, start, size)
            first = source(pl.ds(start * cut, size * cut)) if at is own else there
            self.copies[name] = (
                remote(first, there, sends.at[k], receives.at[k], place),
                remote(here, here, sends.at[k], receives.at[k], place),
            )

    def start(self, *names):
        for name in names:
            self.copies[name][0].start()

    def arrive(self, *names):
        for name in names:
            self.copies[name][1].wait_recv()

    def drain(self):
        for sent, landed in self.copies.values():
            sent.wait_send()


def front_kernel(
    x_hbm, og_hbm, wq_hbm, wk_hbm, wv_hbm, wo_hbm,
    q_hbm, g_hbm, kv_hbm,
    x, wq, wkv, wo, og, acc, q_ref, g_ref, kv_ref,
    loads, stores, head_send, head_receive, ctx_send, ctx_receive, sibling_send, sibling_receive,
):
    places, (far, depth), (line, near, core) = neighbours()
    me = far * RING + depth
    local = [
        pltpu.make_async_copy(x_hbm, x, loads.at[0]),
        pltpu.make_async_copy(wk_hbm, wkv.at[:, :CHANNEL_DIM], loads.at[1]),
        pltpu.make_async_copy(wv_hbm, wkv.at[:, CHANNEL_DIM:], loads.at[2]),
        pltpu.make_async_copy(wq_hbm, wq, loads.at[3]),
        pltpu.make_async_copy(og_hbm, og.at[me], loads.at[4]),
        pltpu.make_async_copy(wo_hbm, wo, loads.at[5]),
    ]
    for copy in local[:3]:
        copy.start()
    saved = [
        pltpu.make_async_copy(q_ref, q_hbm, stores.at[0]),
        pltpu.make_async_copy(kv_ref, kv_hbm, stores.at[1]),
        pltpu.make_async_copy(g_ref, g_hbm, stores.at[2]),
    ]
    greet(list(places.values()))

    heads = Gather(
        lambda rows: og_hbm.at[rows, :],
        lambda p, r: og.at[p * RING + r],
        far, depth, head_send, head_receive,
        places["head_up"], places["head_down"], places["head_pair"],
    )
    heads.start(*OWN)
    for copy in local[3:]:
        copy.start()

    def slot(p, r, c=core):
        return r * 4 + p * 2 + c

    spread = Gather(
        lambda rows: kv_ref.at[slot(near, line), rows, :],
        lambda p, r: kv_ref.at[slot(p, r)],
        near, line, ctx_send, ctx_receive,
        places["ctx_up"], places["ctx_down"], places["ctx_pair"],
        places["ctx_far"],
    )
    turns = [(p, (line + d) % RING) for p in (near, 1 - near) for d in (0, 3, 1, 2)]
    passed = [
        (
            remote(
                kv_ref.at[slot(p, r)], kv_ref.at[slot(p, r)],
                sibling_send.at[k], sibling_receive.at[k], places["sibling"],
            ),
            remote(
                kv_ref.at[slot(p, r, 1 - core)], kv_ref.at[slot(p, r, 1 - core)],
                sibling_send.at[k], sibling_receive.at[k], places["sibling"],
            ),
        )
        for k, (p, r) in enumerate(turns)
    ]

    def features(p, r):
        f = p * RING + r
        return lax.dot_general(
            og[f], wo[:, pl.ds(pl.multiple_of(f * FEATURES, FEATURES), FEATURES)],
            (((1,), (1,)), ((), ())), preferred_element_type=jnp.float32,
        )

    for k in (0, 1, 2):
        local[k].wait()
    kv_ref[slot(near, line)] = jnp.dot(
        x[...], wkv[...], preferred_element_type=jnp.float32
    ).astype(jnp.bfloat16)
    def query(k):
        columns = slice(k * wq.shape[1] // 2, (k + 1) * wq.shape[1] // 2)
        q_ref[:, columns] = jnp.dot(
            x[...], wq[:, columns], preferred_element_type=jnp.float32
        ).astype(jnp.bfloat16)

    def keep(at):
        pltpu.make_async_copy(kv_ref.at[at], kv_hbm.at[at], stores.at[1]).start()

    def share(k):
        passed[k][0].start()
        keep(slot(*turns[k]))

    local[3].wait()
    query(0)
    spread.start(*OWN)
    share(0)
    query(1)
    saved[0].start()
    before, after, opposite = (depth + 3) % RING, (depth + 1) % RING, (depth + 2) % RING
    heads.arrive("u0")
    heads.start("ru")
    heads.arrive("d1")
    heads.start("rd")
    heads.arrive("x0", "x2")
    heads.start("ou0", "od2", "od0")
    local[4].wait()
    local[5].wait()
    acc[...] = features(far, depth)
    spread.arrive("u0")
    spread.start("ru")
    spread.arrive("d1")
    spread.start("rd")
    heads.arrive("u1")
    heads.start("xb")
    heads.arrive("d0")
    heads.start("xa")
    spread.arrive("x0", "x1")
    spread.start("ou0", "od0")
    spread.arrive("x2", "x3")
    spread.start("oo", "od2", "ou1")
    share(4)
    acc[...] += features(far, before)
    heads.arrive("x1")
    heads.start("ou1")
    heads.arrive("x3")
    heads.start("od3")
    spread.arrive("u1")
    share(1)
    spread.arrive("d0")
    share(2)
    acc[...] += features(far, after)
    heads.arrive("ru")
    heads.start("xo1")
    heads.arrive("rd")
    heads.start("xo3")
    acc[...] += features(1 - far, depth)
    spread.arrive("ru", "rd")
    share(3)
    heads.arrive("ou0")
    heads.start("rou")
    heads.arrive("od2")
    heads.start("rod")
    spread.arrive("oo")
    share(7)
    acc[...] += features(far, opposite)
    spread.arrive("ou0", "ou1")
    share(5)
    spread.arrive("od0", "od2")
    share(6)
    heads.arrive("ou1", "xb")
    acc[...] += features(1 - far, before)
    heads.arrive("od0", "od3", "xa")
    acc[...] += features(1 - far, after)
    for k, (sent, landed) in enumerate(passed):
        landed.wait_recv()
        keep(slot(*turns[k], 1 - core))
    heads.arrive("rou", "rod", "xo1", "xo3")
    g_ref[...] = (acc[...] + features(1 - far, opposite)).astype(jnp.bfloat16)
    saved[2].start()
    heads.drain()
    spread.drain()
    for sent, landed in passed:
        sent.wait_send()
    for copy in saved:
        copy.wait()


def front(inputs, out_grad, w_query, w_key, value_projection, w_out, peers):
    tokens, width = inputs.shape
    lanes = w_query.shape[1]
    hbm = pl.BlockSpec(memory_space=pl.ANY)
    return pl.pallas_call(
        front_kernel,
        out_shape=(
            jax.ShapeDtypeStruct((tokens, lanes), jnp.bfloat16),
            jax.ShapeDtypeStruct((tokens, lanes), jnp.bfloat16),
            jax.ShapeDtypeStruct((peers, tokens, 2 * CHANNEL_DIM), jnp.bfloat16),
        ),
        in_specs=[hbm] * 6,
        out_specs=(hbm, hbm, hbm),
        scratch_shapes=[
            pltpu.VMEM((tokens, width), jnp.bfloat16),
            pltpu.VMEM((width, lanes), jnp.bfloat16),
            pltpu.VMEM((width, 2 * CHANNEL_DIM), jnp.bfloat16),
            pltpu.VMEM((lanes, width), jnp.bfloat16),
            pltpu.VMEM((2 * RING, tokens, FEATURES), jnp.bfloat16),
            pltpu.VMEM((tokens, lanes), jnp.float32),
            pltpu.VMEM((tokens, lanes), jnp.bfloat16),
            pltpu.VMEM((tokens, lanes), jnp.bfloat16),
            pltpu.VMEM((peers, tokens, 2 * CHANNEL_DIM), jnp.bfloat16),
            pltpu.SemaphoreType.DMA((6,)),
            pltpu.SemaphoreType.DMA((3,)),
            pltpu.SemaphoreType.DMA((21,)),
            pltpu.SemaphoreType.DMA((21,)),
            pltpu.SemaphoreType.DMA((21,)),
            pltpu.SemaphoreType.DMA((21,)),
            pltpu.SemaphoreType.DMA((8,)),
            pltpu.SemaphoreType.DMA((8,)),
        ],
        compiler_params=pltpu.CompilerParams(
            collective_id=0, has_side_effects=True, vmem_limit_bytes=GRANT
        ),
        name="front",
    )(inputs, out_grad, w_query, w_key, value_projection, w_out)


class Reduce:
    def __init__(self, held, gone, sums, ring, sends, receives, up, down):
        self.held, self.gone, self.sums = held, gone, sums
        self.before, self.after = (ring + 3) % RING, (ring + 1) % RING
        opposite = (ring + 2) % RING
        self.cut = held.shape[2] // 2
        low, high = pl.ds(0, self.cut), pl.ds(self.cut, self.cut)
        plan = [
            (held.at[opposite, :, low], gone.at[0], up),
            (held.at[opposite, :, high], gone.at[1], down),
            (held.at[self.after, :, high], sums.at[0, :, high], up),
            (held.at[self.before, :, low], sums.at[1, :, low], down),
            (held.at[self.after, :, low], sums.at[0, :, low], up),
            (held.at[self.before, :, high], sums.at[1, :, high], down),
        ]
        self.copies = [
            remote(src, dst, sends.at[k], receives.at[k], place)
            for k, (src, dst, place) in enumerate(plan)
        ]

    def start(self, *which):
        for k in which:
            self.copies[k].start()

    def relay(self):
        low, high = slice(0, self.cut), slice(self.cut, 2 * self.cut)
        for k, r, rows in ((0, self.after, low), (1, self.before, high)):
            self.copies[k].wait_recv()
            for p in range(2):
                self.held[r, p, rows] = (
                    self.held[r, p, rows].astype(jnp.float32)
                    + self.gone[k, p].astype(jnp.float32)
                ).astype(jnp.bfloat16)
            self.start(4 + k)

    def arrive(self):
        for k in (2, 3, 4, 5):
            self.copies[k].wait_recv()

    def total(self, p):
        return self.sums[0, p].astype(jnp.float32) + self.sums[1, p].astype(jnp.float32)

    def drain(self):
        for copy in self.copies:
            copy.wait_send()


def back_kernel(
    p_hbm, wq_hbm, wk_hbm, wv_hbm,
    out_ref,
    dq, mine, wq, wkv, side, held, inbox, dkv, parts, leaving, left, gone, sums, crossing, crossed,
    loads, side_send, side_receive, ctx_send, ctx_receive, head_send, head_receive,
    pair_send, pair_receive,
):
    places, (far, depth), (line, near, core) = neighbours()
    head, ctx = lax.axis_index("head"), lax.axis_index("ctx")
    others = [
        ((line + d) % RING, (near + n) % 2) for d, n in OFFSETS
    ]
    around = [(head, r * 4 + p * 2 + core) for r, p in others]
    local = [
        pltpu.make_async_copy(p_hbm.at[pl.ds(1, 2 * RING), core], mine, loads.at[0]),
        pltpu.make_async_copy(p_hbm.at[0], dq, loads.at[1]),
        pltpu.make_async_copy(wq_hbm, wq, loads.at[2]),
        pltpu.make_async_copy(wk_hbm, wkv.at[:, :CHANNEL_DIM], loads.at[3]),
        pltpu.make_async_copy(wv_hbm, wkv.at[:, CHANNEL_DIM:], loads.at[4]),
    ]
    for copy in local:
        copy.start()
    greet([places["sibling"], places["head_up"], places["head_down"], places["head_pair"], *around])

    swaps = [
        remote(
            p_hbm.at[pl.ds(1, 2 * RING), 1 - core, rows], side.at[:, rows],
            side_send.at[c], side_receive.at[c], places["sibling"],
        )
        for c, rows in enumerate(PARTS)
    ]
    swaps[0].start()
    sends = [
        [
            remote(
                held.at[r, p, rows], inbox.at[k, rows],
                ctx_send.at[c, k], ctx_receive.at[c, k], around[k],
            )
            for k, (r, p) in enumerate(others)
        ]
        for c, rows in enumerate(PARTS)
    ]
    rounds = [
        Reduce(
            leaving.at[:, :, rows],
            gone.at[:, :, pl.ds(rows.start // 2, rows.size // 2)],
            sums.at[:, :, rows],
            depth, head_send.at[c], head_receive.at[c], places["head_up"], places["head_down"],
        )
        for c, rows in enumerate(PARTS)
    ]
    across = [
        remote(
            crossing.at[rows], crossed.at[rows],
            pair_send.at[c], pair_receive.at[c], places["head_pair"],
        )
        for c, rows in enumerate(PARTS)
    ]

    def join(rows, r, p):
        return mine[2 * r + p, rows].astype(jnp.float32) + side[2 * r + p, rows].astype(jnp.float32)

    def pass_on(c):
        rows = PARTS[c]
        swaps[c].wait_recv()
        if c + 1 < len(PARTS):
            swaps[c + 1].start()
        for k, (r, p) in enumerate(others):
            held[r, p, rows] = join(rows, r, p).astype(jnp.bfloat16)
        for copy in sends[c]:
            copy.start()

    def query_parts(low, high):
        @pl.loop(low, high)
        def _(f):
            at = pl.ds(pl.multiple_of(f * FEATURES, FEATURES), FEATURES)
            query_grad = jnp.concatenate([dq[0], dq[1]], axis=1)
            parts[f] = lax.dot_general(
                query_grad, wq[at, :], (((1,), (1,)), ((), ())),
                preferred_element_type=jnp.float32,
            )

    def term(rows, f):
        return parts[f, rows, :] + lax.dot_general(
            dkv[rows], wkv[pl.ds(pl.multiple_of(f * FEATURES, FEATURES), FEATURES), :],
            (((1,), (1,)), ((), ())), preferred_element_type=jnp.float32,
        )

    def issue(c):
        rows = PARTS[c]
        total = join(rows, line, near)
        for k in range(len(sends[c])):
            sends[c][k].wait_recv()
            total = total + inbox[k, rows].astype(jnp.float32)
        dkv[rows] = total.astype(jnp.bfloat16)
        for d, ready in ((2, (0, 1)), (1, (2,)), (3, (3,))):
            r = (depth + d) % RING
            for p in range(2):
                leaving[r, p, rows] = term(rows, p * RING + r).astype(jnp.bfloat16)
            rounds[c].start(*ready)
        for p in range(2):
            left[p, rows] = term(rows, p * RING + depth)

    def cross(c):
        rows = PARTS[c]
        rounds[c].arrive()
        crossing[rows] = (left[1 - far, rows] + rounds[c].total(1 - far)).astype(jnp.bfloat16)
        across[c].start()
        left[far, rows] = left[far, rows] + rounds[c].total(far)

    last = len(PARTS) - 1
    local[0].wait()
    pass_on(0)
    local[1].wait()
    local[2].wait()
    query_parts(0, RING)
    pass_on(1)
    query_parts(RING, 2 * RING)
    pass_on(2)
    local[3].wait()
    local[4].wait()
    issue(0)
    for c in range(3, len(PARTS)):
        pass_on(c)
    for c in range(1, len(PARTS)):
        issue(c)
        rounds[c - 1].relay()
        if c > 1:
            cross(c - 2)
    rounds[last].relay()
    cross(last - 1)
    cross(last)
    for c, rows in enumerate(PARTS):
        across[c].wait_recv()
        out_ref[rows, :] = (
            left[far, rows] + crossed[rows].astype(jnp.float32)
        ).astype(jnp.bfloat16)
    for c in range(len(PARTS)):
        swaps[c].wait_send()
        across[c].wait_send()
        rounds[c].drain()
        for copy in sends[c]:
            copy.wait_send()


def back(pieces, w_query, w_key, value_projection):
    tokens = pieces.shape[2]
    chunks = len(PARTS)
    width, lanes = w_query.shape
    vmem = pl.BlockSpec(memory_space=pltpu.VMEM)
    hbm = pl.BlockSpec(memory_space=pl.ANY)
    wide = 2 * CHANNEL_DIM
    bf16, f32 = jnp.bfloat16, jnp.float32
    dma = pltpu.SemaphoreType.DMA
    return pl.pallas_call(
        back_kernel,
        out_shape=jax.ShapeDtypeStruct((tokens, FEATURES), bf16),
        in_specs=[hbm] * 4,
        out_specs=vmem,
        scratch_shapes=[
            pltpu.VMEM((2, tokens, wide), bf16),
            pltpu.VMEM((2 * RING, tokens, wide), bf16),
            pltpu.VMEM((width, lanes), bf16),
            pltpu.VMEM((width, wide), bf16),
            pltpu.VMEM((2 * RING, tokens, wide), bf16),
            pltpu.VMEM((RING, 2, tokens, wide), bf16),
            pltpu.VMEM((len(OFFSETS), tokens, wide), bf16),
            pltpu.VMEM((tokens, wide), bf16),
            pltpu.VMEM((2 * RING, tokens, FEATURES), f32),
            pltpu.VMEM((RING, 2, tokens, FEATURES), bf16),
            pltpu.VMEM((2, tokens, FEATURES), f32),
            pltpu.VMEM((2, 2, tokens // 2, FEATURES), bf16),
            pltpu.VMEM((2, 2, tokens, FEATURES), bf16),
            pltpu.VMEM((tokens, FEATURES), bf16),
            pltpu.VMEM((tokens, FEATURES), bf16),
            dma((5,)),
            dma((chunks,)),
            dma((chunks,)),
            dma((chunks, len(OFFSETS))),
            dma((chunks, len(OFFSETS))),
            dma((chunks, 6)),
            dma((chunks, 6)),
            dma((chunks,)),
            dma((chunks,)),
        ],
        compiler_params=pltpu.CompilerParams(
            collective_id=1, has_side_effects=True, vmem_limit_bytes=54000 * 1024
        ),
        name="back",
    )(pieces, w_query, w_key, value_projection)


def attention_kernel(
    span_ref, length_ref, q_hbm, g_hbm, kv_hbm,
    out_hbm,
    kvs, qs, gs, s_buf, d_buf, acc, dqt, q_ref, g_ref, dq_ref, dkv_ref, blank, row_of,
    loads, stores,
):
    exponent = LOG2E / math.sqrt(CHANNEL_DIM)
    scale = 1.0 / math.sqrt(CHANNEL_DIM)
    spans = span_ref.shape[0]
    tokens, wide = q_ref.shape[0], 2 * CHANNEL_DIM
    local = [
        pltpu.make_async_copy(q_hbm, q_ref, loads.at[0]),
        pltpu.make_async_copy(g_hbm, g_ref, loads.at[1]),
    ]
    for copy in local:
        copy.start()
    blank[...] = jnp.zeros_like(blank)

    places = []
    for b in range(2):
        c = span_ref[2 * lax.axis_index("ctx") + b]
        first = 0
        end = 0
        for k in range(length_ref.shape[0]):
            end = end + length_ref[k]
            first = jnp.where(c * HALF >= end, end, first)
        places.append((c, first // TILE, c // (TILE // HALF) + 1))

    def reached(p):
        t = p // (TILE // HALF)
        return jnp.logical_or(
            *[jnp.logical_and(t >= low, t < high) for c, low, high in places]
        )

    def rows_at(n):
        return pl.ds(pl.multiple_of(n * HALF, HALF), HALF)

    def block_in(r, p):
        return pltpu.make_async_copy(
            kv_hbm.at[rows_at(r), :], kvs.at[rows_at(p), :], loads.at[2]
        )

    def block_out(block, r):
        return pltpu.make_async_copy(
            block, out_hbm.at[rows_at(r + 2 * tokens // HALF), :], stores.at[1]
        )

    @pl.loop(0, spans)
    def _(r):
        p = span_ref[r]
        row_of[p] = r

        @pl.when(reached(p))
        def _():
            block_in(r, p).start()

        @pl.when(jnp.logical_not(reached(p)))
        def _():
            block_out(blank, r).start()

    for c, low, high in places:

        @pl.loop(low, high)
        def _(t):
            acc[pl.ds(pl.multiple_of(t * TILE, TILE), TILE), :] = jnp.zeros((TILE, wide), jnp.float32)

    for copy in local:
        copy.wait()

    @pl.loop(0, spans)
    def _(r):
        p = span_ref[r]

        @pl.when(reached(p))
        def _():
            block_in(r, p).wait()

    lanes = BUNDLE * HALF
    for b in range(2):
        rows = slice(b * HALF, (b + 1) * HALF)
        for h in range(BUNDLE):
            cols = slice(h * CHANNEL_DIM, (h + 1) * CHANNEL_DIM)
            qs[h * HALF : (h + 1) * HALF, :] = q_ref[rows, cols]
            gs[h * HALF : (h + 1) * HALF, :] = g_ref[rows, cols]
        c, low, high = places[b]
        position = c * HALF + lax.broadcasted_iota(jnp.int32, (1, HALF), 1)
        start = jnp.zeros((1, HALF), jnp.int32)
        end = 0
        for k in range(length_ref.shape[0]):
            end = end + length_ref[k]
            start = jnp.where(position >= end, end, start)

        def gather_stats(t, carry):
            top, total, inner = carry
            at = pl.ds(pl.multiple_of(t * TILE, TILE), TILE)
            keys = kvs[at, :CHANNEL_DIM]
            values = kvs[at, CHANNEL_DIM:]
            key_position = t * TILE + lax.broadcasted_iota(jnp.int32, (TILE, HALF), 0)
            bias = jnp.where(
                (key_position <= position) & (key_position >= start), 0.0, MASKED
            )
            bias = jnp.concatenate([bias] * BUNDLE, axis=1)
            s = lax.dot_general(
                keys, qs[...], (((1,), (1,)), ((), ())), preferred_element_type=jnp.float32
            )
            s = s * exponent + bias
            s_buf[at, :] = s
            fresh = jnp.maximum(top, jnp.max(s, axis=0, keepdims=True))
            factor = jnp.exp2(top - fresh)
            e = jnp.exp2(s - fresh)
            slopes = lax.dot_general(
                values, gs[...], (((1,), (1,)), ((), ())), preferred_element_type=jnp.float32
            )
            d_buf[at, :] = slopes
            total = total * factor + jnp.sum(e, axis=0, keepdims=True)
            inner = inner * factor + jnp.sum(e * slopes, axis=0, keepdims=True)
            return fresh, total, inner

        zero = jnp.zeros((1, lanes), jnp.float32)
        pairs = (high - low) // 2
        odd = low + 2 * pairs
        top, total, inner = lax.fori_loop(
            odd,
            high,
            gather_stats,
            lax.fori_loop(
                0,
                pairs,
                lambda k, carry: gather_stats(
                    low + 2 * k + 1, gather_stats(low + 2 * k, carry)
                ),
                (jnp.full((1, lanes), MASKED, jnp.float32), zero, zero),
            ),
        )
        delta = inner / total
        level = top + jnp.log2(total)
        dqt[...] = jnp.zeros_like(dqt)

        def spread_grads(t):
            at = pl.ds(pl.multiple_of(t * TILE, TILE), TILE)
            probability = jnp.exp2(s_buf[at, :] - level)
            score_grad = (probability * (d_buf[at, :] - delta)).astype(jnp.bfloat16)
            rounded = probability.astype(jnp.bfloat16)
            acc[at, CHANNEL_DIM:] += jnp.dot(rounded, gs[...], preferred_element_type=jnp.float32)
            acc[at, :CHANNEL_DIM] += jnp.dot(score_grad, qs[...], preferred_element_type=jnp.float32)
            dqt[...] += lax.dot_general(
                kvs[at, :CHANNEL_DIM], score_grad, (((0,), (0,)), ((), ())),
                preferred_element_type=jnp.float32,
            )

        @pl.loop(0, pairs)
        def _(k):
            spread_grads(low + 2 * k)
            spread_grads(low + 2 * k + 1)

        @pl.loop(odd, high)
        def _(t):
            spread_grads(t)

        for h in range(BUNDLE):
            to = slice(h // 2 * tokens + b * HALF, h // 2 * tokens + (b + 1) * HALF)
            dq_ref[to, h % 2 * CHANNEL_DIM : (h % 2 + 1) * CHANNEL_DIM] = (
                (dqt[:, h * HALF : (h + 1) * HALF] * scale).T.astype(jnp.bfloat16)
            )

    grads = pltpu.make_async_copy(dq_ref, out_hbm.at[pl.ds(0, 2 * tokens), :], stores.at[0])
    grads.start()

    def finish(p):
        r = row_of[p]
        at, to = rows_at(p), rows_at(r)
        dkv_ref[to, :CHANNEL_DIM] = (acc[at, :CHANNEL_DIM] * scale).astype(jnp.bfloat16)
        dkv_ref[to, CHANNEL_DIM:] = acc[at, CHANNEL_DIM:].astype(jnp.bfloat16)
        block_out(dkv_ref.at[to, :], r).start()

    for b, (c, low, high) in enumerate(places):

        @pl.loop(low, high)
        def _(t):
            fresh = True
            if b:
                fresh = jnp.logical_or(t < places[0][1], t >= places[0][2])

            @pl.when(fresh)
            def _():
                for k in range(TILE // HALF):
                    finish(t * (TILE // HALF) + k)

    grads.wait()
    pltpu.make_async_copy(
        dkv_ref, out_hbm.at[pl.ds(2 * tokens, dkv_ref.shape[0]), :], stores.at[1]
    ).wait()


def attention(q, g, kv, span_order, doc_lengths):
    tokens = q.shape[0]
    length = kv.shape[0]
    smem = pl.BlockSpec(memory_space=pltpu.SMEM)
    hbm = pl.BlockSpec(memory_space=pl.ANY)
    lanes = BUNDLE * HALF
    return pl.pallas_call(
        attention_kernel,
        out_shape=jax.ShapeDtypeStruct((2 * tokens + length, 2 * CHANNEL_DIM), jnp.bfloat16),
        in_specs=[smem, smem, hbm, hbm, hbm],
        out_specs=hbm,
        scratch_shapes=[
            pltpu.VMEM((length, 2 * CHANNEL_DIM), jnp.bfloat16),
            pltpu.VMEM((lanes, CHANNEL_DIM), jnp.bfloat16),
            pltpu.VMEM((lanes, CHANNEL_DIM), jnp.bfloat16),
            pltpu.VMEM((length, lanes), jnp.float32),
            pltpu.VMEM((length, lanes), jnp.float32),
            pltpu.VMEM((length, 2 * CHANNEL_DIM), jnp.float32),
            pltpu.VMEM((CHANNEL_DIM, lanes), jnp.float32),
            pltpu.VMEM((tokens, lanes), jnp.bfloat16),
            pltpu.VMEM((tokens, lanes), jnp.bfloat16),
            pltpu.VMEM((2 * tokens, 2 * CHANNEL_DIM), jnp.bfloat16),
            pltpu.VMEM((length, 2 * CHANNEL_DIM), jnp.bfloat16),
            pltpu.VMEM((HALF, 2 * CHANNEL_DIM), jnp.bfloat16),
            pltpu.SMEM((length // HALF,), jnp.int32),
            pltpu.SemaphoreType.DMA((3,)),
            pltpu.SemaphoreType.DMA((2,)),
        ],
        compiler_params=pltpu.CompilerParams(vmem_limit_bytes=GRANT),
        name="attention",
    )(span_order, doc_lengths, q, g, kv)


def shards(inputs, out_grad, w_query, w_key, value_projection, w_out, doc_lengths, span_order):
    tokens = inputs.shape[0]
    peers = lax.axis_size("ctx")
    query, context_grad, gathered = front(
        inputs, out_grad, w_query, w_key, value_projection, w_out, peers
    )
    pieces = attention(
        query, context_grad, gathered.reshape(peers * tokens, -1), span_order, doc_lengths
    )
    pieces = pieces.reshape(1 + 2 * RING, 2, tokens, -1)
    return back(pieces, w_query, w_key, value_projection)


def solution(mesh):
    in_specs = (
        P("ctx", None),
        P("ctx", "head"),
        P(None, "head"),
        P(None, "head"),
        P(None, "head"),
        P("head", None),
        P(),
        P(),
    )
    return jax.shard_map(
        shards, mesh=mesh, in_specs=in_specs, out_specs=P("ctx", "head"), check_vma=False
    )
```

```python
import math

import jax
import jax.numpy as jnp
from jax import lax
from jax.experimental import pallas as pl
from jax.experimental.pallas import tpu as pltpu
from jax.sharding import PartitionSpec as P

ASKER_NUM = 32
SHARED_KV_NUM = 8
CHANNEL_DIM = 128
BUNDLE = ASKER_NUM // SHARED_KV_NUM
HALF = 128
TILE = 256
RING = 4
FEATURES = 512
PARTS = tuple(pl.ds(*cut) for cut in ((0, 64), (64, 64), (128, 64), (192, 64)))
OFFSETS = ((2, 1), (2, 0), (1, 1), (3, 1), (1, 0), (3, 0), (0, 1))
LOG2E = 1.4426950408889634
MASKED = -1e30
OWN = ("u0", "d1", "x0", "x2", "u1", "d0", "x1", "x3")
GRANT = 60 * 1024 * 1024
MESH = pl.DeviceIdType.MESH


def remote(src, dst, send, receive, place):
    return pltpu.make_async_remote_copy(
        src_ref=src, dst_ref=dst, send_sem=send, recv_sem=receive,
        device_id=place, device_id_type=MESH,
    )


def greet(places):
    barrier = pltpu.get_barrier_semaphore()
    for place in places:
        pl.semaphore_signal(barrier, inc=1, device_id=place, device_id_type=MESH)
    pl.semaphore_wait(barrier, len(places))


def neighbours():
    head = lax.axis_index("head")
    ctx = lax.axis_index("ctx")
    far, depth = head // RING, head % RING
    line, near, core = ctx // 4, (ctx // 2) % 2, ctx % 2

    def head_of(f, d):
        return f * RING + d

    def ctx_of(r, n, c):
        return r * 4 + n * 2 + c

    places = {
        "head_up": (head_of(far, (depth + 1) % RING), ctx),
        "head_down": (head_of(far, (depth + 3) % RING), ctx),
        "head_pair": (head_of(1 - far, depth), ctx),
        "ctx_up": (head, ctx_of((line + 1) % RING, near, core)),
        "ctx_down": (head, ctx_of((line + 3) % RING, near, core)),
        "ctx_pair": (head, ctx_of(line, 1 - near, core)),
        "ctx_far": (head, ctx_of((line + 2) % RING, near, core)),
        "sibling": (head, ctx_of(line, near, 1 - core)),
    }
    return places, (far, depth), (line, near, core)


class Gather:
    def __init__(self, source, block, pair, ring, sends, receives, up, down, across, opposed=None):
        other = 1 - pair
        before, after, opposite = (ring + 3) % RING, (ring + 1) % RING, (ring + 2) % RING
        cut = HALF // 2

        def part(p, r, start, size):
            return block(p, r).at[pl.ds(start * cut, size * cut), :]

        own, facing = (pair, ring), (other, ring)
        plan = {
            "u0": (own, (pair, before), 0, 2, up),
            "d1": (own, (pair, after), 2, 2, down),
            "x0": (own, facing, 0, 1, across),
            "x2": (own, facing, 2, 1, across),
            "u1": (own, (pair, before), 2, 2, up),
            "d0": (own, (pair, after), 0, 2, down),
            "x1": (own, facing, 1, 1, across),
            "x3": (own, facing, 3, 1, across),
            "ru": ((pair, before), (pair, opposite), 0, 2, up),
            "rd": ((pair, after), (pair, opposite), 2, 2, down),
            "ou0": (facing, (other, before), 0, 1, up),
            "od2": (facing, (other, after), 2, 1, down),
            "ou1": (facing, (other, before), 1, 2, up),
            "od0": (facing, (other, after), 0, 1, down),
            "od3": (facing, (other, after), 3, 1, down),
            "xb": ((pair, before), (other, before), 3, 1, across),
            "xa": ((pair, after), (other, after), 1, 1, across),
            "rou": ((other, before), (other, opposite), 0, 1, up),
            "rod": ((other, after), (other, opposite), 2, 1, down),
            "xo1": ((pair, opposite), (other, opposite), 1, 1, across),
            "xo3": ((pair, opposite), (other, opposite), 3, 1, across),
        }
        if opposed is not None:
            plan["ou0"] = (facing, (other, before), 0, 2, up)
            plan["ou1"] = (facing, (other, before), 2, 2, up)
            plan["od0"] = (facing, (other, after), 0, 2, down)
            plan["od2"] = (facing, (other, after), 2, 2, down)
            plan["oo"] = (facing, (other, opposite), 0, 4, opposed)
            for name in ("od3", "xb", "xa", "xo1", "xo3", "rou", "rod"):
                del plan[name]
        self.copies = {}
        for k, (name, (at, to, start, size, place)) in enumerate(plan.items()):
            there, here = part(*at, start, size), part(*to, start, size)
            first = source(pl.ds(start * cut, size * cut)) if at is own else there
            self.copies[name] = (
                remote(first, there, sends.at[k], receives.at[k], place),
                remote(here, here, sends.at[k], receives.at[k], place),
            )

    def start(self, *names):
        for name in names:
            self.copies[name][0].start()

    def arrive(self, *names):
        for name in names:
            self.copies[name][1].wait_recv()

    def drain(self):
        for sent, landed in self.copies.values():
            sent.wait_send()


def front_kernel(
    x_hbm, og_hbm, wq_hbm, wk_hbm, wv_hbm, wo_hbm,
    q_hbm, g_hbm, kv_hbm,
    x, wq, wkv, wo, og, acc, q_ref, g_ref, kv_ref,
    loads, stores, head_send, head_receive, ctx_send, ctx_receive, sibling_send, sibling_receive,
):
    places, (far, depth), (line, near, core) = neighbours()
    me = far * RING + depth
    local = [
        pltpu.make_async_copy(x_hbm, x, loads.at[0]),
        pltpu.make_async_copy(wk_hbm, wkv.at[:, :CHANNEL_DIM], loads.at[1]),
        pltpu.make_async_copy(wv_hbm, wkv.at[:, CHANNEL_DIM:], loads.at[2]),
        pltpu.make_async_copy(wq_hbm, wq, loads.at[3]),
        pltpu.make_async_copy(og_hbm, og.at[me], loads.at[4]),
        pltpu.make_async_copy(wo_hbm, wo, loads.at[5]),
    ]
    for copy in local[:3]:
        copy.start()
    saved = [
        pltpu.make_async_copy(q_ref, q_hbm, stores.at[0]),
        pltpu.make_async_copy(kv_ref, kv_hbm, stores.at[1]),
        pltpu.make_async_copy(g_ref, g_hbm, stores.at[2]),
    ]
    greet(list(places.values()))

    heads = Gather(
        lambda rows: og_hbm.at[rows, :],
        lambda p, r: og.at[p * RING + r],
        far, depth, head_send, head_receive,
        places["head_up"], places["head_down"], places["head_pair"],
    )
    heads.start(*OWN)
    for copy in local[3:]:
        copy.start()

    def slot(p, r, c=core):
        return r * 4 + p * 2 + c

    spread = Gather(
        lambda rows: kv_ref.at[slot(near, line), rows, :],
        lambda p, r: kv_ref.at[slot(p, r)],
        near, line, ctx_send, ctx_receive,
        places["ctx_up"], places["ctx_down"], places["ctx_pair"],
        places["ctx_far"],
    )
    turns = [(p, (line + d) % RING) for p in (near, 1 - near) for d in (0, 3, 1, 2)]
    passed = [
        (
            remote(
                kv_ref.at[slot(p, r)], kv_ref.at[slot(p, r)],
                sibling_send.at[k], sibling_receive.at[k], places["sibling"],
            ),
            remote(
                kv_ref.at[slot(p, r, 1 - core)], kv_ref.at[slot(p, r, 1 - core)],
                sibling_send.at[k], sibling_receive.at[k], places["sibling"],
            ),
        )
        for k, (p, r) in enumerate(turns)
    ]

    def features(p, r):
        f = p * RING + r
        return lax.dot_general(
            og[f], wo[:, pl.ds(pl.multiple_of(f * FEATURES, FEATURES), FEATURES)],
            (((1,), (1,)), ((), ())), preferred_element_type=jnp.float32,
        )

    for k in (0, 1, 2):
        local[k].wait()
    kv_ref[slot(near, line)] = jnp.dot(
        x[...], wkv[...], preferred_element_type=jnp.float32
    ).astype(jnp.bfloat16)
    def query(k):
        columns = slice(k * wq.shape[1] // 2, (k + 1) * wq.shape[1] // 2)
        q_ref[:, columns] = jnp.dot(
            x[...], wq[:, columns], preferred_element_type=jnp.float32
        ).astype(jnp.bfloat16)

    def keep(at):
        pltpu.make_async_copy(kv_ref.at[at], kv_hbm.at[at], stores.at[1]).start()

    def share(k):
        passed[k][0].start()
        keep(slot(*turns[k]))

    local[3].wait()
    query(0)
    spread.start(*OWN)
    share(0)
    query(1)
    saved[0].start()
    before, after, opposite = (depth + 3) % RING, (depth + 1) % RING, (depth + 2) % RING
    heads.arrive("u0")
    heads.start("ru")
    heads.arrive("d1")
    heads.start("rd")
    heads.arrive("x0", "x2")
    heads.start("ou0", "od2", "od0")
    local[4].wait()
    local[5].wait()
    acc[...] = features(far, depth)
    spread.arrive("u0")
    spread.start("ru")
    spread.arrive("d1")
    spread.start("rd")
    heads.arrive("u1")
    heads.start("xb")
    heads.arrive("d0")
    heads.start("xa")
    spread.arrive("x0", "x1")
    spread.start("ou0", "od0")
    spread.arrive("x2", "x3")
    spread.start("oo", "od2", "ou1")
    share(4)
    acc[...] += features(far, before)
    heads.arrive("x1")
    heads.start("ou1")
    heads.arrive("x3")
    heads.start("od3")
    spread.arrive("u1")
    share(1)
    spread.arrive("d0")
    share(2)
    acc[...] += features(far, after)
    heads.arrive("ru")
    heads.start("xo1")
    heads.arrive("rd")
    heads.start("xo3")
    acc[...] += features(1 - far, depth)
    spread.arrive("ru", "rd")
    share(3)
    heads.arrive("ou0")
    heads.start("rou")
    heads.arrive("od2")
    heads.start("rod")
    spread.arrive("oo")
    share(7)
    acc[...] += features(far, opposite)
    spread.arrive("ou0", "ou1")
    share(5)
    spread.arrive("od0", "od2")
    share(6)
    heads.arrive("ou1", "xb")
    acc[...] += features(1 - far, before)
    heads.arrive("od0", "od3", "xa")
    acc[...] += features(1 - far, after)
    for k, (sent, landed) in enumerate(passed):
        landed.wait_recv()
        keep(slot(*turns[k], 1 - core))
    heads.arrive("rou", "rod", "xo1", "xo3")
    g_ref[...] = (acc[...] + features(1 - far, opposite)).astype(jnp.bfloat16)
    saved[2].start()
    heads.drain()
    spread.drain()
    for sent, landed in passed:
        sent.wait_send()
    for copy in saved:
        copy.wait()


def front(inputs, out_grad, w_query, w_key, value_projection, w_out, peers):
    tokens, width = inputs.shape
    lanes = w_query.shape[1]
    hbm = pl.BlockSpec(memory_space=pl.ANY)
    return pl.pallas_call(
        front_kernel,
        out_shape=(
            jax.ShapeDtypeStruct((tokens, lanes), jnp.bfloat16),
            jax.ShapeDtypeStruct((tokens, lanes), jnp.bfloat16),
            jax.ShapeDtypeStruct((peers, tokens, 2 * CHANNEL_DIM), jnp.bfloat16),
        ),
        in_specs=[hbm] * 6,
        out_specs=(hbm, hbm, hbm),
        scratch_shapes=[
            pltpu.VMEM((tokens, width), jnp.bfloat16),
            pltpu.VMEM((width, lanes), jnp.bfloat16),
            pltpu.VMEM((width, 2 * CHANNEL_DIM), jnp.bfloat16),
            pltpu.VMEM((lanes, width), jnp.bfloat16),
            pltpu.VMEM((2 * RING, tokens, FEATURES), jnp.bfloat16),
            pltpu.VMEM((tokens, lanes), jnp.float32),
            pltpu.VMEM((tokens, lanes), jnp.bfloat16),
            pltpu.VMEM((tokens, lanes), jnp.bfloat16),
            pltpu.VMEM((peers, tokens, 2 * CHANNEL_DIM), jnp.bfloat16),
            pltpu.SemaphoreType.DMA((6,)),
            pltpu.SemaphoreType.DMA((3,)),
            pltpu.SemaphoreType.DMA((21,)),
            pltpu.SemaphoreType.DMA((21,)),
            pltpu.SemaphoreType.DMA((21,)),
            pltpu.SemaphoreType.DMA((21,)),
            pltpu.SemaphoreType.DMA((8,)),
            pltpu.SemaphoreType.DMA((8,)),
        ],
        compiler_params=pltpu.CompilerParams(
            collective_id=0, has_side_effects=True, vmem_limit_bytes=GRANT
        ),
        name="front",
    )(inputs, out_grad, w_query, w_key, value_projection, w_out)


class Reduce:
    def __init__(self, held, gone, sums, ring, sends, receives, up, down):
        self.held, self.gone, self.sums = held, gone, sums
        self.before, self.after = (ring + 3) % RING, (ring + 1) % RING
        opposite = (ring + 2) % RING
        self.cut = held.shape[2] // 2
        low, high = pl.ds(0, self.cut), pl.ds(self.cut, self.cut)
        plan = [
            (held.at[opposite, :, low], gone.at[0], up),
            (held.at[opposite, :, high], gone.at[1], down),
            (held.at[self.after, :, high], sums.at[0, :, high], up),
            (held.at[self.before, :, low], sums.at[1, :, low], down),
            (held.at[self.after, :, low], sums.at[0, :, low], up),
            (held.at[self.before, :, high], sums.at[1, :, high], down),
        ]
        self.copies = [
            remote(src, dst, sends.at[k], receives.at[k], place)
            for k, (src, dst, place) in enumerate(plan)
        ]

    def start(self, *which):
        for k in which:
            self.copies[k].start()

    def relay(self):
        low, high = slice(0, self.cut), slice(self.cut, 2 * self.cut)
        for k, r, rows in ((0, self.after, low), (1, self.before, high)):
            self.copies[k].wait_recv()
            for p in range(2):
                self.held[r, p, rows] = (
                    self.held[r, p, rows].astype(jnp.float32)
                    + self.gone[k, p].astype(jnp.float32)
                ).astype(jnp.bfloat16)
            self.start(4 + k)

    def arrive(self):
        for k in (2, 3, 4, 5):
            self.copies[k].wait_recv()

    def total(self, p):
        return self.sums[0, p].astype(jnp.float32) + self.sums[1, p].astype(jnp.float32)

    def drain(self):
        for copy in self.copies:
            copy.wait_send()


def back_kernel(
    p_hbm, wq_hbm, wk_hbm, wv_hbm,
    out_ref,
    dq, mine, wq, wkv, side, held, inbox, dkv, parts, leaving, left, gone, sums, crossing, crossed,
    loads, side_send, side_receive, ctx_send, ctx_receive, head_send, head_receive,
    pair_send, pair_receive,
):
    places, (far, depth), (line, near, core) = neighbours()
    head, ctx = lax.axis_index("head"), lax.axis_index("ctx")
    others = [
        ((line + d) % RING, (near + n) % 2) for d, n in OFFSETS
    ]
    around = [(head, r * 4 + p * 2 + core) for r, p in others]
    local = [
        pltpu.make_async_copy(p_hbm.at[pl.ds(1, 2 * RING), core], mine, loads.at[0]),
        pltpu.make_async_copy(p_hbm.at[0], dq, loads.at[1]),
        pltpu.make_async_copy(wq_hbm, wq, loads.at[2]),
        pltpu.make_async_copy(wk_hbm, wkv.at[:, :CHANNEL_DIM], loads.at[3]),
        pltpu.make_async_copy(wv_hbm, wkv.at[:, CHANNEL_DIM:], loads.at[4]),
    ]
    for copy in local:
        copy.start()
    greet([places["sibling"], places["head_up"], places["head_down"], places["head_pair"], *around])

    swaps = [
        remote(
            p_hbm.at[pl.ds(1, 2 * RING), 1 - core, rows], side.at[:, rows],
            side_send.at[c], side_receive.at[c], places["sibling"],
        )
        for c, rows in enumerate(PARTS)
    ]
    swaps[0].start()
    sends = [
        [
            remote(
                held.at[r, p, rows], inbox.at[k, rows],
                ctx_send.at[c, k], ctx_receive.at[c, k], around[k],
            )
            for k, (r, p) in enumerate(others)
        ]
        for c, rows in enumerate(PARTS)
    ]
    rounds = [
        Reduce(
            leaving.at[:, :, rows],
            gone.at[:, :, pl.ds(rows.start // 2, rows.size // 2)],
            sums.at[:, :, rows],
            depth, head_send.at[c], head_receive.at[c], places["head_up"], places["head_down"],
        )
        for c, rows in enumerate(PARTS)
    ]
    across = [
        remote(
            crossing.at[rows], crossed.at[rows],
            pair_send.at[c], pair_receive.at[c], places["head_pair"],
        )
        for c, rows in enumerate(PARTS)
    ]

    def join(rows, r, p):
        return mine[2 * r + p, rows].astype(jnp.float32) + side[2 * r + p, rows].astype(jnp.float32)

    def pass_on(c):
        rows = PARTS[c]
        swaps[c].wait_recv()
        if c + 1 < len(PARTS):
            swaps[c + 1].start()
        for k, (r, p) in enumerate(others):
            held[r, p, rows] = join(rows, r, p).astype(jnp.bfloat16)
        for copy in sends[c]:
            copy.start()

    def query_parts(low, high):
        @pl.loop(low, high)
        def _(f):
            at = pl.ds(pl.multiple_of(f * FEATURES, FEATURES), FEATURES)
            query_grad = jnp.concatenate([dq[0], dq[1]], axis=1)
            parts[f] = lax.dot_general(
                query_grad, wq[at, :], (((1,), (1,)), ((), ())),
                preferred_element_type=jnp.float32,
            )

    def term(rows, f):
        return parts[f, rows, :] + lax.dot_general(
            dkv[rows], wkv[pl.ds(pl.multiple_of(f * FEATURES, FEATURES), FEATURES), :],
            (((1,), (1,)), ((), ())), preferred_element_type=jnp.float32,
        )

    def issue(c):
        rows = PARTS[c]
        total = join(rows, line, near)
        for k in range(len(sends[c])):
            sends[c][k].wait_recv()
            total = total + inbox[k, rows].astype(jnp.float32)
        dkv[rows] = total.astype(jnp.bfloat16)
        for d, ready in ((2, (0, 1)), (1, (2,)), (3, (3,))):
            r = (depth + d) % RING
            for p in range(2):
                leaving[r, p, rows] = term(rows, p * RING + r).astype(jnp.bfloat16)
            rounds[c].start(*ready)
        for p in range(2):
            left[p, rows] = term(rows, p * RING + depth)

    def cross(c):
        rows = PARTS[c]
        rounds[c].arrive()
        crossing[rows] = (left[1 - far, rows] + rounds[c].total(1 - far)).astype(jnp.bfloat16)
        across[c].start()
        left[far, rows] = left[far, rows] + rounds[c].total(far)

    last = len(PARTS) - 1
    local[0].wait()
    pass_on(0)
    local[1].wait()
    local[2].wait()
    query_parts(0, RING)
    pass_on(1)
    query_parts(RING, 2 * RING)
    pass_on(2)
    local[3].wait()
    local[4].wait()
    issue(0)
    for c in range(3, len(PARTS)):
        pass_on(c)
    for c in range(1, len(PARTS)):
        issue(c)
        rounds[c - 1].relay()
    for c in range(len(PARTS) - 2):
        cross(c)
    rounds[last].relay()
    cross(last - 1)
    cross(last)
    for c, rows in enumerate(PARTS):
        across[c].wait_recv()
        out_ref[rows, :] = (
            left[far, rows] + crossed[rows].astype(jnp.float32)
        ).astype(jnp.bfloat16)
    for c in range(len(PARTS)):
        swaps[c].wait_send()
        across[c].wait_send()
        rounds[c].drain()
        for copy in sends[c]:
            copy.wait_send()


def back(pieces, w_query, w_key, value_projection):
    tokens = pieces.shape[2]
    chunks = len(PARTS)
    width, lanes = w_query.shape
    vmem = pl.BlockSpec(memory_space=pltpu.VMEM)
    hbm = pl.BlockSpec(memory_space=pl.ANY)
    wide = 2 * CHANNEL_DIM
    bf16, f32 = jnp.bfloat16, jnp.float32
    dma = pltpu.SemaphoreType.DMA
    return pl.pallas_call(
        back_kernel,
        out_shape=jax.ShapeDtypeStruct((tokens, FEATURES), bf16),
        in_specs=[hbm] * 4,
        out_specs=vmem,
        scratch_shapes=[
            pltpu.VMEM((2, tokens, wide), bf16),
            pltpu.VMEM((2 * RING, tokens, wide), bf16),
            pltpu.VMEM((width, lanes), bf16),
            pltpu.VMEM((width, wide), bf16),
            pltpu.VMEM((2 * RING, tokens, wide), bf16),
            pltpu.VMEM((RING, 2, tokens, wide), bf16),
            pltpu.VMEM((len(OFFSETS), tokens, wide), bf16),
            pltpu.VMEM((tokens, wide), bf16),
            pltpu.VMEM((2 * RING, tokens, FEATURES), f32),
            pltpu.VMEM((RING, 2, tokens, FEATURES), bf16),
            pltpu.VMEM((2, tokens, FEATURES), f32),
            pltpu.VMEM((2, 2, tokens // 2, FEATURES), bf16),
            pltpu.VMEM((2, 2, tokens, FEATURES), bf16),
            pltpu.VMEM((tokens, FEATURES), bf16),
            pltpu.VMEM((tokens, FEATURES), bf16),
            dma((5,)),
            dma((chunks,)),
            dma((chunks,)),
            dma((chunks, len(OFFSETS))),
            dma((chunks, len(OFFSETS))),
            dma((chunks, 6)),
            dma((chunks, 6)),
            dma((chunks,)),
            dma((chunks,)),
        ],
        compiler_params=pltpu.CompilerParams(
            collective_id=1, has_side_effects=True, vmem_limit_bytes=54000 * 1024
        ),
        name="back",
    )(pieces, w_query, w_key, value_projection)


def attention_kernel(
    span_ref, length_ref, q_hbm, g_hbm, kv_hbm,
    out_hbm,
    kvs, qs, gs, s_buf, d_buf, acc, dqt, q_ref, g_ref, dq_ref, dkv_ref, blank, row_of,
    loads, stores,
):
    exponent = LOG2E / math.sqrt(CHANNEL_DIM)
    scale = 1.0 / math.sqrt(CHANNEL_DIM)
    spans = span_ref.shape[0]
    tokens, wide = q_ref.shape[0], 2 * CHANNEL_DIM
    local = [
        pltpu.make_async_copy(q_hbm, q_ref, loads.at[0]),
        pltpu.make_async_copy(g_hbm, g_ref, loads.at[1]),
    ]
    for copy in local:
        copy.start()
    places = []
    for b in range(2):
        c = span_ref[2 * lax.axis_index("ctx") + b]
        first = 0
        end = 0
        for k in range(length_ref.shape[0]):
            end = end + length_ref[k]
            first = jnp.where(c * HALF >= end, end, first)
        places.append((c, first // TILE, c // (TILE // HALF) + 1))

    def rows_at(n):
        return pl.ds(pl.multiple_of(n * HALF, HALF), HALF)

    def block_in(r, p):
        return pltpu.make_async_copy(
            kv_hbm.at[rows_at(r), :], kvs.at[rows_at(p), :], loads.at[2]
        )

    def block_out(block, r):
        return pltpu.make_async_copy(
            block, out_hbm.at[rows_at(r + 2 * tokens // HALF), :], stores.at[1]
        )

    for r in range(spans):
        row_of[span_ref[r]] = r
    (_, first_low, first_high), (_, later_low, later_high) = places
    each = TILE // HALF
    last = spans // each

    def fresh(t):
        return jnp.logical_or(t < first_low, t >= first_high)

    def load(t):
        for k in range(each):
            p = t * each + k
            block_in(row_of[p], p).start()

    @pl.loop(first_low, first_high)
    def _(t):
        load(t)

    @pl.loop(later_low, later_high)
    def _(t):
        @pl.when(fresh(t))
        def _():
            load(t)

    blank[...] = jnp.zeros_like(blank)

    @pl.loop(0, last)
    def _(t):
        idle = jnp.logical_and(
            fresh(t), jnp.logical_or(t < later_low, t >= later_high)
        )

        @pl.when(idle)
        def _():
            for k in range(each):
                block_out(blank, row_of[t * each + k]).start()

    def ready(t):
        at = pl.ds(pl.multiple_of(t * TILE, TILE), TILE)
        acc[at, :] = jnp.zeros((TILE, wide), jnp.float32)
        pltpu.make_async_copy(kv_hbm.at[pl.ds(0, TILE), :], kvs.at[at, :], loads.at[2]).wait()

    @pl.loop(first_low, first_high)
    def _(t):
        ready(t)

    @pl.loop(later_low, later_high)
    def _(t):
        @pl.when(fresh(t))
        def _():
            ready(t)

    for copy in local:
        copy.wait()

    lanes = BUNDLE * HALF
    for b in range(2):
        rows = slice(b * HALF, (b + 1) * HALF)
        for h in range(BUNDLE):
            cols = slice(h * CHANNEL_DIM, (h + 1) * CHANNEL_DIM)
            qs[h * HALF : (h + 1) * HALF, :] = q_ref[rows, cols]
            gs[h * HALF : (h + 1) * HALF, :] = g_ref[rows, cols]
        c, low, high = places[b]
        position = c * HALF + lax.broadcasted_iota(jnp.int32, (1, HALF), 1)
        start = jnp.zeros((1, HALF), jnp.int32)
        end = 0
        for k in range(length_ref.shape[0]):
            end = end + length_ref[k]
            start = jnp.where(position >= end, end, start)

        def gather_stats(t, carry):
            top, total, inner = carry
            at = pl.ds(pl.multiple_of(t * TILE, TILE), TILE)
            keys = kvs[at, :CHANNEL_DIM]
            values = kvs[at, CHANNEL_DIM:]
            key_position = t * TILE + lax.broadcasted_iota(jnp.int32, (TILE, HALF), 0)
            bias = jnp.where(
                (key_position <= position) & (key_position >= start), 0.0, MASKED
            )
            bias = jnp.concatenate([bias] * BUNDLE, axis=1)
            s = lax.dot_general(
                keys, qs[...], (((1,), (1,)), ((), ())), preferred_element_type=jnp.float32
            )
            s = s * exponent + bias
            s_buf[at, :] = s
            fresh = jnp.maximum(top, jnp.max(s, axis=0, keepdims=True))
            factor = jnp.exp2(top - fresh)
            e = jnp.exp2(s - fresh)
            slopes = lax.dot_general(
                values, gs[...], (((1,), (1,)), ((), ())), preferred_element_type=jnp.float32
            )
            d_buf[at, :] = slopes
            total = total * factor + jnp.sum(e, axis=0, keepdims=True)
            inner = inner * factor + jnp.sum(e * slopes, axis=0, keepdims=True)
            return fresh, total, inner

        zero = jnp.zeros((1, lanes), jnp.float32)
        pairs = (high - low) // 2
        odd = low + 2 * pairs
        top, total, inner = lax.fori_loop(
            odd,
            high,
            gather_stats,
            lax.fori_loop(
                0,
                pairs,
                lambda k, carry: gather_stats(
                    low + 2 * k + 1, gather_stats(low + 2 * k, carry)
                ),
                (jnp.full((1, lanes), MASKED, jnp.float32), zero, zero),
            ),
        )
        delta = inner / total
        level = top + jnp.log2(total)
        dqt[...] = jnp.zeros_like(dqt)

        def spread_grads(t):
            at = pl.ds(pl.multiple_of(t * TILE, TILE), TILE)
            probability = jnp.exp2(s_buf[at, :] - level)
            score_grad = (probability * (d_buf[at, :] - delta)).astype(jnp.bfloat16)
            rounded = probability.astype(jnp.bfloat16)
            acc[at, CHANNEL_DIM:] += jnp.dot(rounded, gs[...], preferred_element_type=jnp.float32)
            acc[at, :CHANNEL_DIM] += jnp.dot(score_grad, qs[...], preferred_element_type=jnp.float32)
            dqt[...] += lax.dot_general(
                kvs[at, :CHANNEL_DIM], score_grad, (((0,), (0,)), ((), ())),
                preferred_element_type=jnp.float32,
            )

        @pl.loop(0, pairs)
        def _(k):
            spread_grads(low + 2 * k)
            spread_grads(low + 2 * k + 1)

        @pl.loop(odd, high)
        def _(t):
            spread_grads(t)

        for h in range(BUNDLE):
            to = slice(h // 2 * tokens + b * HALF, h // 2 * tokens + (b + 1) * HALF)
            dq_ref[to, h % 2 * CHANNEL_DIM : (h % 2 + 1) * CHANNEL_DIM] = (
                (dqt[:, h * HALF : (h + 1) * HALF] * scale).T.astype(jnp.bfloat16)
            )

    grads = pltpu.make_async_copy(dq_ref, out_hbm.at[pl.ds(0, 2 * tokens), :], stores.at[0])
    grads.start()

    def finish(p):
        r = row_of[p]
        at, to = rows_at(p), rows_at(r)
        dkv_ref[to, :CHANNEL_DIM] = (acc[at, :CHANNEL_DIM] * scale).astype(jnp.bfloat16)
        dkv_ref[to, CHANNEL_DIM:] = acc[at, CHANNEL_DIM:].astype(jnp.bfloat16)
        block_out(dkv_ref.at[to, :], r).start()

    def finish_tile(t):
        for k in range(each):
            finish(t * each + k)

    @pl.loop(first_low, first_high)
    def _(t):
        finish_tile(t)

    @pl.loop(later_low, later_high)
    def _(t):
        @pl.when(fresh(t))
        def _():
            finish_tile(t)

    grads.wait()
    pltpu.make_async_copy(
        dkv_ref, out_hbm.at[pl.ds(2 * tokens, dkv_ref.shape[0]), :], stores.at[1]
    ).wait()


def attention(q, g, kv, span_order, doc_lengths):
    tokens = q.shape[0]
    length = kv.shape[0]
    smem = pl.BlockSpec(memory_space=pltpu.SMEM)
    hbm = pl.BlockSpec(memory_space=pl.ANY)
    lanes = BUNDLE * HALF
    return pl.pallas_call(
        attention_kernel,
        out_shape=jax.ShapeDtypeStruct((2 * tokens + length, 2 * CHANNEL_DIM), jnp.bfloat16),
        in_specs=[smem, smem, hbm, hbm, hbm],
        out_specs=hbm,
        scratch_shapes=[
            pltpu.VMEM((length, 2 * CHANNEL_DIM), jnp.bfloat16),
            pltpu.VMEM((lanes, CHANNEL_DIM), jnp.bfloat16),
            pltpu.VMEM((lanes, CHANNEL_DIM), jnp.bfloat16),
            pltpu.VMEM((length, lanes), jnp.float32),
            pltpu.VMEM((length, lanes), jnp.float32),
            pltpu.VMEM((length, 2 * CHANNEL_DIM), jnp.float32),
            pltpu.VMEM((CHANNEL_DIM, lanes), jnp.float32),
            pltpu.VMEM((tokens, lanes), jnp.bfloat16),
            pltpu.VMEM((tokens, lanes), jnp.bfloat16),
            pltpu.VMEM((2 * tokens, 2 * CHANNEL_DIM), jnp.bfloat16),
            pltpu.VMEM((length, 2 * CHANNEL_DIM), jnp.bfloat16),
            pltpu.VMEM((HALF, 2 * CHANNEL_DIM), jnp.bfloat16),
            pltpu.SMEM((length // HALF,), jnp.int32),
            pltpu.SemaphoreType.DMA((3,)),
            pltpu.SemaphoreType.DMA((2,)),
        ],
        compiler_params=pltpu.CompilerParams(vmem_limit_bytes=GRANT),
        name="attention",
    )(span_order, doc_lengths, q, g, kv)


def shards(inputs, out_grad, w_query, w_key, value_projection, w_out, doc_lengths, span_order):
    tokens = inputs.shape[0]
    peers = lax.axis_size("ctx")
    query, context_grad, gathered = front(
        inputs, out_grad, w_query, w_key, value_projection, w_out, peers
    )
    pieces = attention(
        query, context_grad, gathered.reshape(peers * tokens, -1), span_order, doc_lengths
    )
    pieces = pieces.reshape(1 + 2 * RING, 2, tokens, -1)
    return back(pieces, w_query, w_key, value_projection)


def solution(mesh):
    in_specs = (
        P("ctx", None),
        P("ctx", "head"),
        P(None, "head"),
        P(None, "head"),
        P(None, "head"),
        P("head", None),
        P(),
        P(),
    )
    return jax.shard_map(
        shards, mesh=mesh, in_specs=in_specs, out_specs=P("ctx", "head"), check_vma=False
    )
```
